32 devices in a mesh: dp: 8 (over z, y), tp: 4 (over x, core).
Axes of the slice: x: 2, y: 2, z: 4, core: 2. Of those that a mesh axis runs over, the one named last changes fastest.
Arguments:
- tokens: bfloat16 [32, 1024, 768], P(('dp', 'tp')), may hold values from -11 to 11
- clip_lengths: int32 [32, 4], P(('dp', 'tp')), may hold values from 1 to 384, as said below
- out_grad: bfloat16 [32, 1024, 768], P(('dp', 'tp')), may hold values from -6 to 6
- w_query: bfloat16 [768, 768], P(('dp', 'tp')), may hold values from -0.21875 to 0.21875
- w_key: bfloat16 [768, 768], P(('dp', 'tp')), may hold values from -0.21875 to 0.21875
- w_value: bfloat16 [768, 768], P(('dp', 'tp')), may hold values from -0.21875 to 0.21875
- w_output: bfloat16 [768, 768], P(('dp', 'tp')), may hold values from -2.5 to 2.5
- gain_attention: bfloat16 [768], P(('dp', 'tp')), may hold values from 0.099609375 to 1.8984375
- gain_feed: bfloat16 [768], P(('dp', 'tp')), may hold values from 0.099609375 to 1.8984375
- w_expand: bfloat16 [768, 3072], P('dp', 'tp'), may hold values from -0.21875 to 0.21875
- w_reduce: bfloat16 [3072, 768], P('tp', 'dp'), may hold values from -0.4375 to 0.4375
Outputs:
- block_out: bfloat16 [32, 1024, 768], P(('dp', 'tp'))
- grad_tokens: float32 [32, 1024, 768], P(('dp', 'tp'))
- grad_w_query: float32 [768, 768], P(('dp', 'tp'))
- grad_w_key: float32 [768, 768], P(('dp', 'tp'))
- grad_w_value: float32 [768, 768], P(('dp', 'tp'))
- grad_w_output: float32 [768, 768], P(('dp', 'tp'))
- grad_gain_attention: float32 [768], P(('dp', 'tp'))
- grad_gain_feed: float32 [768], P(('dp', 'tp'))
- grad_w_expand: float32 [768, 3072], P('dp', 'tp')
- grad_w_reduce: float32 [3072, 768], P('tp', 'dp')
- root_mean_squares: float32 [3], replicated
The draws below stay inside these ranges and needn't reach their ends.
Inputs may be any that keep to these rules, and one draw needn't show every extreme that they name: Each row of clip_lengths gives the lengths of its 3 clips in order, each at most 384 with one of exactly 384 in every row, then the number of padding slots at the row's end, 1 to 256; a row's entries sum to 1024.
All inputs are finite; a program needn't handle non-finite values.
Results may differ from the reference program's by a relative error of at most 0.015.
Values may be sent and summed in bfloat16 or wider, within the bound.
A program may use at most 192 MiB of HBM per device.

```python
from functools import partial
import jax
import jax.numpy as jnp
from jax import lax

D = 768
HEADS = 12
HEAD_DIM = 64
FF = 3072
PACK = 1024
MAXCLIP = 384
SLOTS = 4
ROWS = 32


def draw_tokens(key, part):
    position = jnp.arange(ROWS, dtype=jnp.float32) / max(ROWS - 1, 1)
    noise = jnp.clip(jax.random.normal(key, (ROWS, PACK, D), jnp.float32), -6.0, 6.0)
    row_scale = 0.6 * jnp.power(3.0, position)
    return (noise * row_scale[:, None, None]).astype(jnp.bfloat16)


def draw_clip_lengths(key, part):
    key_pad = jax.random.fold_in(key, 11)
    key_split = jax.random.fold_in(key, 12)
    key_turn = jax.random.fold_in(key, 13)
    row_index = jnp.arange(ROWS, dtype=jnp.int32)
    pad_most = 1 + (PACK // 4 - 1) * row_index // max(ROWS - 1, 1)
    pad_offset = jax.random.randint(key_pad, (ROWS,), 0, 1 << 20, dtype=jnp.int32)
    padding = 1 + pad_offset % pad_most
    remain = PACK - padding - MAXCLIP
    lower = jnp.maximum(1, remain - MAXCLIP)
    upper = jnp.minimum(MAXCLIP, remain - 1)
    offset = jax.random.randint(key_split, (ROWS,), 0, 1 << 20, dtype=jnp.int32)
    first = lower + offset % (upper - lower + 1)
    second = remain - first
    longest = jnp.full((ROWS,), MAXCLIP, jnp.int32)
    clips = jnp.stack([longest, first, second], axis=-1)
    turn = jax.random.randint(key_turn, (ROWS,), 0, 3, dtype=jnp.int32)
    order = (jnp.arange(3, dtype=jnp.int32)[None, :] + turn[:, None]) % 3
    clips = jnp.take_along_axis(clips, order, axis=1)
    return jnp.concatenate([clips, padding[:, None]], axis=1).astype(jnp.int32)


def raised(drawn, key, source, target, blocks, factor):
    def block_of(axis_at):
        return (jnp.arange(drawn.shape[axis_at]) // (drawn.shape[axis_at] // blocks)).reshape((-1,) + (1,) * (drawn.ndim - 1 - axis_at))

    first = jax.random.permutation(key, blocks)[block_of(target)]
    far = (block_of(target) + blocks // 2) % blocks
    return jnp.where((block_of(source) == first) | (block_of(source) == far), factor * drawn, drawn)


def levels(key, dims, cuts, low, top_value):
    def one(axis_at, blocks):
        heights = jax.random.uniform(jax.random.fold_in(jax.random.fold_in(key, 6), axis_at), (blocks,), jnp.float32, low / len(cuts), top_value / len(cuts))
        return jnp.repeat(jnp.exp(heights), dims[axis_at] // blocks).reshape((-1,) + (1,) * (len(dims) - axis_at - 1))

    level = one(*cuts[0])
    for cut in cuts[1:]:
        level = level * one(*cut)
    return level


def normal_values(rng, dims, scale, limit, shards=(), kind=jnp.bfloat16):
    loudness = levels(rng, dims, shards, -0.22, 0.18) if shards else 1.0
    entries = jax.random.normal(rng, dims, jnp.float32) * scale * loudness
    return jnp.minimum(jnp.maximum(entries, -limit), limit).astype(kind)


def noise_with(key, extent, deviation, limit, split, heavy, kind=jnp.bfloat16):
    values = deviation * jax.random.normal(key, extent, jnp.float32)
    if split:
        values = values * levels(key, extent, split, -0.22, 0.18)
    return jnp.clip(raised(values, jax.random.fold_in(key, 3), *heavy), -limit, limit).astype(kind)


def setup_inputs(seed: int = 0) -> dict:
    key_list = jax.random.split(jax.random.key(seed), 12)
    return {
        "tokens": draw_tokens(jax.random.fold_in(key_list[11], 71), 0),
        "clip_lengths": draw_clip_lengths(jax.random.fold_in(key_list[11], 71), 0),
        "out_grad": noise_with(key_list[2], (ROWS, PACK, D), 1.0, 6.0, ((0, 32),), (0, 2, 32, 2.75)),
        "w_query": normal_values(key_list[3], (D, D), D ** -0.5, 0.21875, ((0, 32),)),
        "w_key": normal_values(key_list[4], (D, D), D ** -0.5, 0.21875, ((0, 32),)),
        "w_value": normal_values(key_list[5], (D, D), D ** -0.5, 0.21875, ((0, 32),)),
        "w_output": normal_values(key_list[6], (D, D), (D // 128) ** -0.5, 2.5, ((0, 32),)),
        "gain_attention": jnp.clip(1.0 + 0.18 * jax.random.normal(key_list[7], (D,), jnp.float32), 0.099609375, 1.8984375).astype(jnp.bfloat16),
        "gain_feed": jnp.clip(1.0 + 0.18 * jax.random.normal(key_list[8], (D,), jnp.float32), 0.099609375, 1.8984375).astype(jnp.bfloat16),
        "w_expand": normal_values(key_list[9], (D, FF), D ** -0.5, 0.21875, ((0, 8), (1, 4))),
        "w_reduce": normal_values(key_list[10], (FF, D), (FF // 16) ** -0.5, 0.4375, ((0, 4), (1, 8))),
    }


@jax.custom_vjp
def low(v):
    return lax.optimization_barrier(v.astype(jnp.bfloat16)).astype(jnp.float32)

@jax.custom_vjp
def low_back(v):
    return v

def low_keep(v):
    return (low(v), None)

def low_pass(kept, grad):
    return (grad,)

def back_keep(v):
    return (v, None)

def back_low(kept, grad):
    return (low(grad),)
low.defvjp(low_keep, low_pass)
low_back.defvjp(back_keep, back_low)
highest = lax.Precision.HIGHEST

def layer_norm(array_in, gain_vec):
    average = lax.optimization_barrier(jnp.mean(array_in, axis=-1, keepdims=True))
    centred = array_in - average
    spread = lax.optimization_barrier(jnp.mean(centred * centred, axis=-1, keepdims=True))
    return centred * lax.rsqrt(spread + 1e-06) * gain_vec

def project(array_in, weight):
    return jnp.einsum('gpd,de->gpe', array_in, weight, precision=highest)

def segment_numbers(lengths, pack_len):
    clip_ends = jnp.cumsum(lengths[:, :-1], axis=-1, dtype=jnp.int32)
    position = jnp.arange(pack_len, dtype=jnp.int32)
    return lax.optimization_barrier(jnp.sum((position[None, :, None] >= clip_ends[:, None, :]).astype(jnp.int32), axis=-1, dtype=jnp.int32))

def forward(params, block_rows, segments):
    w_query, w_key, w_value, w_output, gain_attention, gain_feed, w_expand, w_reduce = params
    groups, pack_len, width = block_rows.shape
    normed = low(layer_norm(block_rows, gain_attention))
    query_rows = low(low_back(project(normed, w_query)))
    key_rows = low(low_back(project(normed, w_key)))
    value_rows = low(low_back(project(normed, w_value)))
    head_shape = (groups, pack_len, HEADS, HEAD_DIM)
    scores = jnp.einsum('gqhe,gkhe->ghqk', query_rows.reshape(head_shape), key_rows.reshape(head_shape), precision=highest) * 0.125
    scores = low_back(scores)
    same_clip = segments[:, None, :, None] == segments[:, None, None, :]
    scores = jnp.where(same_clip, scores, -1e+30)
    weights = low(jax.nn.softmax(scores, axis=-1))
    mixed_rows = jnp.einsum('ghqk,gkhe->gqhe', weights, value_rows.reshape(head_shape), precision=highest).reshape(groups, pack_len, width)
    mixed_rows = low(low_back(mixed_rows))
    branch = low_back(project(mixed_rows, w_output))
    middle = block_rows + branch
    normed_feed = low(layer_norm(middle, gain_feed))
    hidden = low_back(project(normed_feed, w_expand))
    active = low(jax.nn.gelu(hidden, approximate=False))
    feed_out = low_back(project(active, w_reduce))
    result = middle + feed_out
    valid_rows = (segments < SLOTS - 1).astype(jnp.float32)[:, :, None]
    block_sums = jnp.stack([jnp.sum(block_rows * block_rows * valid_rows), jnp.sum(branch * branch * valid_rows), jnp.sum(feed_out * feed_out * valid_rows)])
    return (result, block_sums)

def reference(tokens, clip_lengths, out_grad, w_query, w_key, w_value, w_output, gain_attention, gain_feed, w_expand, w_reduce):
    params = tuple((weight.astype(jnp.float32) for weight in (w_query, w_key, w_value, w_output, gain_attention, gain_feed, w_expand, w_reduce)))
    segments = segment_numbers(clip_lengths, PACK)
    groups = ROWS // 2
    scanned = (tokens.astype(jnp.float32).reshape(groups, 2, PACK, D), segments.reshape(groups, 2, PACK), out_grad.astype(jnp.float32).reshape(groups, 2, PACK, D))

    def accumulate(running, block_item):
        grad_sums, stat_sums = running
        block_rows, block_segments, cotangent = block_item
        result, pullback, block_sums = jax.vjp(partial(forward, segments=block_segments), params, block_rows, has_aux=True)
        valid_rows = (block_segments < SLOTS - 1).astype(jnp.float32)[:, :, None]
        grad_params, grad_block = pullback(cotangent * valid_rows)
        grad_sums = jax.tree.map(jnp.add, grad_sums, grad_params)
        return ((grad_sums, stat_sums + block_sums), (result.astype(jnp.bfloat16), grad_block))
    initial = (tuple((jnp.zeros(weight.shape, jnp.float32) for weight in params)), jnp.zeros((3,), jnp.float32))
    (grad_sums, stat_sums), (results, grad_blocks) = lax.scan(accumulate, initial, scanned)
    valid_total = jnp.sum((segments < SLOTS - 1).astype(jnp.float32)) * D
    rms_stats = jnp.sqrt(stat_sums / valid_total)
    return (results.reshape(ROWS, PACK, D), grad_blocks.reshape(ROWS, PACK, D), grad_sums[0], grad_sums[1], grad_sums[2], grad_sums[3], grad_sums[4], grad_sums[5], grad_sums[6], grad_sums[7], rms_stats)
```

```python
import jax
import jax.numpy as jnp
from jax import lax
from jax.experimental import pallas as pl
from jax.experimental.pallas import tpu as pltpu
from jax.sharding import PartitionSpec as P

HEADS = 12
HEAD_DIM = 64
SLOTS = 4
LANES = 128
BLOCK = 256
NEG = -1e30
f32 = jnp.float32
bf16 = jnp.bfloat16
BOTH = ("dp", "tp")
VM = pl.BlockSpec(memory_space=pltpu.VMEM)
SM = pl.BlockSpec(memory_space=pltpu.SMEM)


def dot_plain(left, right):
    return jnp.dot(left, right, preferred_element_type=f32)


def dot_first(left, right):
    return lax.dot_general(left, right, (((0,), (0,)), ((), ())), preferred_element_type=f32)


def dot_last(left, right):
    return lax.dot_general(left, right, (((1,), (1,)), ((), ())), preferred_element_type=f32)


def unit_of(rows):
    centred = rows - jnp.mean(rows, axis=-1, keepdims=True)
    inv = lax.rsqrt(jnp.mean(centred * centred, axis=-1, keepdims=True) + 1e-06)
    return centred * inv, inv


def unit_back(grad, unit, inv, gain):
    scaled = grad * gain
    inner = (
        scaled
        - jnp.mean(scaled, axis=-1, keepdims=True)
        - unit * jnp.mean(scaled * unit, axis=-1, keepdims=True)
    )
    return inv * inner


def clip_ends(clip_ref):
    ends, total = [], jnp.int32(0)
    for j in range(SLOTS - 1):
        total = total + clip_ref[0, j]
        ends.append(total)
    return ends


def segment_of(position, ends):
    return sum((position >= e).astype(jnp.int32) for e in ends)


def valid_of(start, count, ends):
    position = start + lax.broadcasted_iota(jnp.int32, (count, 1), 0)
    return (position < ends[-1]).astype(f32)


def window_of(low, high, ends, total):
    start, stop = jnp.int32(0), jnp.int32(total)
    for e in ends:
        start = jnp.where(low >= e, e, start)
    for e in ends[::-1]:
        stop = jnp.where(high < e, e, stop)
    block = start // LANES
    return block, (stop + LANES - 1) // LANES - block


def by_width(block, count, total, run):
    most = total // LANES
    widths = [w for w in range(2, most + 1) if w != most - 1]
    before = 0
    for w in widths:

        @pl.when((count > before) & (count <= w))
        def _(w=w):
            run(pl.multiple_of(jnp.minimum(block, most - w) * LANES, LANES), w * LANES)

        before = w


def row_loop(total, size, body):
    def step(i, carry):
        body(pl.multiple_of(i * size, size))
        return carry

    lax.fori_loop(0, total // size, step, 0)


def head_masks(scale):
    lane = lax.broadcasted_iota(jnp.int32, (1, LANES), 1)
    low = lane < HEAD_DIM
    return lane, low, (jnp.where(low, scale, 0.0).astype(bf16), jnp.where(low, 0.0, scale).astype(bf16))


def set_bias(bias_ref, row_start, rows, col_start, cols, ends):
    row_seg = segment_of(row_start + lax.broadcasted_iota(jnp.int32, (rows, 1), 0), ends)
    col_seg = segment_of(col_start + lax.broadcasted_iota(jnp.int32, (1, cols), 1), ends)
    bias_ref[:, :cols] = jnp.where(row_seg == col_seg, 0.0, NEG)


def attend(qkv_ref, ends, mixed_ref, stat_ref, bias_ref):
    total, width = mixed_ref.shape
    lane, low, scaled = head_masks(0.125)

    def block(r0):
        rows = pl.ds(r0, BLOCK)

        def run(k0, cols):
            win = pl.ds(k0, cols)
            set_bias(bias_ref, r0, BLOCK, k0, cols, ends)

            def pair(p, carry):
                c = pl.multiple_of(p * LANES, LANES)
                query = qkv_ref[rows, pl.ds(c, LANES)]
                keys = qkv_ref[win, pl.ds(width + c, LANES)]
                values = qkv_ref[win, pl.ds(2 * width + c, LANES)]
                values = jnp.concatenate([values, jnp.ones_like(values)], axis=1)
                stats, outs = stat_ref[rows, :], []
                for h, mask in enumerate(scaled):
                    scores = dot_last(query * mask, keys) + bias_ref[:, :cols]
                    top = jnp.max(scores, axis=1, keepdims=True)
                    mixed = dot_plain(jnp.exp(scores - top).astype(bf16), values)
                    row_sum = mixed[:, LANES:]
                    outs.append(mixed[:, :LANES] / row_sum)
                    stats = jnp.where(lane == 2 * p + h, top + jnp.log(row_sum), stats)
                stat_ref[rows, :] = stats
                mixed_ref[rows, pl.ds(c, LANES)] = jnp.where(low, outs[0], outs[1]).astype(bf16)
                return carry

            lax.fori_loop(0, width // LANES, pair, 0)

        by_width(*window_of(r0, r0 + BLOCK - 1, ends, total), total, run)

    row_loop(total, BLOCK, block)


def inner_sums(grad_ref, mixed_ref, stat_ref):
    total, width = mixed_ref.shape
    lane, low, _ = head_masks(1.0)

    def block(r0):
        rows = pl.ds(r0, LANES)
        sums = jnp.zeros((LANES, LANES), f32)
        for p in range(width // LANES):
            cols = slice(p * LANES, (p + 1) * LANES)
            both = grad_ref[rows, cols].astype(f32) * mixed_ref[rows, cols].astype(f32)
            first = jnp.sum(jnp.where(low, both, 0.0), axis=1, keepdims=True)
            second = jnp.sum(jnp.where(low, 0.0, both), axis=1, keepdims=True)
            sums = jnp.where(lane == 2 * p, first, jnp.where(lane == 2 * p + 1, second, sums))
        stat_ref[rows, :] = sums

    row_loop(total, LANES, block)


def attend_back(qkv_ref, ends, grad_ref, lse_ref, inner_ref, dqkv_ref, bias_ref, dq_ref):
    total, width = grad_ref.shape
    _, low, scaled = head_masks(0.125)
    _, _, plain = head_masks(1.0)
    dq_ref[...] = jnp.zeros_like(dq_ref)

    def block(r0):
        rows = pl.ds(r0, BLOCK)

        def run(q0, cols):
            win = pl.ds(q0, cols)
            set_bias(bias_ref, r0, BLOCK, q0, cols, ends)

            def pair(p, carry):
                c = pl.multiple_of(p * LANES, LANES)
                keys = qkv_ref[rows, pl.ds(width + c, LANES)]
                values = qkv_ref[rows, pl.ds(2 * width + c, LANES)]
                query = qkv_ref[win, pl.ds(c, LANES)]
                grad = grad_ref[win, pl.ds(c, LANES)]
                dk, dv, dq = [], [], 0.0
                for h in range(2):
                    one = pl.ds(2 * p + h, 1)
                    key = keys * scaled[h]
                    scores = dot_last(key, query) + bias_ref[:, :cols]
                    probs = jnp.exp(scores - lse_ref[one, win])
                    dv.append(dot_plain(probs.astype(bf16), grad))
                    grad_probs = dot_last(values * plain[h], grad)
                    ds = (probs * (grad_probs - inner_ref[one, win])).astype(bf16)
                    dk.append(dot_plain(ds, query))
                    dq = dq + dot_first(ds, key)
                dq_ref[win, pl.ds(c, LANES)] += dq
                dqkv_ref[rows, pl.ds(width + c, LANES)] = (jnp.where(low, dk[0], dk[1]) * 0.125).astype(bf16)
                dqkv_ref[rows, pl.ds(2 * width + c, LANES)] = jnp.where(low, dv[0], dv[1]).astype(bf16)
                return carry

            lax.fori_loop(0, width // LANES, pair, 0)

        by_width(*window_of(r0, r0 + BLOCK - 1, ends, total), total, run)

    row_loop(total, BLOCK, block)
    dqkv_ref[:, :width] = dq_ref[...].astype(bf16)


def set_row(ref, row, value):
    at = lax.broadcasted_iota(jnp.int32, ref.shape, 0) == row
    ref[...] += jnp.where(at, value, 0.0)


def forward_kernel(
    clip_ref, tokens_ref, weights_ref, gains_ref,
    qkv_ref, mixed_ref, lse_ref, middle_ref, feed_ref, normed_ref, sums_ref,
    stat_ref, bias_ref,
):
    total, width = tokens_ref.shape
    ends = clip_ends(clip_ref)
    sums_ref[...] = jnp.zeros_like(sums_ref)

    def norm(r0):
        rows = pl.ds(r0, BLOCK)
        x = tokens_ref[rows, :].astype(f32)
        normed_ref[rows, :] = (unit_of(x)[0] * gains_ref[0:1, :]).astype(bf16)
        set_row(sums_ref, 0, jnp.sum(x * x * valid_of(r0, BLOCK, ends), axis=0, keepdims=True))

    row_loop(total, BLOCK, norm)
    for j in range(3):
        cols = slice(j * width, (j + 1) * width)
        qkv_ref[:, cols] = dot_plain(normed_ref[...], weights_ref[:, cols]).astype(bf16)
    attend(qkv_ref, ends, mixed_ref, stat_ref, bias_ref)
    lse_ref[...] = stat_ref[...].T[: lse_ref.shape[0]]
    middle_ref[...] = dot_plain(mixed_ref[...], weights_ref[:, 3 * width : 4 * width])

    def second(r0):
        rows = pl.ds(r0, BLOCK)
        branch = middle_ref[rows, :]
        middle = tokens_ref[rows, :].astype(f32) + branch
        middle_ref[rows, :] = middle
        feed_ref[rows, :] = (unit_of(middle)[0] * gains_ref[1:2, :]).astype(bf16)
        set_row(sums_ref, 1, jnp.sum(branch * branch * valid_of(r0, BLOCK, ends), axis=0, keepdims=True))

    row_loop(total, BLOCK, second)


def feed_kernel(
    clip_ref, feed_ref, out_grad_ref, middle_ref, gains_ref, weights_ref,
    grads_ref, result_ref, grad_middle_ref, sums_ref,
    grad_ref, active_ref, hidden_ref, out_ref, back_ref,
):
    total, width = feed_ref.shape
    ends = clip_ends(clip_ref)
    step = pl.program_id(0)

    @pl.when(step == 0)
    def _():
        def mask(r0):
            rows = pl.ds(r0, BLOCK)
            grad_ref[rows, :] = (out_grad_ref[rows, :].astype(f32) * valid_of(r0, BLOCK, ends)).astype(bf16)

        row_loop(total, BLOCK, mask)
        out_ref[...] = jnp.zeros_like(out_ref)
        back_ref[...] = jnp.zeros_like(back_ref)
        sums_ref[...] = jnp.zeros_like(sums_ref)

    hid = weights_ref.shape[2] - width
    part = 256
    for n in range(hid // part):
        cols = slice(n * part, (n + 1) * part)
        late = slice(hid + n * part, hid + (n + 1) * part)
        hidden = dot_plain(feed_ref[...], weights_ref[0, :, cols])
        grad_active = dot_plain(grad_ref[...], weights_ref[0, :, late])
        share = 0.5 * (1.0 + lax.erf(hidden * 0.7071067811865476))
        active_ref[:, cols] = (hidden * share).astype(bf16)
        slope = share + hidden * (jnp.exp(-0.5 * hidden * hidden) * 0.3989422804014327)
        hidden_ref[:, cols] = (grad_active * slope).astype(bf16)
    expand, reduce = weights_ref[0, :, :hid], weights_ref[0, :, hid:]
    out_ref[...] += dot_last(active_ref[...], reduce)
    back_ref[...] += dot_last(hidden_ref[...], expand)
    grads_ref[0, :, :hid] = dot_first(feed_ref[...], hidden_ref[...]).astype(bf16)
    grads_ref[0, :, hid:] = dot_first(grad_ref[...], active_ref[...]).astype(bf16)

    @pl.when(step == pl.num_programs(0) - 1)
    def _():
        def finish(r0):
            rows = pl.ds(r0, BLOCK)
            valid = valid_of(r0, BLOCK, ends)
            middle, out, back = middle_ref[rows, :], out_ref[rows, :], back_ref[rows, :]
            result_ref[rows, :] = (middle + out).astype(bf16)
            unit, inv = unit_of(middle)
            grad_middle_ref[rows, :] = (
                grad_ref[rows, :].astype(f32) + unit_back(back, unit, inv, gains_ref[1:2, :])
            )
            set_row(sums_ref, 0, jnp.sum(out * out * valid, axis=0, keepdims=True))
            set_row(sums_ref, 1, jnp.sum(back * unit, axis=0, keepdims=True))

        row_loop(total, BLOCK, finish)


def backward_kernel(
    clip_ref, grad_middle_ref, mixed_ref, qkv_ref, lse_ref, normed_ref, tokens_ref, weights_ref, gains_ref,
    grads_ref, grad_tokens_ref, sums_ref,
    low_ref, grad_ref, dqkv_ref, dq_ref, stat_ref, inner_ref, bias_ref,
):
    total, width = tokens_ref.shape
    ends = clip_ends(clip_ref)
    sums_ref[...] = jnp.zeros_like(sums_ref)
    last = slice(3 * width, 4 * width)
    low_ref[...] = grad_middle_ref[...].astype(bf16)
    grads_ref[:, last] = dot_first(mixed_ref[...], low_ref[...]).astype(bf16)
    grad_ref[...] = dot_last(low_ref[...], weights_ref[:, last]).astype(bf16)
    inner_sums(grad_ref, mixed_ref, stat_ref)
    inner_ref[...] = stat_ref[...].T[: inner_ref.shape[0]]
    attend_back(qkv_ref, ends, grad_ref, lse_ref, inner_ref, dqkv_ref, bias_ref, dq_ref)
    for j in range(3):
        cols = slice(j * width, (j + 1) * width)
        grads_ref[:, cols] = dot_first(normed_ref[...], dqkv_ref[:, cols]).astype(bf16)
    dq_ref[...] = dot_last(dqkv_ref[...], weights_ref[:, : 3 * width])

    def finish(r0):
        rows = pl.ds(r0, BLOCK)
        grad = dq_ref[rows, :]
        unit, inv = unit_of(tokens_ref[rows, :].astype(f32))
        grad_tokens_ref[rows, :] = grad_middle_ref[rows, :] + unit_back(grad, unit, inv, gains_ref[0:1, :])
        set_row(sums_ref, 0, jnp.sum(grad * unit, axis=0, keepdims=True))

    row_loop(total, BLOCK, finish)


def params(**more):
    return pltpu.CompilerParams(vmem_limit_bytes=58 << 20, **more)


def shape(*dims, kind=bf16):
    return jax.ShapeDtypeStruct(dims, kind)


def run_forward(clip, tokens, weights, gains):
    total, width = tokens.shape
    return pl.pallas_call(
        forward_kernel,
        name="layer_forward",
        out_shape=(
            shape(total, 3 * width), shape(total, width), shape(16, total, kind=f32),
            shape(total, width, kind=f32), shape(total, width), shape(total, width), shape(8, width, kind=f32),
        ),
        in_specs=[SM, VM, VM, VM],
        out_specs=(VM,) * 7,
        scratch_shapes=[pltpu.VMEM((total, LANES), f32), pltpu.VMEM((BLOCK, total), f32)],
        compiler_params=params(),
        cost_estimate=pl.CostEstimate(flops=12 * 10**9, bytes_accessed=20 << 20, transcendentals=0),
    )(clip, tokens, weights, gains)


def run_feed(clip, feed, out_grad, middle, gains, weights):
    total, width = feed.shape
    parts, _, both = weights.shape
    one = pl.BlockSpec((1, width, both), lambda t: (t, 0, 0))
    return pl.pallas_call(
        feed_kernel,
        name="feed_both",
        grid=(parts,),
        out_shape=(
            shape(parts, width, both), shape(total, width), shape(total, width, kind=f32), shape(8, width, kind=f32),
        ),
        in_specs=[SM, VM, VM, VM, VM, one],
        out_specs=(one, VM, VM, VM),
        scratch_shapes=[
            pltpu.VMEM((total, width), bf16), pltpu.VMEM((total, both - width), bf16),
            pltpu.VMEM((total, both - width), bf16), pltpu.VMEM((total, width), f32), pltpu.VMEM((total, width), f32),
        ],
        compiler_params=params(),
        cost_estimate=pl.CostEstimate(flops=30 * 10**9, bytes_accessed=30 << 20, transcendentals=0),
    )(clip, feed, out_grad, middle, gains, weights)


def run_backward(clip, grad_middle, mixed, qkv, lse, normed, tokens, weights, gains):
    total, width = tokens.shape
    return pl.pallas_call(
        backward_kernel,
        name="layer_backward",
        out_shape=(shape(width, 4 * width), shape(total, width, kind=f32), shape(8, width, kind=f32)),
        in_specs=[SM] + [VM] * 8,
        out_specs=(VM,) * 3,
        scratch_shapes=[
            pltpu.VMEM((total, width), bf16), pltpu.VMEM((total, width), bf16), pltpu.VMEM((total, 3 * width), bf16),
            pltpu.VMEM((total, width), f32), pltpu.VMEM((total, LANES), f32), pltpu.VMEM((16, total), f32),
            pltpu.VMEM((BLOCK, total), f32),
        ],
        compiler_params=params(),
        cost_estimate=pl.CostEstimate(flops=22 * 10**9, bytes_accessed=30 << 20, transcendentals=0),
    )(clip, grad_middle, mixed, qkv, lse, normed, tokens, weights, gains)


def on_device(
    tokens, clip_lengths, out_grad, w_query, w_key, w_value, w_output, gain_attention, gain_feed, w_expand, w_reduce,
):
    _, total, width = tokens.shape
    rows = tokens.reshape(total, width)
    gain_pair = jnp.stack([gain_attention, gain_feed], axis=1)
    mine = jnp.concatenate([w_query, w_key, w_value, w_output, jnp.pad(gain_pair, ((0, 0), (0, LANES - 2)))], axis=1)
    weights = lax.all_gather(mine, BOTH, axis=0, tiled=True)
    gains = jnp.pad(weights[:, 4 * width : 4 * width + 2].T.astype(f32), ((0, 6), (0, 0)))
    hid = w_expand.shape[1]
    both = jnp.concatenate([w_expand, w_reduce.T], axis=1)
    feed_weights = lax.all_gather(both, ("tp", "dp"), axis=0, tiled=True).reshape(-1, width, both.shape[1])

    qkv, mixed, lse, middle, feed, normed, sums_one = run_forward(clip_lengths, rows, weights, gains)
    feed_grads, result, grad_middle, sums_two = run_feed(
        clip_lengths, feed, out_grad.reshape(total, width), middle, gains, feed_weights
    )
    shard_feed = lax.psum_scatter(
        feed_grads.reshape(-1, feed_grads.shape[-1]), ("tp", "dp"), scatter_dimension=0, tiled=True
    )
    grads, grad_tokens, sums_three = run_backward(
        clip_lengths, grad_middle, mixed, qkv, lse, normed, rows, weights, gains
    )
    shard = lax.psum_scatter(grads, BOTH, scatter_dimension=0, tiled=True).astype(f32)
    count = jnp.sum(clip_lengths[:, : SLOTS - 1]).astype(f32)
    squares = [jnp.sum(sums_one[0]), jnp.sum(sums_one[1]), jnp.sum(sums_two[0]), count]
    small = jnp.concatenate([sums_three[0], sums_two[1], jnp.stack(squares)])
    small = lax.psum(small, BOTH)
    gain_grads = lax.dynamic_slice_in_dim(
        small[: 2 * width].reshape(2, width), lax.axis_index(BOTH) * gain_feed.shape[0], gain_feed.shape[0], axis=1
    )
    stats = small[2 * width :]
    means = jnp.sqrt(stats[:3] / (stats[3] * width))
    shard_feed = shard_feed.astype(f32)
    return (
        result.reshape(1, total, width),
        grad_tokens.reshape(1, total, width),
        shard[:, :width],
        shard[:, width : 2 * width],
        shard[:, 2 * width : 3 * width],
        shard[:, 3 * width :],
        gain_grads[0],
        gain_grads[1],
        shard_feed[:, :hid],
        shard_feed[:, hid:].T,
        means,
    )


def solution(mesh):
    row, flat = P(BOTH, None), P(BOTH)
    whole = P(BOTH, None, None)
    in_specs = (whole, row, whole, row, row, row, row, flat, flat, P("dp", "tp"), P("tp", "dp"))
    out_specs = (whole, whole, row, row, row, row, flat, flat, P("dp", "tp"), P("tp", "dp"), P())
    return jax.shard_map(on_device, mesh=mesh, in_specs=in_specs, out_specs=out_specs, check_vma=False)
```

```python
import jax
import jax.numpy as jnp
from jax import lax
from jax.experimental import pallas as pl
from jax.experimental.pallas import tpu as pltpu
from jax.sharding import PartitionSpec as P

HEADS = 12
HEAD_DIM = 64
SLOTS = 4
LANES = 128
BLOCK = 256
NEG = -1e30
f32 = jnp.float32
bf16 = jnp.bfloat16
BOTH = ("dp", "tp")
VM = pl.BlockSpec(memory_space=pltpu.VMEM)
SM = pl.BlockSpec(memory_space=pltpu.SMEM)


def dot_plain(left, right):
    return jnp.dot(left, right, preferred_element_type=f32)


def dot_first(left, right):
    return lax.dot_general(left, right, (((0,), (0,)), ((), ())), preferred_element_type=f32)


def dot_last(left, right):
    return lax.dot_general(left, right, (((1,), (1,)), ((), ())), preferred_element_type=f32)


def unit_of(rows):
    centred = rows - jnp.mean(rows, axis=-1, keepdims=True)
    inv = lax.rsqrt(jnp.mean(centred * centred, axis=-1, keepdims=True) + 1e-06)
    return centred * inv, inv


def unit_back(grad, unit, inv, gain):
    scaled = grad * gain
    inner = (
        scaled
        - jnp.mean(scaled, axis=-1, keepdims=True)
        - unit * jnp.mean(scaled * unit, axis=-1, keepdims=True)
    )
    return inv * inner


def clip_ends(clip_ref):
    ends, total = [], jnp.int32(0)
    for j in range(SLOTS - 1):
        total = total + clip_ref[0, j]
        ends.append(total)
    return ends


def segment_of(position, ends):
    return sum((position >= e).astype(jnp.int32) for e in ends)


def valid_of(start, count, ends):
    position = start + lax.broadcasted_iota(jnp.int32, (count, 1), 0)
    return (position < ends[-1]).astype(f32)


def window_of(low, high, ends, total):
    start, stop = jnp.int32(0), jnp.int32(total)
    for e in ends:
        start = jnp.where(low >= e, e, start)
    for e in ends[::-1]:
        stop = jnp.where(high < e, e, stop)
    block = start // LANES
    return block, (stop + LANES - 1) // LANES - block


def by_width(block, count, total, run):
    most = total // LANES
    widths = [w for w in range(2, most + 1) if w != most - 1]
    before = 0
    for w in widths:

        @pl.when((count > before) & (count <= w))
        def _(w=w):
            run(pl.multiple_of(jnp.minimum(block, most - w) * LANES, LANES), w * LANES)

        before = w


def row_loop(total, size, body):
    def step(i, carry):
        body(pl.multiple_of(i * size, size))
        return carry

    lax.fori_loop(0, total // size, step, 0)


def head_masks(scale):
    lane = lax.broadcasted_iota(jnp.int32, (1, LANES), 1)
    low = lane < HEAD_DIM
    return lane, low, (jnp.where(low, scale, 0.0).astype(bf16), jnp.where(low, 0.0, scale).astype(bf16))


def set_bias(bias_ref, row_start, rows, col_start, cols, ends):
    row_seg = segment_of(row_start + lax.broadcasted_iota(jnp.int32, (rows, 1), 0), ends)
    col_seg = segment_of(col_start + lax.broadcasted_iota(jnp.int32, (1, cols), 1), ends)
    bias_ref[:, :cols] = jnp.where(row_seg == col_seg, 0.0, NEG)


def attend(qkv_ref, ends, mixed_ref, stat_ref, bias_ref):
    total, width = mixed_ref.shape
    lane, low, scaled = head_masks(0.125)

    def block(r0):
        rows = pl.ds(r0, BLOCK)

        def run(k0, cols):
            win = pl.ds(k0, cols)
            set_bias(bias_ref, r0, BLOCK, k0, cols, ends)

            def pair(p, carry):
                c = pl.multiple_of(p * LANES, LANES)
                query = qkv_ref[rows, pl.ds(c, LANES)]
                keys = qkv_ref[win, pl.ds(width + c, LANES)]
                values = qkv_ref[win, pl.ds(2 * width + c, LANES)]
                values = jnp.concatenate([values, jnp.ones_like(values)], axis=1)
                stats, outs = stat_ref[rows, :], []
                for h, mask in enumerate(scaled):
                    scores = dot_last(query * mask, keys) + bias_ref[:, :cols]
                    top = jnp.max(scores, axis=1, keepdims=True)
                    mixed = dot_plain(jnp.exp(scores - top).astype(bf16), values)
                    row_sum = mixed[:, LANES:]
                    outs.append(mixed[:, :LANES] / row_sum)
                    stats = jnp.where(lane == 2 * p + h, top + jnp.log(row_sum), stats)
                stat_ref[rows, :] = stats
                mixed_ref[rows, pl.ds(c, LANES)] = jnp.where(low, outs[0], outs[1]).astype(bf16)
                return carry

            lax.fori_loop(0, width // LANES, pair, 0)

        by_width(*window_of(r0, r0 + BLOCK - 1, ends, total), total, run)

    row_loop(total, BLOCK, block)


def inner_sums(grad_ref, mixed_ref, stat_ref):
    total, width = mixed_ref.shape
    lane, low, _ = head_masks(1.0)

    def block(r0):
        rows = pl.ds(r0, LANES)
        sums = jnp.zeros((LANES, LANES), f32)
        for p in range(width // LANES):
            cols = slice(p * LANES, (p + 1) * LANES)
            both = grad_ref[rows, cols].astype(f32) * mixed_ref[rows, cols].astype(f32)
            first = jnp.sum(jnp.where(low, both, 0.0), axis=1, keepdims=True)
            second = jnp.sum(jnp.where(low, 0.0, both), axis=1, keepdims=True)
            sums = jnp.where(lane == 2 * p, first, jnp.where(lane == 2 * p + 1, second, sums))
        stat_ref[rows, :] = sums

    row_loop(total, LANES, block)


def attend_back(qkv_ref, ends, grad_ref, lse_ref, inner_ref, dqkv_ref, bias_ref, dq_ref):
    total, width = grad_ref.shape
    _, low, scaled = head_masks(0.125)
    _, _, plain = head_masks(1.0)
    dq_ref[...] = jnp.zeros_like(dq_ref)

    def block(r0):
        rows = pl.ds(r0, BLOCK)

        def run(q0, cols):
            win = pl.ds(q0, cols)
            set_bias(bias_ref, r0, BLOCK, q0, cols, ends)

            def pair(p, carry):
                c = pl.multiple_of(p * LANES, LANES)
                keys = qkv_ref[rows, pl.ds(width + c, LANES)]
                values = qkv_ref[rows, pl.ds(2 * width + c, LANES)]
                query = qkv_ref[win, pl.ds(c, LANES)]
                grad = grad_ref[win, pl.ds(c, LANES)]
                dk, dv, dq = [], [], 0.0
                for h in range(2):
                    one = pl.ds(2 * p + h, 1)
                    key = keys * scaled[h]
                    scores = dot_last(key, query) + bias_ref[:, :cols]
                    probs = jnp.exp(scores - lse_ref[one, win])
                    dv.append(dot_plain(probs.astype(bf16), grad))
                    grad_probs = dot_last(values * plain[h], grad)
                    ds = (probs * (grad_probs - inner_ref[one, win])).astype(bf16)
                    dk.append(dot_plain(ds, query))
                    dq = dq + dot_first(ds, key)
                dq_ref[win, pl.ds(c, LANES)] += dq
                dqkv_ref[rows, pl.ds(width + c, LANES)] = (jnp.where(low, dk[0], dk[1]) * 0.125).astype(bf16)
                dqkv_ref[rows, pl.ds(2 * width + c, LANES)] = jnp.where(low, dv[0], dv[1]).astype(bf16)
                return carry

            lax.fori_loop(0, width // LANES, pair, 0)

        by_width(*window_of(r0, r0 + BLOCK - 1, ends, total), total, run)

    row_loop(total, BLOCK, block)
    dqkv_ref[:, :width] = dq_ref[...].astype(bf16)


def set_row(ref, row, value):
    at = lax.broadcasted_iota(jnp.int32, ref.shape, 0) == row
    ref[...] += jnp.where(at, value, 0.0)


def forward_kernel(
    clip_ref, tokens_ref, weights_ref, gains_ref,
    qkv_ref, mixed_ref, lse_ref, middle_ref, feed_ref, normed_ref, sums_ref,
    stat_ref, bias_ref,
):
    total, width = tokens_ref.shape
    ends = clip_ends(clip_ref)
    sums_ref[...] = jnp.zeros_like(sums_ref)

    def norm(r0):
        rows = pl.ds(r0, BLOCK)
        x = tokens_ref[rows, :].astype(f32)
        normed_ref[rows, :] = (unit_of(x)[0] * gains_ref[0:1, :]).astype(bf16)
        set_row(sums_ref, 0, jnp.sum(x * x * valid_of(r0, BLOCK, ends), axis=0, keepdims=True))

    row_loop(total, BLOCK, norm)
    for j in range(3):
        cols = slice(j * width, (j + 1) * width)
        qkv_ref[:, cols] = dot_plain(normed_ref[...], weights_ref[:, cols]).astype(bf16)
    attend(qkv_ref, ends, mixed_ref, stat_ref, bias_ref)
    lse_ref[...] = stat_ref[...].T[: lse_ref.shape[0]]
    middle_ref[...] = dot_plain(mixed_ref[...], weights_ref[:, 3 * width : 4 * width])

    def second(r0):
        rows = pl.ds(r0, BLOCK)
        branch = middle_ref[rows, :]
        middle = tokens_ref[rows, :].astype(f32) + branch
        middle_ref[rows, :] = middle
        feed_ref[rows, :] = (unit_of(middle)[0] * gains_ref[1:2, :]).astype(bf16)
        set_row(sums_ref, 1, jnp.sum(branch * branch * valid_of(r0, BLOCK, ends), axis=0, keepdims=True))

    row_loop(total, BLOCK, second)


def feed_kernel(
    clip_ref, feed_ref, out_grad_ref, middle_ref, gains_ref, weights_ref,
    grads_ref, result_ref, grad_middle_ref, sums_ref,
    grad_ref, active_ref, hidden_ref, out_ref, back_ref,
):
    total, width = feed_ref.shape
    ends = clip_ends(clip_ref)
    step = pl.program_id(0)

    @pl.when(step == 0)
    def _():
        def mask(r0):
            rows = pl.ds(r0, BLOCK)
            grad_ref[rows, :] = (out_grad_ref[rows, :].astype(f32) * valid_of(r0, BLOCK, ends)).astype(bf16)

        row_loop(total, BLOCK, mask)
        out_ref[...] = jnp.zeros_like(out_ref)
        back_ref[...] = jnp.zeros_like(back_ref)
        sums_ref[...] = jnp.zeros_like(sums_ref)

    hid = weights_ref.shape[2] - width
    part = 256
    for n in range(hid // part):
        cols = slice(n * part, (n + 1) * part)
        late = slice(hid + n * part, hid + (n + 1) * part)
        hidden = dot_plain(feed_ref[...], weights_ref[0, :, cols])
        grad_active = dot_plain(grad_ref[...], weights_ref[0, :, late])
        share = 0.5 * (1.0 + lax.erf(hidden * 0.7071067811865476))
        active_ref[:, cols] = (hidden * share).astype(bf16)
        slope = share + hidden * (jnp.exp(-0.5 * hidden * hidden) * 0.3989422804014327)
        hidden_ref[:, cols] = (grad_active * slope).astype(bf16)
    expand, reduce = weights_ref[0, :, :hid], weights_ref[0, :, hid:]
    out_ref[...] += dot_last(active_ref[...], reduce)
    back_ref[...] += dot_last(hidden_ref[...], expand)
    grads_ref[0, :, :hid] = dot_first(feed_ref[...], hidden_ref[...]).astype(bf16)
    grads_ref[0, :, hid:] = dot_first(grad_ref[...], active_ref[...]).astype(bf16)

    @pl.when(step == pl.num_programs(0) - 1)
    def _():
        def finish(r0):
            rows = pl.ds(r0, BLOCK)
            valid = valid_of(r0, BLOCK, ends)
            middle, out, back = middle_ref[rows, :], out_ref[rows, :], back_ref[rows, :]
            result_ref[rows, :] = (middle + out).astype(bf16)
            unit, inv = unit_of(middle)
            grad_middle_ref[rows, :] = (
                grad_ref[rows, :].astype(f32) + unit_back(back, unit, inv, gains_ref[1:2, :])
            )
            set_row(sums_ref, 0, jnp.sum(out * out * valid, axis=0, keepdims=True))
            set_row(sums_ref, 1, jnp.sum(back * unit, axis=0, keepdims=True))

        row_loop(total, BLOCK, finish)


def backward_kernel(
    clip_ref, grad_middle_ref, mixed_ref, qkv_ref, lse_ref, normed_ref, tokens_ref, weights_ref, gains_ref,
    grads_ref, grad_tokens_ref, sums_ref,
    low_ref, grad_ref, dqkv_ref, dq_ref, stat_ref, inner_ref, bias_ref,
):
    total, width = tokens_ref.shape
    ends = clip_ends(clip_ref)
    sums_ref[...] = jnp.zeros_like(sums_ref)
    last = slice(3 * width, 4 * width)
    low_ref[...] = grad_middle_ref[...].astype(bf16)
    grads_ref[:, last] = dot_first(mixed_ref[...], low_ref[...]).astype(bf16)
    grad_ref[...] = dot_last(low_ref[...], weights_ref[:, last]).astype(bf16)
    inner_sums(grad_ref, mixed_ref, stat_ref)
    inner_ref[...] = stat_ref[...].T[: inner_ref.shape[0]]
    attend_back(qkv_ref, ends, grad_ref, lse_ref, inner_ref, dqkv_ref, bias_ref, dq_ref)
    for j in range(3):
        cols = slice(j * width, (j + 1) * width)
        grads_ref[:, cols] = dot_first(normed_ref[...], dqkv_ref[:, cols]).astype(bf16)
    dq_ref[...] = dot_last(dqkv_ref[...], weights_ref[:, : 3 * width])

    def finish(r0):
        rows = pl.ds(r0, BLOCK)
        grad = dq_ref[rows, :]
        unit, inv = unit_of(tokens_ref[rows, :].astype(f32))
        grad_tokens_ref[rows, :] = grad_middle_ref[rows, :] + unit_back(grad, unit, inv, gains_ref[0:1, :])
        set_row(sums_ref, 0, jnp.sum(grad * unit, axis=0, keepdims=True))

    row_loop(total, BLOCK, finish)


def params(**more):
    return pltpu.CompilerParams(vmem_limit_bytes=58 << 20, **more)


def shape(*dims, kind=bf16):
    return jax.ShapeDtypeStruct(dims, kind)


def run_forward(clip, tokens, weights, gains):
    total, width = tokens.shape
    return pl.pallas_call(
        forward_kernel,
        name="layer_forward",
        out_shape=(
            shape(total, 3 * width), shape(total, width), shape(16, total, kind=f32),
            shape(total, width, kind=f32), shape(total, width), shape(total, width), shape(8, width, kind=f32),
        ),
        in_specs=[SM, VM, VM, VM],
        out_specs=(VM,) * 7,
        scratch_shapes=[pltpu.VMEM((total, LANES), f32), pltpu.VMEM((BLOCK, total), f32)],
        compiler_params=params(),
        cost_estimate=pl.CostEstimate(flops=12 * 10**9, bytes_accessed=20 << 20, transcendentals=0),
    )(clip, tokens, weights, gains)


def run_feed(clip, feed, out_grad, middle, gains, weights):
    total, width = feed.shape
    parts, _, both = weights.shape
    one = pl.BlockSpec((1, width, both), lambda t: (t, 0, 0))
    return pl.pallas_call(
        feed_kernel,
        name="feed_both",
        grid=(parts,),
        out_shape=(
            shape(parts, width, both), shape(total, width), shape(total, width, kind=f32), shape(8, width, kind=f32),
        ),
        in_specs=[SM, VM, VM, VM, VM, one],
        out_specs=(one, VM, VM, VM),
        scratch_shapes=[
            pltpu.VMEM((total, width), bf16), pltpu.VMEM((total, both - width), bf16),
            pltpu.VMEM((total, both - width), bf16), pltpu.VMEM((total, width), f32), pltpu.VMEM((total, width), f32),
        ],
        compiler_params=params(),
        cost_estimate=pl.CostEstimate(flops=30 * 10**9, bytes_accessed=30 << 20, transcendentals=0),
    )(clip, feed, out_grad, middle, gains, weights)


def run_backward(clip, grad_middle, mixed, qkv, lse, normed, tokens, weights, gains):
    total, width = tokens.shape
    return pl.pallas_call(
        backward_kernel,
        name="layer_backward",
        out_shape=(shape(width, 4 * width), shape(total, width, kind=f32), shape(8, width, kind=f32)),
        in_specs=[SM] + [VM] * 8,
        out_specs=(VM,) * 3,
        scratch_shapes=[
            pltpu.VMEM((total, width), bf16), pltpu.VMEM((total, width), bf16), pltpu.VMEM((total, 3 * width), bf16),
            pltpu.VMEM((total, width), f32), pltpu.VMEM((total, LANES), f32), pltpu.VMEM((16, total), f32),
            pltpu.VMEM((BLOCK, total), f32),
        ],
        compiler_params=params(),
        cost_estimate=pl.CostEstimate(flops=22 * 10**9, bytes_accessed=30 << 20, transcendentals=0),
    )(clip, grad_middle, mixed, qkv, lse, normed, tokens, weights, gains)


MESH = pl.DeviceIdType.MESH
ANY = pl.BlockSpec(memory_space=pl.ANY)
FACTORS = {
    (8, 4): ((("z", 4), ("y", 2)), (("x", 2), ("c", 2))),
    (64, 4): ((("y", 4), ("z", 8), ("c", 2)), (("x", 4),)),
}


class Net:
    def __init__(self, factors):
        self.factors = factors
        self.size = {n: s for axis in factors for n, s in axis}

    def locate(self):
        self.place = {}
        for name, axis in zip(BOTH, self.factors):
            left = lax.axis_index(name)
            for n, s in axis[::-1]:
                self.place[n] = lax.rem(left, s)
                left = lax.div(left, s)

    def device(self, dim, value):
        out = []
        for axis in self.factors:
            index = 0
            for n, s in axis:
                index = index * s + (value if n == dim else self.place[n])
            out.append(index)
        return tuple(out)

    def names(self, order):
        axes = dict(zip(BOTH, self.factors))
        return [n for a in order for n, _ in axes[a]]

    def dims(self, order):
        return tuple(self.size[n] for n in self.names(order))

    def view(self, ref, order, lanes, **fixed):
        index = tuple(fixed.get(n, slice(None)) for n in self.names(order))
        return ref.at[index + (slice(None), pl.ds(*lanes))]

    def peers(self, dim):
        s = self.size[dim]
        return [lax.rem(self.place[dim] + o, s) for o in range(1, s)]

    def enter(self):
        barrier, count = pltpu.get_barrier_semaphore(), 0
        for dim in self.size:
            for v in self.peers(dim):
                pl.semaphore_signal(barrier, inc=1, device_id=self.device(dim, v), device_id_type=MESH)
                count += 1
        pl.semaphore_wait(barrier, count)


class Sems:
    def __init__(self, send, recv):
        self.send, self.recv, self.used = send, recv, 0

    def take(self):
        self.used += 1
        return self.send.at[self.used - 1], self.recv.at[self.used - 1]


def spread(net, sems, dim, source, target):
    out = []
    for v in net.peers(dim):
        send, recv = sems.take()
        copy = pltpu.make_async_remote_copy(
            src_ref=source, dst_ref=target, send_sem=send, recv_sem=recv,
            device_id=net.device(dim, v), device_id_type=MESH,
        )
        copy.start()
        out.append(copy)
    return out


def arrive(copies):
    for copy in copies:
        copy.wait_recv()


class Piece:
    def __init__(self, net, sems, mine, ref, order, lanes, first, second):
        self.net, self.sems, self.mine, self.ref, self.order, self.lanes = net, sems, mine, ref, order, lanes
        self.first, self.second, self.sent, self.twin = first, second, [], []

    def block(self, free, **other):
        fixed = {n: v for n, v in self.net.place.items() if n not in free}
        return self.net.view(self.ref, self.order, self.lanes, **{**fixed, **other})

    def pass_on(self, dim, block, source=None):
        copies = spread(self.net, self.sems, dim, block if source is None else source, block)
        self.sent += copies
        return copies

    def start(self):
        self.z = self.pass_on("z", self.block(()), self.mine.at[:, pl.ds(*self.lanes)])

    def step_one(self):
        arrive(self.z)
        self.one = self.pass_on(self.first, self.block(("z",)))
        self.twin += self.pass_on("c", self.block(("z",)))

    def step_two(self):
        arrive(self.one)
        self.two = self.pass_on(self.second, self.block(("z", self.first)))
        for v in self.net.peers(self.first):
            self.twin += self.pass_on("c", self.block(("z",), **{self.first: v}))

    def step_three(self):
        arrive(self.two)
        for v in self.net.peers(self.second):
            self.twin += self.pass_on("c", self.block(("z", self.first), **{self.second: v}))

    def ready(self):
        arrive(self.twin)

    def drain(self):
        for copy in self.sent:
            copy.wait_send()


def copies_of(net):
    z, y, x, c = (net.size[n] - 1 for n in "zyxc")
    return z + y + x + c * (1 + y + x)


def lane_parts(width, count):
    tiles, out, at = width // LANES, [], 0
    for i in range(count):
        take = (tiles - at) // (count - i)
        out.append((at * LANES, take * LANES))
        at += take
    return out


ORDERS = (("y", "x"), ("x", "y"))
ATT_PARTS = 4
FEED_PARTS = 4


def gather_kernel(net, att_ref, feed_ref, att_all, feed_all, send, recv, local):
    net.locate()
    net.enter()
    sems = Sems(send, recv)
    flip = BOTH[::-1]
    att = [
        Piece(net, sems, att_ref, att_all, BOTH, lanes, *ORDERS[i % 2])
        for i, lanes in enumerate(lane_parts(att_ref.shape[1], ATT_PARTS))
    ]
    feed = [
        Piece(net, sems, feed_ref, feed_all, flip, lanes, *ORDERS[i % 2])
        for i, lanes in enumerate(lane_parts(feed_ref.shape[1], FEED_PARTS))
    ]
    own = [
        pltpu.make_async_copy(att_ref, net.view(att_all, BOTH, (0, att_ref.shape[1]), **net.place), local.at[0]),
        pltpu.make_async_copy(feed_ref, net.view(feed_all, flip, (0, feed_ref.shape[1]), **net.place), local.at[1]),
    ]
    for copy in own:
        copy.start()
    for p in att:
        p.start()
    for copy in own:
        copy.wait()
    for p in att:
        p.step_one()
    for p in feed:
        p.start()
    for p in att:
        p.step_two()
    for p in att:
        p.step_three()
    for p in feed:
        p.step_one()
    for p in feed:
        p.step_two()
    for p in feed:
        p.step_three()
    for p in att + feed:
        p.ready()
    for p in att + feed:
        p.drain()


def run_gather(net, att, feed):
    count = (ATT_PARTS + FEED_PARTS) * copies_of(net)
    return pl.pallas_call(
        lambda *refs: gather_kernel(net, *refs),
        name="gather_weights",
        out_shape=(shape(*net.dims(BOTH), *att.shape), shape(*net.dims(BOTH[::-1]), *feed.shape)),
        in_specs=[ANY, ANY],
        out_specs=(ANY, ANY),
        scratch_shapes=[
            pltpu.SemaphoreType.DMA((count,)), pltpu.SemaphoreType.DMA((count,)), pltpu.SemaphoreType.DMA((2,)),
        ],
        compiler_params=pltpu.CompilerParams(collective_id=1, has_side_effects=True),
    )(att, feed)


def on_device(
    net,
    tokens, clip_lengths, out_grad, w_query, w_key, w_value, w_output, gain_attention, gain_feed, w_expand, w_reduce,
):
    _, total, width = tokens.shape
    rows = tokens.reshape(total, width)
    gain_pair = jnp.stack([gain_attention, gain_feed], axis=1)
    mine = jnp.concatenate([w_query, w_key, w_value, w_output, jnp.pad(gain_pair, ((0, 0), (0, LANES - 2)))], axis=1)
    hid = w_expand.shape[1]
    both = jnp.concatenate([w_expand, w_reduce.T], axis=1)
    weights, feed_weights = run_gather(net, mine, both)
    weights = weights.reshape(width, -1)
    feed_weights = feed_weights.reshape(-1, width, both.shape[1])
    gains = jnp.pad(weights[:, 4 * width : 4 * width + 2].T.astype(f32), ((0, 6), (0, 0)))
    qkv, mixed, lse, middle, feed, normed, sums_one = run_forward(clip_lengths, rows, weights, gains)
    feed_grads, result, grad_middle, sums_two = run_feed(
        clip_lengths, feed, out_grad.reshape(total, width), middle, gains, feed_weights
    )
    shard_feed = lax.psum_scatter(
        feed_grads.reshape(-1, feed_grads.shape[-1]), ("tp", "dp"), scatter_dimension=0, tiled=True
    )
    grads, grad_tokens, sums_three = run_backward(
        clip_lengths, grad_middle, mixed, qkv, lse, normed, rows, weights, gains
    )
    shard = lax.psum_scatter(grads, BOTH, scatter_dimension=0, tiled=True).astype(f32)
    count = jnp.sum(clip_lengths[:, : SLOTS - 1]).astype(f32)
    squares = [jnp.sum(sums_one[0]), jnp.sum(sums_one[1]), jnp.sum(sums_two[0]), count]
    small = jnp.concatenate([sums_three[0], sums_two[1], jnp.stack(squares)])
    small = lax.psum(small, BOTH)
    gain_grads = lax.dynamic_slice_in_dim(
        small[: 2 * width].reshape(2, width), lax.axis_index(BOTH) * gain_feed.shape[0], gain_feed.shape[0], axis=1
    )
    stats = small[2 * width :]
    means = jnp.sqrt(stats[:3] / (stats[3] * width))
    shard_feed = shard_feed.astype(f32)
    return (
        result.reshape(1, total, width),
        grad_tokens.reshape(1, total, width),
        shard[:, :width],
        shard[:, width : 2 * width],
        shard[:, 2 * width : 3 * width],
        shard[:, 3 * width :],
        gain_grads[0],
        gain_grads[1],
        shard_feed[:, :hid],
        shard_feed[:, hid:].T,
        means,
    )


def solution(mesh):
    row, flat = P(BOTH, None), P(BOTH)
    whole = P(BOTH, None, None)
    in_specs = (whole, row, whole, row, row, row, row, flat, flat, P("dp", "tp"), P("tp", "dp"))
    out_specs = (whole, whole, row, row, row, row, flat, flat, P("dp", "tp"), P("tp", "dp"), P())
    net = Net(FACTORS[mesh.shape["dp"], mesh.shape["tp"]])
    return jax.shard_map(lambda *args: on_device(net, *args), mesh=mesh, in_specs=in_specs, out_specs=out_specs, check_vma=False)
```

```python
import jax
import jax.numpy as jnp
import numpy as np
from jax import lax
from jax.experimental import pallas as pl
from jax.experimental.pallas import tpu as pltpu
from jax.sharding import PartitionSpec as P

HEADS = 12
HEAD_DIM = 64
SLOTS = 4
LANES = 128
BLOCK = 256
WIDE = 512
MAXCLIP = 384
GROUP = 256
NEG = -1e30
f32 = jnp.float32
bf16 = jnp.bfloat16
BOTH = ("dp", "tp")
VM = pl.BlockSpec(memory_space=pltpu.VMEM)
SM = pl.BlockSpec(memory_space=pltpu.SMEM)


def dot_plain(left, right):
    return jnp.dot(left, right, preferred_element_type=f32)


def dot_first(left, right):
    return lax.dot_general(left, right, (((0,), (0,)), ((), ())), preferred_element_type=f32)


def dot_last(left, right):
    return lax.dot_general(left, right, (((1,), (1,)), ((), ())), preferred_element_type=f32)


def unit_of(rows):
    centred = rows - jnp.mean(rows, axis=-1, keepdims=True)
    inv = lax.rsqrt(jnp.mean(centred * centred, axis=-1, keepdims=True) + 1e-06)
    return centred * inv, inv


def unit_back(grad, unit, inv, gain):
    scaled = grad * gain
    inner = (
        scaled
        - jnp.mean(scaled, axis=-1, keepdims=True)
        - unit * jnp.mean(scaled * unit, axis=-1, keepdims=True)
    )
    return inv * inner


def clip_ends(clip_ref):
    ends, total = [], jnp.int32(0)
    for j in range(SLOTS - 1):
        total = total + clip_ref[0, j]
        ends.append(total)
    return ends


def segment_of(position, ends):
    return sum((position >= e).astype(jnp.int32) for e in ends)


def valid_of(start, count, ends):
    position = start + lax.broadcasted_iota(jnp.int32, (count, 1), 0)
    return (position < ends[-1]).astype(f32)


def window_of(low, high, ends, total):
    start, stop = jnp.int32(0), jnp.int32(total)
    for e in ends:
        start = jnp.where(low >= e, e, start)
    for e in ends[::-1]:
        stop = jnp.where(high < e, e, stop)
    block = start // LANES
    return block, (stop + LANES - 1) // LANES - block


def by_width(block, count, total, run):
    most = total // LANES
    widths = [w for w in range(2, most + 1) if w != most - 1]
    before = 0
    for w in widths:

        @pl.when((count > before) & (count <= w))
        def _(w=w):
            run(pl.multiple_of(jnp.minimum(block, most - w) * LANES, LANES), w * LANES)

        before = w


def row_loop(total, size, body):
    def step(i, carry):
        body(pl.multiple_of(i * size, size))
        return carry

    lax.fori_loop(0, total // size, step, 0)


def head_masks(scale):
    lane = lax.broadcasted_iota(jnp.int32, (1, LANES), 1)
    low = lane < HEAD_DIM
    return lane, low, (jnp.where(low, scale, 0.0).astype(bf16), jnp.where(low, 0.0, scale).astype(bf16))


def set_bias(bias_ref, row_start, rows, col_start, cols, ends):
    row_seg = segment_of(row_start + lax.broadcasted_iota(jnp.int32, (rows, 1), 0), ends)
    col_seg = segment_of(col_start + lax.broadcasted_iota(jnp.int32, (1, cols), 1), ends)
    bias_ref[:, :cols] = jnp.where(row_seg == col_seg, 0.0, NEG)


def attend(qkv_ref, ends, mixed_ref, stat_ref, bias_ref):
    total, width = mixed_ref.shape
    lane, low, scaled = head_masks(0.125)

    def block(r0):
        rows = pl.ds(r0, BLOCK)

        def run(k0, cols):
            win = pl.ds(k0, cols)
            set_bias(bias_ref, r0, BLOCK, k0, cols, ends)

            def pair(p, carry):
                c = pl.multiple_of(p * LANES, LANES)
                at = pl.multiple_of(p // 2 * (3 * GROUP) + p % 2 * LANES, LANES)
                query = qkv_ref[rows, pl.ds(at, LANES)]
                keys = qkv_ref[win, pl.ds(at + GROUP, LANES)]
                values = qkv_ref[win, pl.ds(at + 2 * GROUP, LANES)]
                values = jnp.concatenate([values, jnp.ones_like(values)], axis=1)
                stats, outs = stat_ref[rows, :], []
                for h, mask in enumerate(scaled):
                    scores = dot_last(query * mask, keys) + bias_ref[:, :cols]
                    top = jnp.max(scores, axis=1, keepdims=True)
                    mixed = dot_plain(jnp.exp(scores - top).astype(bf16), values)
                    row_sum = mixed[:, LANES:]
                    outs.append(mixed[:, :LANES] / row_sum)
                    stats = jnp.where(lane == 2 * p + h, top + jnp.log(row_sum), stats)
                stat_ref[rows, :] = stats
                mixed_ref[rows, pl.ds(c, LANES)] = jnp.where(low, outs[0], outs[1]).astype(bf16)
                return carry

            lax.fori_loop(0, width // LANES, pair, 0)

        by_width(*window_of(r0, r0 + BLOCK - 1, ends, total), total, run)

    row_loop(total, BLOCK, block)


def inner_sums(grad_ref, mixed_ref, stat_ref):
    total, width = mixed_ref.shape
    lane, low, _ = head_masks(1.0)

    def block(r0):
        rows = pl.ds(r0, LANES)
        sums = jnp.zeros((LANES, LANES), f32)
        for p in range(width // LANES):
            cols = slice(p * LANES, (p + 1) * LANES)
            both = grad_ref[rows, cols].astype(f32) * mixed_ref[rows, cols].astype(f32)
            first = jnp.sum(jnp.where(low, both, 0.0), axis=1, keepdims=True)
            second = jnp.sum(jnp.where(low, 0.0, both), axis=1, keepdims=True)
            sums = jnp.where(lane == 2 * p, first, jnp.where(lane == 2 * p + 1, second, sums))
        stat_ref[rows, :] = sums

    row_loop(total, LANES, block)


def group_lanes(width, g):
    start = width + LANES + g * 3 * GROUP
    return slice(start, start + 3 * GROUP)


def set_row(ref, row, value):
    at = lax.broadcasted_iota(jnp.int32, ref.shape, 0) == row
    ref[...] += jnp.where(at, value, 0.0)


def forward_kernel(
    clip_ref, tokens_ref, weights_ref, gains_ref,
    qkv_ref, mixed_ref, lse_ref, middle_ref, feed_ref, normed_ref, sums_ref,
    stat_ref, bias_ref,
):
    total, width = tokens_ref.shape
    ends = clip_ends(clip_ref)
    sums_ref[...] = jnp.zeros_like(sums_ref)

    def norm(r0):
        rows = pl.ds(r0, BLOCK)
        x = tokens_ref[rows, :].astype(f32)
        normed_ref[rows, :] = (unit_of(x)[0] * gains_ref[0:1, :]).astype(bf16)
        set_row(sums_ref, 0, jnp.sum(x * x * valid_of(r0, BLOCK, ends), axis=0, keepdims=True))

    row_loop(total, BLOCK, norm)
    for g in range(width // GROUP):
        cols = slice(g * 3 * GROUP, (g + 1) * 3 * GROUP)
        qkv_ref[:, cols] = dot_plain(normed_ref[...], weights_ref[:, group_lanes(width, g)]).astype(bf16)
    attend(qkv_ref, ends, mixed_ref, stat_ref, bias_ref)
    lse_ref[...] = stat_ref[...].T[: lse_ref.shape[0]]
    middle_ref[...] = dot_plain(mixed_ref[...], weights_ref[:, :width])

    def second(r0):
        rows = pl.ds(r0, BLOCK)
        branch = middle_ref[rows, :]
        middle = tokens_ref[rows, :].astype(f32) + branch
        middle_ref[rows, :] = middle
        feed_ref[rows, :] = (unit_of(middle)[0] * gains_ref[1:2, :]).astype(bf16)
        set_row(sums_ref, 1, jnp.sum(branch * branch * valid_of(r0, BLOCK, ends), axis=0, keepdims=True))

    row_loop(total, BLOCK, second)


def feed_kernel(
    clip_ref, feed_ref, out_grad_ref, middle_ref, gains_ref, weights_ref,
    grads_ref, result_ref, grad_middle_ref, sums_ref,
    grad_ref, active_ref, hidden_ref, out_ref, back_ref,
):
    total, width = feed_ref.shape
    ends = clip_ends(clip_ref)
    step = pl.program_id(0)

    @pl.when(step == 0)
    def _():
        def mask(r0):
            rows = pl.ds(r0, BLOCK)
            grad_ref[rows, :] = (out_grad_ref[rows, :].astype(f32) * valid_of(r0, BLOCK, ends)).astype(bf16)

        row_loop(total, BLOCK, mask)
        out_ref[...] = jnp.zeros_like(out_ref)
        back_ref[...] = jnp.zeros_like(back_ref)
        sums_ref[...] = jnp.zeros_like(sums_ref)

    hid = weights_ref.shape[2] - width
    part = 256
    for n in range(hid // part):
        cols = slice(n * part, (n + 1) * part)
        late = slice(hid + n * part, hid + (n + 1) * part)
        hidden = dot_plain(feed_ref[...], weights_ref[0, :, cols])
        grad_active = dot_plain(grad_ref[...], weights_ref[0, :, late])
        share = 0.5 * (1.0 + lax.erf(hidden * 0.7071067811865476))
        active_ref[:, cols] = (hidden * share).astype(bf16)
        slope = share + hidden * (jnp.exp(-0.5 * hidden * hidden) * 0.3989422804014327)
        hidden_ref[:, cols] = (grad_active * slope).astype(bf16)
    expand, reduce = weights_ref[0, :, :hid], weights_ref[0, :, hid:]
    out_ref[...] += dot_last(active_ref[...], reduce)
    back_ref[...] += dot_last(hidden_ref[...], expand)
    grads_ref[0, :, :hid] = dot_first(feed_ref[...], hidden_ref[...]).astype(bf16)
    grads_ref[0, :, hid:] = dot_first(grad_ref[...], active_ref[...]).astype(bf16)

    @pl.when(step == pl.num_programs(0) - 1)
    def _():
        def finish(r0):
            rows = pl.ds(r0, BLOCK)
            valid = valid_of(r0, BLOCK, ends)
            middle, out, back = middle_ref[rows, :], out_ref[rows, :], back_ref[rows, :]
            result_ref[rows, :] = (middle + out).astype(bf16)
            unit, inv = unit_of(middle)
            grad_middle_ref[rows, :] = (
                grad_ref[rows, :].astype(f32) + unit_back(back, unit, inv, gains_ref[1:2, :])
            )
            set_row(sums_ref, 0, jnp.sum(out * out * valid, axis=0, keepdims=True))
            set_row(sums_ref, 1, jnp.sum(back * unit, axis=0, keepdims=True))

        row_loop(total, BLOCK, finish)


def static_windows(total):
    spans = []
    for r0 in range(0, total, WIDE):
        low = max(0, r0 - MAXCLIP + 1) // LANES * LANES
        high = min(total, -(-(r0 + WIDE + MAXCLIP - 1) // LANES) * LANES)
        spans.append((low, high))
    width = max(high - low for low, high in spans)
    return [min(low, total - width) for low, _ in spans], width


def start_of(starts, block):
    at = jnp.int32(starts[0])
    for i, s in enumerate(starts):
        at = jnp.where(block == i, s, at)
    return pl.multiple_of(at, LANES)


def pair_back(g, block, pair, total, qkv_ref, ends, grad_ref, lse_ref, inner_ref, dqkv_ref, bias_ref, dq_ref):
    starts, cols = static_windows(total)
    _, low, scaled = head_masks(0.125)
    _, _, plain = head_masks(1.0)
    r0 = pl.multiple_of(block * WIDE, WIDE)
    q0 = start_of(starts, block)
    rows, win = pl.ds(r0, WIDE), pl.ds(q0, cols)

    @pl.when(pair == 0)
    def _():
        set_bias(bias_ref, r0, WIDE, q0, cols, ends)

    c = pl.multiple_of(pair * LANES, LANES)
    at = pl.multiple_of(g * 3 * GROUP + c, LANES)
    keys = qkv_ref[rows, pl.ds(at + GROUP, LANES)]
    values = qkv_ref[rows, pl.ds(at + 2 * GROUP, LANES)]
    query = qkv_ref[win, pl.ds(at, LANES)]
    grad = grad_ref[win, pl.ds(pl.multiple_of(g * GROUP + c, LANES), LANES)]
    dk, dv, dq = [], [], 0.0
    for h in range(2):
        one = pl.ds(4 * g + 2 * pair + h, 1)
        key = keys * scaled[h]
        scores = dot_last(key, query) + bias_ref[:, :cols]
        probs = jnp.exp(scores - lse_ref[one, win])
        dv.append(dot_plain(probs.astype(bf16), grad))
        grad_probs = dot_last(values * plain[h], grad)
        ds = (probs * (grad_probs - inner_ref[one, win])).astype(bf16)
        dk.append(dot_plain(ds, query))
        dq = dq + dot_first(ds, key)
    dq_ref[win, pl.ds(c, LANES)] += dq
    dqkv_ref[rows, pl.ds(GROUP + c, LANES)] = (jnp.where(low, dk[0], dk[1]) * 0.125).astype(bf16)
    dqkv_ref[rows, pl.ds(2 * GROUP + c, LANES)] = jnp.where(low, dv[0], dv[1]).astype(bf16)


def backward_kernel(
    net,
    clip_ref, grad_middle_ref, mixed_ref, qkv_ref, lse_ref, normed_ref, tokens_ref, weights_ref, gains_ref,
    *refs,
):
    total, width = tokens_ref.shape
    ends = clip_ends(clip_ref)
    if net is None:
        grads_ref, grad_tokens_ref, low_ref, grad_ref, dqkv_ref, dq_ref, stat_ref, inner_ref, bias_ref = refs
        pieces, plan = [], {}
    else:
        small_ref, feed_grads_ref, shard_ref, shard_feed_ref, grad_tokens_ref = refs[:5]
        low_ref, grad_ref, dqkv_ref, dq_ref, stat_ref, inner_ref, bias_ref, grads_ref, own_ref = refs[5:14]
        send, recv, local, *bufs = refs[14:]
        net.locate()
        net.enter()
        sems = Sems(send, recv)
        feed, att = [], []
        for lanes, along in feed_folds(feed_grads_ref.shape[-1]):
            feed.append(Fold(net, sems, feed_grads_ref, BOTH[::-1], lanes, along, bufs[:4], shard_feed_ref, own_ref))
            bufs = bufs[4:]
        for lanes, along in att_folds(width):
            att.append(Fold(net, sems, grads_ref, BOTH, lanes, along, bufs[:4], shard_ref))
            bufs = bufs[4:]
        for p in feed:
            p.send(0)
        mine = tuple(net.place["c"] if n == "c" else slice(None) for n in net.names(BOTH[::-1]))
        own = pltpu.make_async_copy(feed_grads_ref.at[mine], own_ref, local)
        own.start()
        each(net.dims(BOTH), lambda i: store_at(grads_ref, i, slice(width, width + LANES), small_ref[i]))

    def advance(*moves):
        for piece, step in moves:
            piece.add(step)
            if step < 3:
                piece.send(step + 1)

    def store(lanes, value):
        if net is None:
            grads_ref[:, lanes] = value.astype(bf16)
        else:
            rows = grads_ref.shape[-2]
            for i, index in enumerate(np.ndindex(*net.dims(BOTH))):
                grads_ref[index + (slice(None), lanes)] = value[i * rows : (i + 1) * rows].astype(bf16)

    low_ref[...] = grad_middle_ref[...].astype(bf16)
    store(slice(0, width), dot_first(mixed_ref[...], low_ref[...]))
    grad_ref[...] = dot_last(low_ref[...], weights_ref[:, :width]).astype(bf16)
    inner_sums(grad_ref, mixed_ref, stat_ref)
    inner_ref[...] = stat_ref[...].T[: inner_ref.shape[0]]
    if net is not None:
        for p in att[:2]:
            p.send(0)
        own.wait()
        f0, f1, f2, f3 = feed
        plan = {
            (0, 0): [(f0, 0), (f1, 0), (f2, 0), (f3, 0)],
            (0, 1): [(att[0], 0), (att[1], 0)],
            (0, 3): [(f0, 1), (f1, 1)],
            (1, 1): [(att[2], 0), (att[3], 0), (f0, 2), (f1, 2)],
            (1, 3): [(f2, 1), (f3, 1), (att[0], 1), (att[1], 1)],
            (2, 1): [(att[4], 0), (att[5], 0), (f2, 2), (f3, 2), (att[0], 2), (att[1], 2)],
            (2, 2): [(att[2], 1), (att[3], 1), (f0, 3), (f1, 3)],
            (2, 3): [(att[2], 2), (att[3], 2), (att[4], 1), (att[5], 1)],
        }
    for g in range(width // GROUP):
        dq_ref[...] = jnp.zeros_like(dq_ref)

        def step(i, carry, g=g):
            for j in range(4):
                moves = plan.get((g, j))
                if moves:
                    pl.when(i == j)(lambda moves=moves: advance(*moves))
            pair_back(
                g, i // 2, i % 2, total, qkv_ref, ends, grad_ref, lse_ref, inner_ref, dqkv_ref, bias_ref, dq_ref
            )
            return carry

        lax.fori_loop(0, 2 * total // WIDE, step, 0)
        dqkv_ref[:, :GROUP] = dq_ref[...].astype(bf16)
        lanes = group_lanes(width, g)
        store(lanes, dot_first(normed_ref[...], dqkv_ref[...]))
        if net is not None:
            for p in att[2 + 2 * g : 4 + 2 * g]:
                p.send(0)
        back = dot_last(dqkv_ref[...], weights_ref[:, lanes])
        if g == 0:
            grad_tokens_ref[...] = back
        else:
            grad_tokens_ref[...] += back
    if net is not None:
        advance((att[6], 0), (att[7], 0))

    def finish(r0):
        rows = pl.ds(r0, BLOCK)
        unit, inv = unit_of(tokens_ref[rows, :].astype(f32))
        grad_tokens_ref[rows, :] = grad_middle_ref[rows, :] + unit_back(
            grad_tokens_ref[rows, :], unit, inv, gains_ref[0:1, :]
        )

    row_loop(total, BLOCK, finish)
    if net is not None:
        advance((att[6], 1), (att[7], 1), (att[4], 2), (att[5], 2), (att[0], 3), (att[1], 3), (f2, 3), (f3, 3))
        advance((att[6], 2), (att[7], 2), (att[2], 3), (att[3], 3), (att[4], 3), (att[5], 3))
        advance((att[6], 3), (att[7], 3))
        for p in feed + att:
            p.drain()


def params(**more):
    return pltpu.CompilerParams(vmem_limit_bytes=58 << 20, **more)


def shape(*dims, kind=bf16):
    return jax.ShapeDtypeStruct(dims, kind)


def run_forward(clip, tokens, weights, gains):
    total, width = tokens.shape
    return pl.pallas_call(
        forward_kernel,
        name="layer_forward",
        out_shape=(
            shape(total, 3 * width), shape(total, width), shape(16, total, kind=f32),
            shape(total, width, kind=f32), shape(total, width), shape(total, width), shape(8, width, kind=f32),
        ),
        in_specs=[SM, VM, VM, VM],
        out_specs=(VM,) * 7,
        scratch_shapes=[pltpu.VMEM((total, LANES), f32), pltpu.VMEM((BLOCK, total), f32)],
        compiler_params=params(),
        cost_estimate=pl.CostEstimate(flops=12 * 10**9, bytes_accessed=20 << 20, transcendentals=0),
    )(clip, tokens, weights, gains)


def run_feed(clip, feed, out_grad, middle, gains, weights):
    total, width = feed.shape
    parts, _, both = weights.shape
    one = pl.BlockSpec((1, width, both), lambda t: (t, 0, 0))
    return pl.pallas_call(
        feed_kernel,
        name="feed_both",
        grid=(parts,),
        out_shape=(
            shape(parts, width, both), shape(total, width), shape(total, width, kind=f32), shape(8, width, kind=f32),
        ),
        in_specs=[SM, VM, VM, VM, VM, one],
        out_specs=(one, VM, VM, VM),
        scratch_shapes=[
            pltpu.VMEM((total, width), bf16), pltpu.VMEM((total, both - width), bf16),
            pltpu.VMEM((total, both - width), bf16), pltpu.VMEM((total, width), f32), pltpu.VMEM((total, width), f32),
        ],
        compiler_params=params(),
        cost_estimate=pl.CostEstimate(flops=30 * 10**9, bytes_accessed=30 << 20, transcendentals=0),
    )(clip, feed, out_grad, middle, gains, weights)


MESH = pl.DeviceIdType.MESH
ANY = pl.BlockSpec(memory_space=pl.ANY)
FACTORS = {
    (8, 4): ((("z", 4), ("y", 2)), (("x", 2), ("c", 2))),
}


class Net:
    def __init__(self, factors):
        self.factors = factors
        self.size = {n: s for axis in factors for n, s in axis}
        self.count = 1
        for s in self.size.values():
            self.count *= s

    def locate(self):
        self.place = {}
        for name, axis in zip(BOTH, self.factors):
            left = lax.axis_index(name)
            for n, s in axis[::-1]:
                self.place[n] = lax.rem(left, s)
                left = lax.div(left, s)

    def device(self, dim, value):
        out = []
        for axis in self.factors:
            index = 0
            for n, s in axis:
                index = index * s + (value if n == dim else self.place[n])
            out.append(index)
        return tuple(out)

    def names(self, order):
        axes = dict(zip(BOTH, self.factors))
        return [n for a in order for n, _ in axes[a]]

    def dims(self, order):
        return tuple(self.size[n] for n in self.names(order))

    def view(self, ref, order, lanes, **fixed):
        index = tuple(fixed.get(n, slice(None)) for n in self.names(order))
        return ref.at[index + (slice(None), pl.ds(*lanes))]

    def peers(self, dim):
        s = self.size[dim]
        return [lax.rem(self.place[dim] + o, s) for o in range(1, s)]

    def enter(self):
        barrier, count = pltpu.get_barrier_semaphore(), 0
        for dim in self.size:
            for v in self.peers(dim):
                pl.semaphore_signal(barrier, inc=1, device_id=self.device(dim, v), device_id_type=MESH)
                count += 1
        pl.semaphore_wait(barrier, count)


class Sems:
    def __init__(self, send, recv):
        self.send, self.recv, self.used = send, recv, 0

    def take(self):
        self.used += 1
        return self.send.at[self.used - 1], self.recv.at[self.used - 1]


def spread(net, sems, dim, source, target):
    out = []
    for v in net.peers(dim):
        send, recv = sems.take()
        copy = pltpu.make_async_remote_copy(
            src_ref=source, dst_ref=target, send_sem=send, recv_sem=recv,
            device_id=net.device(dim, v), device_id_type=MESH,
        )
        copy.start()
        out.append(copy)
    return out


def arrive(copies):
    for copy in copies:
        copy.wait_recv()


class Piece:
    def __init__(self, net, sems, mine, ref, order, lanes, first, second):
        self.net, self.sems, self.mine, self.ref, self.order, self.lanes = net, sems, mine, ref, order, lanes
        self.first, self.second, self.sent, self.twin = first, second, [], []

    def block(self, free, **other):
        fixed = {n: v for n, v in self.net.place.items() if n not in free}
        return self.net.view(self.ref, self.order, self.lanes, **{**fixed, **other})

    def pass_on(self, dim, block, source=None):
        copies = spread(self.net, self.sems, dim, block if source is None else source, block)
        self.sent += copies
        return copies

    def start(self):
        self.z = self.pass_on("z", self.block(()), self.mine.at[:, pl.ds(*self.lanes)])

    def step_one(self):
        arrive(self.z)
        self.one = self.pass_on(self.first, self.block(("z",)))
        self.twin += self.pass_on("c", self.block(("z",)))

    def step_two(self):
        arrive(self.one)
        self.two = self.pass_on(self.second, self.block(("z", self.first)))
        for v in self.net.peers(self.first):
            self.twin += self.pass_on("c", self.block(("z",), **{self.first: v}))

    def step_three(self):
        arrive(self.two)
        for v in self.net.peers(self.second):
            self.twin += self.pass_on("c", self.block(("z", self.first), **{self.second: v}))

    def ready(self):
        arrive(self.twin)

    def drain(self):
        for copy in self.sent:
            copy.wait_send()


def copies_of(net):
    z, y, x, c = (net.size[n] - 1 for n in "zyxc")
    return z + y + x + c * (1 + y + x)


def lane_parts(width, count):
    tiles, out, at = width // LANES, [], 0
    for i in range(count):
        take = (tiles - at) // (count - i)
        out.append((at * LANES, take * LANES))
        at += take
    return out


ORDERS = (("y", "x"), ("x", "y"))
ATT_PARTS = 4
FEED_PARTS = 4


def gather_kernel(net, att_ref, feed_ref, att_all, feed_all, send, recv, local):
    net.locate()
    net.enter()
    sems = Sems(send, recv)
    flip = BOTH[::-1]
    att = [
        Piece(net, sems, att_ref, att_all, BOTH, lanes, *ORDERS[i % 2])
        for i, lanes in enumerate(lane_parts(att_ref.shape[1], ATT_PARTS))
    ]
    feed = [
        Piece(net, sems, feed_ref, feed_all, flip, lanes, *ORDERS[i % 2])
        for i, lanes in enumerate(lane_parts(feed_ref.shape[1], FEED_PARTS))
    ]
    own = [
        pltpu.make_async_copy(att_ref, net.view(att_all, BOTH, (0, att_ref.shape[1]), **net.place), local.at[0]),
        pltpu.make_async_copy(feed_ref, net.view(feed_all, flip, (0, feed_ref.shape[1]), **net.place), local.at[1]),
    ]
    for copy in own:
        copy.start()
    for p in att:
        p.start()
    for copy in own:
        copy.wait()
    for p in att:
        p.step_one()
    for p in feed:
        p.start()
    for p in att:
        p.step_two()
    for p in att:
        p.step_three()
    for p in feed:
        p.step_one()
    for p in feed:
        p.step_two()
    for p in feed:
        p.step_three()
    for p in att + feed:
        p.ready()
    for p in att + feed:
        p.drain()


def run_gather(net, att, feed):
    count = (ATT_PARTS + FEED_PARTS) * copies_of(net)
    return pl.pallas_call(
        lambda *refs: gather_kernel(net, *refs),
        name="gather_weights",
        out_shape=(shape(*net.dims(BOTH), *att.shape), shape(*net.dims(BOTH[::-1]), *feed.shape)),
        in_specs=[ANY, ANY],
        out_specs=(ANY, ANY),
        scratch_shapes=[
            pltpu.SemaphoreType.DMA((count,)), pltpu.SemaphoreType.DMA((count,)), pltpu.SemaphoreType.DMA((2,)),
        ],
        compiler_params=pltpu.CompilerParams(collective_id=1, has_side_effects=True),
    )(att, feed)


def store_at(ref, index, lanes, value):
    ref[tuple(index) + (slice(None), lanes)] = value


def each(dims, body):
    count = 1
    for s in dims:
        count *= s

    def step(i, carry):
        index, left = [], i
        for s in dims[::-1]:
            index.append(lax.rem(left, s))
            left = lax.div(left, s)
        body(tuple(index[::-1]))
        return carry

    lax.fori_loop(0, count, step, 0)


class Fold:
    def __init__(self, net, sems, ref, order, lanes, along, bufs, out, own=None):
        self.net, self.lanes, self.along, self.bufs, self.out = net, lanes, along, bufs, out
        names = net.names(order)
        self.names = [[n for n in names if n not in along[:k]] for k in range(5)]
        self.start = ref if own is None else None
        self.own = own
        self.copies = []
        for k, dim in enumerate(along):
            source, cols = (ref, lanes) if k == 0 else (bufs[k - 1].at[0], (0, lanes[1]))
            copies = []
            for o, v in enumerate(net.peers(dim)):
                index = tuple(v if n == dim else slice(None) for n in self.names[k])
                s, r = sems.take()
                copies.append(
                    pltpu.make_async_remote_copy(
                        src_ref=source.at[index + (slice(None), pl.ds(*cols))], dst_ref=bufs[k].at[o],
                        send_sem=s, recv_sem=r, device_id=net.device(dim, v), device_id_type=MESH,
                    )
                )
            self.copies.append(copies)

    @staticmethod
    def buffers(net, order, rows, lanes, along):
        names, out = net.names(order), []
        for k, dim in enumerate(along):
            left = [net.size[n] for n in names if n not in along[: k + 1]]
            out.append(pltpu.VMEM((net.size[dim] - 1, *left, rows, lanes[1]), bf16))
        return out

    def send(self, k):
        for copy in self.copies[k]:
            copy.start()

    def add(self, k):
        arrive(self.copies[k])
        dim, buf, cols = self.along[k], self.bufs[k], slice(0, self.lanes[1])
        here = self.net.place[dim]
        wide = pl.ds(*self.lanes)

        def one(index):
            at = dict(zip(self.names[k + 1], index))
            full = tuple(at.get(n, here) for n in self.names[k])
            if k > 0:
                total = self.bufs[k - 1][(0,) + full + (slice(None), cols)].astype(f32)
            elif self.own is not None:
                total = self.own[index + (slice(None), wide)].astype(f32)
            else:
                total = self.start[full + (slice(None), wide)].astype(f32)
            terms = [total] + [buf[(o,) + index].astype(f32) for o in range(self.net.size[dim] - 1)]
            if len(terms) > 2:
                size = len(terms)
                total = 0.0
                for v in range(size):
                    back = lax.rem(here - v + size, size)
                    term = terms[0]
                    for o in range(1, size):
                        term = jnp.where(back == o, terms[o], term)
                    total = total + term
            else:
                total = terms[0] + terms[1]
            if k == 3:
                self.out[:, wide] = total
            else:
                buf[(0,) + index] = total.astype(bf16)

        each([self.net.size[n] for n in self.names[k + 1]], one)

    def drain(self):
        for copies in self.copies:
            for copy in copies:
                copy.wait_send()


ALONG = (("c", "x", "y", "z"), ("c", "y", "x", "z"))


def feed_folds(width):
    return [(lanes, ALONG[i % 2]) for i, lanes in enumerate(lane_parts(width, 4))]


def att_folds(width):
    out = []
    spans = [(0, width + LANES)] + [(width + LANES + g * 3 * GROUP, 3 * GROUP) for g in range(width // GROUP)]
    for start, size in spans:
        for i, (at, take) in enumerate(lane_parts(size, 2)):
            out.append(((start + at, take), ALONG[i % 2]))
    return out


def run_backward(net, clip, grad_middle, mixed, qkv, lse, normed, tokens, weights, gains, small=None, feed_grads=None):
    total, width = tokens.shape
    lanes = weights.shape[1]
    scratch = [
        pltpu.VMEM((total, width), bf16), pltpu.VMEM((total, width), bf16), pltpu.VMEM((total, 3 * GROUP), bf16),
        pltpu.VMEM((total, GROUP), f32), pltpu.VMEM((total, LANES), f32), pltpu.VMEM((16, total), f32),
        pltpu.VMEM((WIDE, total), f32),
    ]
    operands = [clip, grad_middle, mixed, qkv, lse, normed, tokens, weights, gains]
    in_specs = [SM] + [VM] * 8
    out_shape = (shape(width, lanes), shape(total, width, kind=f32))
    more = {}
    if net is not None:
        rows, rows_feed = width // net.count, feed_grads.shape[-2]
        flip = BOTH[::-1]
        operands += [small.reshape(*net.dims(BOTH), rows, LANES), feed_grads]
        in_specs += [VM, ANY]
        out_shape = (
            shape(rows, lanes, kind=f32), shape(rows_feed, feed_grads.shape[-1], kind=f32), out_shape[1],
        )
        scratch.append(pltpu.VMEM((*net.dims(BOTH), rows, lanes), bf16))
        scratch.append(pltpu.VMEM(tuple(net.size[n] for n in net.names(flip) if n != "c") + feed_grads.shape[-2:], bf16))
        folds = [(flip, rows_feed, *f) for f in feed_folds(feed_grads.shape[-1])]
        folds += [(BOTH, rows, *f) for f in att_folds(width)]
        count = len(folds) * sum(net.size[n] - 1 for n in "zyxc")
        scratch += [pltpu.SemaphoreType.DMA((count,)), pltpu.SemaphoreType.DMA((count,)), pltpu.SemaphoreType.DMA]
        for f in folds:
            scratch += Fold.buffers(net, *f)
        more = dict(collective_id=2, has_side_effects=True)
    return pl.pallas_call(
        lambda *refs: backward_kernel(net, *refs),
        name="layer_backward",
        out_shape=out_shape,
        in_specs=in_specs,
        out_specs=(VM,) * len(out_shape),
        scratch_shapes=scratch,
        compiler_params=params(**more),
        cost_estimate=pl.CostEstimate(flops=22 * 10**9, bytes_accessed=30 << 20, transcendentals=0),
    )(*operands)


def on_device(
    net,
    tokens, clip_lengths, out_grad, w_query, w_key, w_value, w_output, gain_attention, gain_feed, w_expand, w_reduce,
):
    _, total, width = tokens.shape
    rows = tokens.reshape(total, width)
    gain_pair = jnp.stack([gain_attention, gain_feed], axis=1)
    mine = [w_output, jnp.pad(gain_pair, ((0, 0), (0, LANES - 2)))]
    for g in range(width // GROUP):
        mine += [w[:, g * GROUP : (g + 1) * GROUP] for w in (w_query, w_key, w_value)]
    mine = jnp.concatenate(mine, axis=1)
    hid = w_expand.shape[1]
    both = jnp.concatenate([w_expand, w_reduce.T], axis=1)
    if net is None:
        weights = lax.all_gather(mine, BOTH, axis=0, tiled=True)
        feed_weights = lax.all_gather(both, BOTH[::-1], axis=0, tiled=True)
    else:
        weights, feed_weights = run_gather(net, mine, both)
    weights = weights.reshape(width, -1)
    feed_weights = feed_weights.reshape(-1, width, both.shape[1])
    gains = jnp.pad(weights[:, width : width + 2].T.astype(f32), ((0, 6), (0, 0)))

    qkv, mixed, lse, middle, feed, normed, sums_one = run_forward(clip_lengths, rows, weights, gains)
    feed_grads, result, grad_middle, sums_two = run_feed(
        clip_lengths, feed, out_grad.reshape(total, width), middle, gains, feed_weights
    )
    count = jnp.sum(clip_lengths[:, : SLOTS - 1]).astype(f32)
    squares = jnp.stack([jnp.sum(sums_one[0]), jnp.sum(sums_one[1]), jnp.sum(sums_two[0]), count])
    fixed = (clip_lengths, grad_middle, mixed, qkv, lse, normed, rows, weights, gains)
    if net is None:
        grads, grad_tokens = run_backward(None, *fixed)
        shard = lax.psum_scatter(grads, BOTH, scatter_dimension=0, tiled=True).astype(f32)
        shard_feed = lax.psum_scatter(
            feed_grads.reshape(-1, feed_grads.shape[-1]), BOTH[::-1], scatter_dimension=0, tiled=True
        ).astype(f32)
        stats = lax.psum(squares, BOTH)
        gain_two = lax.psum_scatter(sums_two[1], BOTH, scatter_dimension=0, tiled=True)
    else:
        small = jnp.concatenate([sums_two[1][:, None], jnp.broadcast_to(squares, (width, 4))], axis=1)
        small = jnp.pad(small, ((0, 0), (0, LANES - 5))).astype(bf16)
        feed_grads = feed_grads.reshape(*net.dims(BOTH[::-1]), both.shape[0], both.shape[1])
        shard, shard_feed, grad_tokens = run_backward(net, *fixed, small, feed_grads)
        gain_two = shard[:, width]
        stats = shard[0, width + 1 : width + 5]
    means = jnp.sqrt(stats[:3] / (stats[3] * width))
    parts = shard[:, width + LANES :].reshape(-1, width // GROUP, 3, GROUP)
    query, key, value = (parts[:, :, j].reshape(-1, width) for j in range(3))
    gain_one = sum(jnp.sum(w.astype(f32) * g, axis=1) for w, g in ((w_query, query), (w_key, key), (w_value, value)))
    gain_one = gain_one / gain_attention.astype(f32)
    return (
        result.reshape(1, total, width),
        grad_tokens.reshape(1, total, width),
        query,
        key,
        value,
        shard[:, :width],
        gain_one,
        gain_two,
        shard_feed[:, :hid],
        shard_feed[:, hid:].T,
        means,
    )


def solution(mesh):
    row, flat = P(BOTH, None), P(BOTH)
    whole = P(BOTH, None, None)
    in_specs = (whole, row, whole, row, row, row, row, flat, flat, P("dp", "tp"), P("tp", "dp"))
    out_specs = (whole, whole, row, row, row, row, flat, flat, P("dp", "tp"), P("tp", "dp"), P())
    factors = FACTORS.get((mesh.shape["dp"], mesh.shape["tp"]))
    net = Net(factors) if factors else None
    return jax.shard_map(
        lambda *args: on_device(net, *args), mesh=mesh, in_specs=in_specs, out_specs=out_specs, check_vma=False
    )
```

```python
import jax
import jax.numpy as jnp
import numpy as np
from jax import lax
from jax.experimental import pallas as pl
from jax.experimental.pallas import tpu as pltpu
from jax.sharding import PartitionSpec as P

HEADS = 12
HEAD_DIM = 64
SLOTS = 4
LANES = 128
BLOCK = 256
WIDE = 512
MAXCLIP = 384
GROUP = 256
NEG = -1e30
f32 = jnp.float32
bf16 = jnp.bfloat16
BOTH = ("dp", "tp")
VM = pl.BlockSpec(memory_space=pltpu.VMEM)
SM = pl.BlockSpec(memory_space=pltpu.SMEM)


def dot_plain(left, right):
    return jnp.dot(left, right, preferred_element_type=f32)


def dot_first(left, right):
    return lax.dot_general(left, right, (((0,), (0,)), ((), ())), preferred_element_type=f32)


def dot_last(left, right):
    return lax.dot_general(left, right, (((1,), (1,)), ((), ())), preferred_element_type=f32)


def unit_of(rows):
    centred = rows - jnp.mean(rows, axis=-1, keepdims=True)
    inv = lax.rsqrt(jnp.mean(centred * centred, axis=-1, keepdims=True) + 1e-06)
    return centred * inv, inv


def unit_back(grad, unit, inv, gain):
    scaled = grad * gain
    inner = (
        scaled
        - jnp.mean(scaled, axis=-1, keepdims=True)
        - unit * jnp.mean(scaled * unit, axis=-1, keepdims=True)
    )
    return inv * inner


def clip_ends(clip_ref):
    ends, total = [], jnp.int32(0)
    for j in range(SLOTS - 1):
        total = total + clip_ref[0, j]
        ends.append(total)
    return ends


def segment_of(position, ends):
    return sum((position >= e).astype(jnp.int32) for e in ends)


def valid_of(start, count, ends):
    position = start + lax.broadcasted_iota(jnp.int32, (count, 1), 0)
    return (position < ends[-1]).astype(f32)


def window_of(low, high, ends, total):
    start, stop = jnp.int32(0), jnp.int32(total)
    for e in ends:
        start = jnp.where(low >= e, e, start)
    for e in ends[::-1]:
        stop = jnp.where(high < e, e, stop)
    block = start // LANES
    return block, (stop + LANES - 1) // LANES - block


def by_width(block, count, total, run):
    most = total // LANES
    widths = [w for w in range(2, most + 1) if w != most - 1]
    before = 0
    for w in widths:

        @pl.when((count > before) & (count <= w))
        def _(w=w):
            run(pl.multiple_of(jnp.minimum(block, most - w) * LANES, LANES), w * LANES)

        before = w


def row_loop(total, size, body):
    def step(i, carry):
        body(pl.multiple_of(i * size, size))
        return carry

    lax.fori_loop(0, total // size, step, 0)


def head_masks(scale):
    lane = lax.broadcasted_iota(jnp.int32, (1, LANES), 1)
    low = lane < HEAD_DIM
    return lane, low, (jnp.where(low, scale, 0.0).astype(bf16), jnp.where(low, 0.0, scale).astype(bf16))


def set_bias(bias_ref, row_start, rows, col_start, cols, ends):
    row_seg = segment_of(row_start + lax.broadcasted_iota(jnp.int32, (rows, 1), 0), ends)
    col_seg = segment_of(col_start + lax.broadcasted_iota(jnp.int32, (1, cols), 1), ends)
    bias_ref[:, :cols] = jnp.where(row_seg == col_seg, 0.0, NEG)


def attend(qkv_ref, ends, mixed_ref, stat_ref, bias_ref):
    total, width = mixed_ref.shape
    lane, low, scaled = head_masks(0.125)

    def block(r0):
        rows = pl.ds(r0, BLOCK)

        def run(k0, cols):
            win = pl.ds(k0, cols)
            set_bias(bias_ref, r0, BLOCK, k0, cols, ends)

            def pair(p, carry):
                c = pl.multiple_of(p * LANES, LANES)
                at = pl.multiple_of(p // 2 * (3 * GROUP) + p % 2 * LANES, LANES)
                query = qkv_ref[rows, pl.ds(at, LANES)]
                keys = qkv_ref[win, pl.ds(at + GROUP, LANES)]
                values = qkv_ref[win, pl.ds(at + 2 * GROUP, LANES)]
                values = jnp.concatenate([values, jnp.ones_like(values)], axis=1)
                stats, outs = stat_ref[rows, :], []
                for h, mask in enumerate(scaled):
                    scores = dot_last(query * mask, keys) + bias_ref[:, :cols]
                    top = jnp.max(scores, axis=1, keepdims=True)
                    mixed = dot_plain(jnp.exp(scores - top).astype(bf16), values)
                    row_sum = mixed[:, LANES:]
                    outs.append(mixed[:, :LANES] / row_sum)
                    stats = jnp.where(lane == 2 * p + h, top + jnp.log(row_sum), stats)
                stat_ref[rows, :] = stats
                mixed_ref[rows, pl.ds(c, LANES)] = jnp.where(low, outs[0], outs[1]).astype(bf16)
                return carry

            lax.fori_loop(0, width // LANES, pair, 0)

        by_width(*window_of(r0, r0 + BLOCK - 1, ends, total), total, run)

    row_loop(total, BLOCK, block)


def inner_sums(grad_ref, mixed_ref, stat_ref):
    total, width = mixed_ref.shape
    lane, low, _ = head_masks(1.0)

    def block(r0):
        rows = pl.ds(r0, LANES)
        sums = jnp.zeros((LANES, LANES), f32)
        for p in range(width // LANES):
            cols = slice(p * LANES, (p + 1) * LANES)
            both = grad_ref[rows, cols].astype(f32) * mixed_ref[rows, cols].astype(f32)
            first = jnp.sum(jnp.where(low, both, 0.0), axis=1, keepdims=True)
            second = jnp.sum(jnp.where(low, 0.0, both), axis=1, keepdims=True)
            sums = jnp.where(lane == 2 * p, first, jnp.where(lane == 2 * p + 1, second, sums))
        stat_ref[rows, :] = sums

    row_loop(total, LANES, block)


def group_lanes(width, g):
    start = width + LANES + g * 3 * GROUP
    return slice(start, start + 3 * GROUP)


def set_row(ref, row, value):
    at = lax.broadcasted_iota(jnp.int32, ref.shape, 0) == row
    ref[...] += jnp.where(at, value, 0.0)


def forward_kernel(
    clip_ref, tokens_ref, weights_ref, gains_ref,
    qkv_ref, mixed_ref, lse_ref, middle_ref, feed_ref, normed_ref, sums_ref,
    stat_ref, bias_ref,
):
    total, width = tokens_ref.shape
    ends = clip_ends(clip_ref)
    sums_ref[...] = jnp.zeros_like(sums_ref)

    def norm(r0):
        rows = pl.ds(r0, BLOCK)
        x = tokens_ref[rows, :].astype(f32)
        normed_ref[rows, :] = (unit_of(x)[0] * gains_ref[0:1, :]).astype(bf16)
        set_row(sums_ref, 0, jnp.sum(x * x * valid_of(r0, BLOCK, ends), axis=0, keepdims=True))

    row_loop(total, BLOCK, norm)
    for g in range(width // GROUP):
        cols = slice(g * 3 * GROUP, (g + 1) * 3 * GROUP)
        qkv_ref[:, cols] = dot_plain(normed_ref[...], weights_ref[:, group_lanes(width, g)]).astype(bf16)
    attend(qkv_ref, ends, mixed_ref, stat_ref, bias_ref)
    lse_ref[...] = stat_ref[...].T[: lse_ref.shape[0]]
    middle_ref[...] = dot_plain(mixed_ref[...], weights_ref[:, :width])

    def second(r0):
        rows = pl.ds(r0, BLOCK)
        branch = middle_ref[rows, :]
        middle = tokens_ref[rows, :].astype(f32) + branch
        middle_ref[rows, :] = middle
        feed_ref[rows, :] = (unit_of(middle)[0] * gains_ref[1:2, :]).astype(bf16)
        set_row(sums_ref, 1, jnp.sum(branch * branch * valid_of(r0, BLOCK, ends), axis=0, keepdims=True))

    row_loop(total, BLOCK, second)


def feed_kernel(
    clip_ref, feed_ref, out_grad_ref, middle_ref, gains_ref, weights_ref,
    grads_ref, result_ref, grad_middle_ref, sums_ref,
    grad_ref, active_ref, hidden_ref, out_ref, back_ref,
):
    total, width = feed_ref.shape
    ends = clip_ends(clip_ref)
    step = pl.program_id(0)

    @pl.when(step == 0)
    def _():
        def mask(r0):
            rows = pl.ds(r0, BLOCK)
            grad_ref[rows, :] = (out_grad_ref[rows, :].astype(f32) * valid_of(r0, BLOCK, ends)).astype(bf16)

        row_loop(total, BLOCK, mask)
        out_ref[...] = jnp.zeros_like(out_ref)
        back_ref[...] = jnp.zeros_like(back_ref)
        sums_ref[...] = jnp.zeros_like(sums_ref)

    hid = weights_ref.shape[2] - width
    part = 256
    for n in range(hid // part):
        cols = slice(n * part, (n + 1) * part)
        late = slice(hid + n * part, hid + (n + 1) * part)
        hidden = dot_plain(feed_ref[...], weights_ref[0, :, cols])
        grad_active = dot_plain(grad_ref[...], weights_ref[0, :, late])
        share = 0.5 * (1.0 + lax.erf(hidden * 0.7071067811865476))
        active_ref[:, cols] = (hidden * share).astype(bf16)
        slope = share + hidden * (jnp.exp(-0.5 * hidden * hidden) * 0.3989422804014327)
        hidden_ref[:, cols] = (grad_active * slope).astype(bf16)
    expand, reduce = weights_ref[0, :, :hid], weights_ref[0, :, hid:]
    out_ref[...] += dot_last(active_ref[...], reduce)
    back_ref[...] += dot_last(hidden_ref[...], expand)
    grads_ref[0, :, :hid] = dot_first(feed_ref[...], hidden_ref[...]).astype(bf16)
    grads_ref[0, :, hid:] = dot_first(grad_ref[...], active_ref[...]).astype(bf16)

    @pl.when(step == pl.num_programs(0) - 1)
    def _():
        def finish(r0):
            rows = pl.ds(r0, BLOCK)
            valid = valid_of(r0, BLOCK, ends)
            middle, out, back = middle_ref[rows, :], out_ref[rows, :], back_ref[rows, :]
            result_ref[rows, :] = (middle + out).astype(bf16)
            unit, inv = unit_of(middle)
            grad_middle_ref[rows, :] = (
                grad_ref[rows, :].astype(f32) + unit_back(back, unit, inv, gains_ref[1:2, :])
            )
            set_row(sums_ref, 0, jnp.sum(out * out * valid, axis=0, keepdims=True))
            set_row(sums_ref, 1, jnp.sum(back * unit, axis=0, keepdims=True))

        row_loop(total, BLOCK, finish)


def static_windows(total):
    spans = []
    for r0 in range(0, total, WIDE):
        low = max(0, r0 - MAXCLIP + 1) // LANES * LANES
        high = min(total, -(-(r0 + WIDE + MAXCLIP - 1) // LANES) * LANES)
        spans.append((low, high))
    width = max(high - low for low, high in spans)
    return [min(low, total - width) for low, _ in spans], width


def start_of(starts, block):
    at = jnp.int32(starts[0])
    for i, s in enumerate(starts):
        at = jnp.where(block == i, s, at)
    return pl.multiple_of(at, LANES)


def pair_forward(g, block, pair, total, qkv_ref, ends, mixed_ref, stat_ref, bias_ref):
    starts, cols = static_windows(total)
    lane, low, scaled = head_masks(0.125)
    r0 = pl.multiple_of(block * WIDE, WIDE)
    k0 = start_of(starts, block)
    rows, win = pl.ds(r0, WIDE), pl.ds(k0, cols)

    @pl.when(pair == 0)
    def _():
        set_bias(bias_ref, r0, WIDE, k0, cols, ends)

    c = pl.multiple_of(pair * LANES, LANES)
    at = pl.multiple_of(g * 3 * GROUP + c, LANES)
    query = qkv_ref[rows, pl.ds(at, LANES)]
    keys = qkv_ref[win, pl.ds(at + GROUP, LANES)]
    values = qkv_ref[win, pl.ds(at + 2 * GROUP, LANES)]
    values = jnp.concatenate([values, jnp.ones_like(values)], axis=1)
    stats, outs = stat_ref[rows, :], []
    for h, mask in enumerate(scaled):
        scores = dot_last(query * mask, keys) + bias_ref[:, :cols]
        top = jnp.max(scores, axis=1, keepdims=True)
        mixed = dot_plain(jnp.exp(scores - top).astype(bf16), values)
        row_sum = mixed[:, LANES:]
        outs.append(mixed[:, :LANES] / row_sum)
        stats = jnp.where(lane == 4 * g + 2 * pair + h, top + jnp.log(row_sum), stats)
    stat_ref[rows, :] = stats
    mixed_ref[rows, pl.ds(pl.multiple_of(g * GROUP + c, LANES), LANES)] = jnp.where(low, outs[0], outs[1]).astype(bf16)


def pair_back(g, block, pair, total, qkv_ref, ends, grad_ref, lse_ref, inner_ref, dqkv_ref, bias_ref, dq_ref):
    starts, cols = static_windows(total)
    _, low, scaled = head_masks(0.125)
    _, _, plain = head_masks(1.0)
    r0 = pl.multiple_of(block * WIDE, WIDE)
    q0 = start_of(starts, block)
    rows, win = pl.ds(r0, WIDE), pl.ds(q0, cols)

    @pl.when(pair == 0)
    def _():
        set_bias(bias_ref, r0, WIDE, q0, cols, ends)

    c = pl.multiple_of(pair * LANES, LANES)
    at = pl.multiple_of(g * 3 * GROUP + c, LANES)
    keys = qkv_ref[rows, pl.ds(at + GROUP, LANES)]
    values = qkv_ref[rows, pl.ds(at + 2 * GROUP, LANES)]
    query = qkv_ref[win, pl.ds(at, LANES)]
    grad = grad_ref[win, pl.ds(pl.multiple_of(g * GROUP + c, LANES), LANES)]
    dk, dv, dq = [], [], 0.0
    for h in range(2):
        one = pl.ds(4 * g + 2 * pair + h, 1)
        key = keys * scaled[h]
        scores = dot_last(key, query) + bias_ref[:, :cols]
        probs = jnp.exp(scores - lse_ref[one, win])
        dv.append(dot_plain(probs.astype(bf16), grad))
        grad_probs = dot_last(values * plain[h], grad)
        ds = (probs * (grad_probs - inner_ref[one, win])).astype(bf16)
        dk.append(dot_plain(ds, query))
        dq = dq + dot_first(ds, key)
    dq_ref[win, pl.ds(c, LANES)] += dq
    dqkv_ref[rows, pl.ds(GROUP + c, LANES)] = (jnp.where(low, dk[0], dk[1]) * 0.125).astype(bf16)
    dqkv_ref[rows, pl.ds(2 * GROUP + c, LANES)] = jnp.where(low, dv[0], dv[1]).astype(bf16)


def backward_kernel(
    net,
    clip_ref, grad_middle_ref, mixed_ref, qkv_hbm, lse_ref, normed_hbm, tokens_hbm, weights_hbm, gains_ref,
    *refs,
):
    total, width = mixed_ref.shape
    ends = clip_ends(clip_ref)
    refs, load_sem, store_sem = refs[:-2], *refs[-2:]
    refs, (qkv_ref, normed_ref, group_ref, sum_ref) = refs[:-4], refs[-4:]

    def load(slot, start, size):
        return pltpu.make_async_copy(
            weights_hbm.at[:, pl.ds(start, size)], group_ref.at[slot, :, pl.ds(0, size)], load_sem.at[slot]
        )

    weight = load(0, 0, width)
    weight.start()
    inputs = [
        pltpu.make_async_copy(qkv_hbm, qkv_ref, load_sem.at[2]),
        pltpu.make_async_copy(normed_hbm, normed_ref, load_sem.at[3]),
    ]
    for copy in inputs:
        copy.start()
    if net is None:
        grads_ref, grad_tokens_ref, low_ref, grad_ref, dqkv_ref, dq_ref, stat_ref, inner_ref, bias_ref = refs
        plan = {}
    else:
        sums_ref, feed_grads_ref, *owned = refs[:6]
        *outs, grad_tokens_ref = refs[6:14]
        low_ref, grad_ref, dqkv_ref, dq_ref, stat_ref, inner_ref, bias_ref, grads_ref, own_ref = refs[14:23]
        shard_ref, shard_feed_ref, send, recv, local, *bufs = refs[23:]
        net.locate()
        net.enter()
        sems = Sems(send, recv)
        feed, att = [], []
        for lanes, along in feed_folds(feed_grads_ref.shape[-1]):
            feed.append(Fold(net, sems, feed_grads_ref, BOTH[::-1], lanes, along, bufs[:4], shard_feed_ref, own_ref))
            bufs = bufs[4:]
        for lanes, along in att_folds(width):
            att.append(Fold(net, sems, grads_ref, BOTH, lanes, along, bufs[:4], shard_ref))
            bufs = bufs[4:]
        for p in feed:
            p.send(0)
        mine = tuple(net.place["c"] if n == "c" else slice(None) for n in net.names(BOTH[::-1]))
        own = pltpu.make_async_copy(feed_grads_ref.at[mine], own_ref, local)
        own.start()
        tall = jnp.concatenate([sums_ref[...], jnp.zeros((LANES - 8, width), f32)], axis=0).T
        lane = lax.broadcasted_iota(jnp.int32, (1, LANES), 1)
        for j in range(1, 4):
            tall = jnp.where(lane == j, jnp.sum(sums_ref[j : j + 1, :], axis=1, keepdims=True), tall)
        extras = jnp.where(lane == 4, ends[-1].astype(f32), tall)

    def advance(*moves):
        for piece, step in moves:
            piece.add(step)
            if step < 3:
                piece.send(step + 1)

    def store(lanes, value):
        if net is None:
            grads_ref[:, lanes] = value.astype(bf16)
        else:
            rows = grads_ref.shape[-2]
            for i, index in enumerate(np.ndindex(*net.dims(BOTH))):
                grads_ref[index + (slice(None), lanes)] = value[i * rows : (i + 1) * rows].astype(bf16)

    if net is not None:
        store(slice(width, width + LANES), extras)
    low_ref[...] = grad_middle_ref[...].astype(bf16)
    store(slice(0, width), dot_first(mixed_ref[...], low_ref[...]))
    weight.wait()
    grad_ref[...] = dot_last(low_ref[...], group_ref[0]).astype(bf16)
    weight = load(1, group_lanes(width, 0).start, 3 * GROUP)
    weight.start()
    tokens_ref = low_ref
    tokens = pltpu.make_async_copy(tokens_hbm, tokens_ref, load_sem.at[4])
    tokens.start()
    inner_sums(grad_ref, mixed_ref, stat_ref)
    inner_ref[...] = stat_ref[...].T[: inner_ref.shape[0]]
    if net is not None:
        for p in att[:2]:
            p.send(0)
        own.wait()
        plan = {
            (0, 0): [(p, 0) for p in feed],
            (0, 1): [(att[0], 0), (att[1], 0)],
            (0, 3): [(p, 1) for p in feed[:2]],
            (1, 1): [(att[2], 0), (att[3], 0)] + [(p, 2) for p in feed[:2]],
            (1, 2): [(p, 1) for p in feed[2:4]],
            (2, 0): [(p, 1) for p in feed[4:]] + [(att[0], 1), (att[1], 1)] + [(p, 2) for p in feed[2:4]],
            (2, 1): [(att[4], 0), (att[5], 0)] + [(p, 2) for p in feed[4:]] + [(att[0], 2), (att[1], 2)],
            (2, 2): [(att[2], 1), (att[3], 1)] + [(p, 3) for p in feed[:2]],
            (2, 3): [(att[2], 2), (att[3], 2), (att[4], 1), (att[5], 1)],
        }
    for copy in inputs:
        copy.wait()
    for g in range(width // GROUP):
        dq_ref[...] = jnp.zeros_like(dq_ref)

        def step(i, carry, g=g):
            for j in range(4):
                moves = plan.get((g, j))
                if moves:
                    pl.when(i == j)(lambda moves=moves: advance(*moves))
            pair_back(
                g, i // 2, i % 2, total, qkv_ref, ends, grad_ref, lse_ref, inner_ref, dqkv_ref, bias_ref, dq_ref
            )
            return carry

        lax.fori_loop(0, 2 * total // WIDE, step, 0)
        dqkv_ref[:, :GROUP] = dq_ref[...].astype(bf16)
        lanes = group_lanes(width, g)
        store(lanes, dot_first(normed_ref[...], dqkv_ref[...]))
        if net is not None:
            for p in att[2 + 2 * g : 4 + 2 * g]:
                p.send(0)
        weight.wait()
        back = dot_last(dqkv_ref[...], group_ref[(g + 1) % 2])
        if g + 1 < width // GROUP:
            weight = load(g % 2, group_lanes(width, g + 1).start, 3 * GROUP)
            weight.start()
        if g == 0:
            sum_ref[...] = back
        else:
            sum_ref[...] += back
    if net is not None:
        advance((att[6], 0), (att[7], 0))
    tokens.wait()
    finals = []
    for b in range(total // BLOCK):
        rows = pl.ds(b * BLOCK, BLOCK)
        unit, inv = unit_of(tokens_ref[rows, :].astype(f32))
        sum_ref[rows, :] = grad_middle_ref[rows, :] + unit_back(sum_ref[rows, :], unit, inv, gains_ref[0:1, :])
        finals.append(pltpu.make_async_copy(sum_ref.at[rows], grad_tokens_ref.at[rows], store_sem.at[b]))
        finals[-1].start()
    if net is not None:
        advance((att[6], 1), (att[7], 1), (att[4], 2), (att[5], 2), (att[0], 3), (att[1], 3))
        advance(*((p, 3) for p in feed[2:]))
        advance((att[6], 2), (att[7], 2), (att[2], 3), (att[3], 3), (att[4], 3), (att[5], 3))
        query_ref, key_ref, value_ref, output_ref, expand_ref, reduce_ref, tile_ref = outs
        output_ref[...] = shard_ref[:, :width]
        for k in range(expand_ref.shape[1] // GROUP):
            cols = slice(k * GROUP, (k + 1) * GROUP)
            expand_ref[:, cols] = shard_feed_ref[:, 2 * k * GROUP : (2 * k + 1) * GROUP]
            reduce_ref[cols, :] = shard_feed_ref[:, (2 * k + 1) * GROUP : (2 * k + 2) * GROUP].T
        advance((att[6], 3), (att[7], 3))
        gain = 0.0
        for j, (out, weight) in enumerate(zip((query_ref, key_ref, value_ref), owned)):
            for g in range(width // GROUP):
                at = width + LANES + (3 * g + j) * GROUP
                out[:, g * GROUP : (g + 1) * GROUP] = shard_ref[:, at : at + GROUP]
            gain = gain + jnp.sum(weight[...].astype(f32) * out[...], axis=1, keepdims=True)
        gain = gain / owned[3][:, :1].astype(f32)
        lane = lax.broadcasted_iota(jnp.int32, (1, LANES), 1)
        tile = shard_ref[:, width : width + LANES]
        means = jnp.sqrt(tile / (tile[:, 4:5] * width))
        tile_ref[...] = jnp.where(lane == LANES - 1, gain, jnp.where(lane == 0, tile, means))
        for p in feed + att:
            p.drain()
    for copy in finals:
        copy.wait()


def params(**more):
    return pltpu.CompilerParams(vmem_limit_bytes=58 << 20, **more)


def shape(*dims, kind=bf16):
    return jax.ShapeDtypeStruct(dims, kind)


def run_forward(clip, tokens, weights, gains):
    total, width = tokens.shape
    return pl.pallas_call(
        forward_kernel,
        name="layer_forward",
        out_shape=(
            shape(total, 3 * width), shape(total, width), shape(16, total, kind=f32),
            shape(total, width, kind=f32), shape(total, width), shape(total, width), shape(8, width, kind=f32),
        ),
        in_specs=[SM, VM, VM, VM],
        out_specs=(VM,) * 7,
        scratch_shapes=[pltpu.VMEM((total, LANES), f32), pltpu.VMEM((BLOCK, total), f32)],
        compiler_params=params(),
        cost_estimate=pl.CostEstimate(flops=12 * 10**9, bytes_accessed=20 << 20, transcendentals=0),
    )(clip, tokens, weights, gains)


def run_feed(clip, feed, out_grad, middle, gains, weights):
    total, width = feed.shape
    parts, _, both = weights.shape
    one = pl.BlockSpec((1, width, both), lambda t: (t, 0, 0))
    return pl.pallas_call(
        feed_kernel,
        name="feed_both",
        grid=(parts,),
        out_shape=(
            shape(parts, width, both), shape(total, width), shape(total, width, kind=f32), shape(8, width, kind=f32),
        ),
        in_specs=[SM, VM, VM, VM, VM, one],
        out_specs=(one, VM, VM, VM),
        scratch_shapes=[
            pltpu.VMEM((total, width), bf16), pltpu.VMEM((total, both - width), bf16),
            pltpu.VMEM((total, both - width), bf16), pltpu.VMEM((total, width), f32), pltpu.VMEM((total, width), f32),
        ],
        compiler_params=params(),
        cost_estimate=pl.CostEstimate(flops=30 * 10**9, bytes_accessed=30 << 20, transcendentals=0),
    )(clip, feed, out_grad, middle, gains, weights)


MESH = pl.DeviceIdType.MESH
ANY = pl.BlockSpec(memory_space=pl.ANY)
FACTORS = {
    (8, 4): ((("z", 4), ("y", 2)), (("x", 2), ("c", 2))),
}


class Net:
    def __init__(self, factors):
        self.factors = factors
        self.size = {n: s for axis in factors for n, s in axis}
        self.count = 1
        for s in self.size.values():
            self.count *= s

    def locate(self):
        self.place = {}
        for name, axis in zip(BOTH, self.factors):
            left = lax.axis_index(name)
            for n, s in axis[::-1]:
                self.place[n] = lax.rem(left, s)
                left = lax.div(left, s)

    def device(self, dim, value):
        out = []
        for axis in self.factors:
            index = 0
            for n, s in axis:
                index = index * s + (value if n == dim else self.place[n])
            out.append(index)
        return tuple(out)

    def names(self, order):
        axes = dict(zip(BOTH, self.factors))
        return [n for a in order for n, _ in axes[a]]

    def dims(self, order):
        return tuple(self.size[n] for n in self.names(order))

    def view(self, ref, order, lanes, **fixed):
        index = tuple(fixed.get(n, slice(None)) for n in self.names(order))
        return ref.at[index + (slice(None), pl.ds(*lanes))]

    def peers(self, dim):
        s = self.size[dim]
        return [lax.rem(self.place[dim] + o, s) for o in range(1, s)]

    def enter(self):
        barrier, count = pltpu.get_barrier_semaphore(), 0
        for dim in self.size:
            for v in self.peers(dim):
                pl.semaphore_signal(barrier, inc=1, device_id=self.device(dim, v), device_id_type=MESH)
                count += 1
        pl.semaphore_wait(barrier, count)


class Sems:
    def __init__(self, send, recv):
        self.send, self.recv, self.used = send, recv, 0

    def take(self):
        self.used += 1
        return self.send.at[self.used - 1], self.recv.at[self.used - 1]


def spread(net, sems, dim, source, target):
    out = []
    for v in net.peers(dim):
        send, recv = sems.take()
        out.append(
            pltpu.make_async_remote_copy(
                src_ref=source, dst_ref=target, send_sem=send, recv_sem=recv,
                device_id=net.device(dim, v), device_id_type=MESH,
            )
        )
    return out


def begin(copies):
    for copy in copies:
        copy.start()


def arrive(copies):
    for copy in copies:
        copy.wait_recv()


class Piece:
    def __init__(self, net, sems, mine, ref, order, lanes, first, second):
        def block(free, **other):
            fixed = {n: v for n, v in net.place.items() if n not in free}
            return net.view(ref, order, lanes, **{**fixed, **other})

        def pass_on(dim, part):
            return spread(net, sems, dim, part, part)

        self.z = spread(net, sems, "z", mine.at[:, pl.ds(*lanes)], block(()))
        self.one = pass_on(first, block(("z",)))
        self.two = pass_on(second, block(("z", first)))
        self.twins = [
            pass_on("c", block(("z",))),
            sum((pass_on("c", block(("z",), **{first: v})) for v in net.peers(first)), []),
            sum((pass_on("c", block(("z", first), **{second: v})) for v in net.peers(second)), []),
        ]

    def start(self):
        begin(self.z)

    def step_one(self):
        arrive(self.z)
        begin(self.one + self.twins[0])

    def step_two(self):
        arrive(self.one)
        begin(self.two + self.twins[1])

    def step_three(self):
        arrive(self.two)
        begin(self.twins[2])

    def ready(self):
        arrive(sum(self.twins, []))

    def drain(self):
        for copy in self.z + self.one + self.two + sum(self.twins, []):
            copy.wait_send()


def copies_of(net):
    z, y, x, c = (net.size[n] - 1 for n in "zyxc")
    return z + y + x + c * (1 + y + x)


def lane_parts(width, count):
    tiles, out, at = width // LANES, [], 0
    for i in range(count):
        take = (tiles - at) // (count - i)
        out.append((at * LANES, take * LANES))
        at += take
    return out


ORDERS = (("y", "x"), ("x", "y"))


def att_spans(width):
    start = width + LANES
    spans = [(width, LANES + 3 * GROUP)]
    spans += [(start + g * 3 * GROUP, 3 * GROUP) for g in range(1, width // GROUP)]
    return spans + [(0, width)]


def halves(start, size):
    return [(start + at, take) for at, take in lane_parts(size, 2)]


def fused_forward_kernel(
    net,
    clip_ref, tokens_ref, w_reduce_ref, out_grad_ref, w_query_ref, w_key_ref, w_value_ref, w_output_ref, gain_ref,
    w_expand_ref,
    att_all, feed_all, qkv_hbm, mixed_hbm, lse_ref, normed_hbm, grads_ref, result_hbm, grad_middle_hbm, sums_ref,
    gains_ref, qkv_ref, mixed_ref, normed_ref, result_ref, grad_middle_ref, store_sem, mine_ref, both_ref, gain_tile_ref, group_ref, grad_ref, middle_ref, feed_ref, active_ref, hidden_ref, out_ref,
    chunk_ref, stage_ref, stat_ref, bias_ref, send, recv, local, chunk_sem, stage_sem,
):
    total, width = tokens_ref.shape
    groups = width // GROUP
    hid = w_expand_ref.shape[1]
    chunks = hid // GROUP
    ends = clip_ends(clip_ref)
    flip = BOTH[::-1]
    net.locate()

    moves = [(w_output_ref, mine_ref.at[:, pl.ds(0, width)]), (gain_ref, mine_ref.at[:, pl.ds(width, LANES)])]
    for g in range(groups):
        for j, ref in enumerate((w_query_ref, w_key_ref, w_value_ref)):
            at = width + LANES + (3 * g + j) * GROUP
            moves.append((ref.at[:, pl.ds(g * GROUP, GROUP)], mine_ref.at[:, pl.ds(at, GROUP)]))
    for k in range(chunks):
        moves.append((w_expand_ref.at[:, pl.ds(k * GROUP, GROUP)], both_ref.at[:, pl.ds(2 * k * GROUP, GROUP)]))
    copies = [pltpu.make_async_copy(src, dst, local.at[i]) for i, (src, dst) in enumerate(moves)]
    used = len(copies)
    copies.append(pltpu.make_async_copy(out_grad_ref, grad_ref, local.at[used]))
    for copy in copies:
        copy.start()
    turned = w_reduce_ref[...].T
    for k in range(chunks):
        both_ref[:, (2 * k + 1) * GROUP : (2 * k + 2) * GROUP] = turned[:, k * GROUP : (k + 1) * GROUP]
    for copy in copies[:used]:
        copy.wait()
    net.enter()
    sems = Sems(send, recv)
    att = [
        [Piece(net, sems, mine_ref, att_all, BOTH, lanes, *ORDERS[i]) for i, lanes in enumerate(halves(*span))]
        for span in att_spans(width)
    ]
    feed = [
        [
            Piece(net, sems, both_ref, feed_all, flip, lanes, *ORDERS[i])
            for i, lanes in enumerate(halves(2 * k * GROUP, 2 * GROUP))
        ]
        for k in range(chunks)
    ]
    own = [
        pltpu.make_async_copy(mine_ref, net.view(att_all, BOTH, (0, mine_ref.shape[1]), **net.place), local.at[0]),
        pltpu.make_async_copy(both_ref, net.view(feed_all, flip, (0, both_ref.shape[1]), **net.place), local.at[1]),
    ]
    for copy in own:
        copy.start()

    def act(*moves):
        for name, pair in moves:
            for piece in pair:
                getattr(piece, name)()

    first, *others, last = att
    act(("start", first), ("start", others[0]))
    sums_ref[...] = jnp.zeros_like(sums_ref)
    copies[used].wait()
    for copy in own:
        copy.wait()

    def norm(r0):
        rows = pl.ds(r0, BLOCK)
        x = tokens_ref[rows, :].astype(f32)
        valid = valid_of(r0, BLOCK, ends)
        middle_ref[rows, :] = unit_of(x)[0]
        grad_ref[rows, :] = (grad_ref[rows, :].astype(f32) * valid).astype(bf16)
        set_row(sums_ref, 1, jnp.sum(x * x * valid, axis=0, keepdims=True))

    row_loop(total, BLOCK, norm)
    act(("step_one", first), ("start", others[1]), ("start", last))
    act(("step_one", others[0]), ("step_two", first), ("start", feed[0]))
    act(("step_one", others[1]), ("step_two", others[0]), ("step_three", first), ("ready", first))

    def fetch(lanes, target, sem):
        return pltpu.make_async_copy(net.view(att_all, BOTH, lanes), target, sem)

    def flat(value):
        return value.reshape(width, value.shape[-1])

    tile = fetch((width, LANES), gain_tile_ref, local.at[0])
    tile.start()
    weight = fetch((width + LANES, 3 * GROUP), group_ref.at[0], local.at[1])
    weight.start()
    tile.wait()
    gains_ref[...] = flat(gain_tile_ref[...].astype(f32)).T[:8]

    def scale(r0):
        rows = pl.ds(r0, BLOCK)
        normed_ref[rows, :] = (middle_ref[rows, :] * gains_ref[0:1, :]).astype(bf16)

    row_loop(total, BLOCK, scale)
    plan = {
        (0, 0): [("step_one", last), ("step_two", others[1]), ("step_three", others[0])],
        (0, 2): [("step_two", last), ("step_one", feed[0]), ("start", feed[1]), ("ready", others[0])],
        (0, 3): [("step_three", others[1])],
        (1, 0): [("step_three", last), ("step_two", feed[0]), ("ready", others[1])],
        (1, 2): [("step_one", feed[1]), ("start", feed[2]), ("ready", last)],
        (2, 0): [("step_three", feed[0]), ("step_two", feed[1])],
        (2, 2): [("step_one", feed[2])],
    }
    for g in range(groups):
        weight.wait()
        cols = slice(g * 3 * GROUP, (g + 1) * 3 * GROUP)
        qkv_ref[:, cols] = dot_plain(normed_ref[...], flat(group_ref[g % 2])).astype(bf16)

        def step(i, carry, g=g):
            for j in range(4):
                todo = plan.get((g, j))
                if todo:
                    pl.when(i == j)(lambda todo=todo: act(*todo))
            pair_forward(g, i // 2, i % 2, total, qkv_ref, ends, mixed_ref, stat_ref, bias_ref)
            return carry

        lax.fori_loop(0, 2 * total // WIDE, step, 0)
        start = width + LANES + (g + 1) * 3 * GROUP if g + 1 < groups else 0
        weight = fetch((start, 3 * GROUP), group_ref.at[(g + 1) % 2], local.at[1])
        weight.start()
    outs = [
        pltpu.make_async_copy(ref, target, store_sem.at[i])
        for i, (ref, target) in enumerate(((qkv_ref, qkv_hbm), (mixed_ref, mixed_hbm), (normed_ref, normed_hbm)))
    ]
    for copy in outs:
        copy.start()
    lse_ref[...] = stat_ref[...].T[: lse_ref.shape[0]]
    weight.wait()
    middle_ref[...] = dot_plain(mixed_ref[...], flat(group_ref[groups % 2]))

    def second(r0):
        rows = pl.ds(r0, BLOCK)
        branch = middle_ref[rows, :]
        middle = tokens_ref[rows, :].astype(f32) + branch
        middle_ref[rows, :] = middle
        feed_ref[rows, :] = (unit_of(middle)[0] * gains_ref[1:2, :]).astype(bf16)
        set_row(sums_ref, 2, jnp.sum(branch * branch * valid_of(r0, BLOCK, ends), axis=0, keepdims=True))

    row_loop(total, BLOCK, second)
    act(("ready", feed[0]), ("step_three", feed[1]), ("step_two", feed[2]))

    tp = net.names(("tp",))
    quarters = list(np.ndindex(*(net.size[n] for n in tp)))
    both_kinds = range(2)

    def place(ref, quarter, kind, k):
        at = (2 * k + kind) * GROUP
        at = at if isinstance(at, int) else pl.multiple_of(at, GROUP)
        return ref.at[quarter + (slice(None),) * (len(ref.shape) - len(quarter) - 1) + (pl.ds(at, GROUP),)]

    def part(ref, q):
        return ref.at[(slice(None),) * (len(ref.shape) - 1) + (pl.ds(q * GROUP, GROUP),)]

    def chunk_copies(k, slot):
        return [
            pltpu.make_async_copy(
                place(feed_all, quarter, kind, k), part(chunk_ref.at[slot, kind], q), chunk_sem.at[slot, kind, q]
            )
            for kind in both_kinds
            for q, quarter in enumerate(quarters)
        ]

    def stage_copies(k):
        return [
            pltpu.make_async_copy(part(stage_ref.at[kind], q), place(grads_ref, quarter, kind, k), stage_sem.at[kind, q])
            for kind in both_kinds
            for q, quarter in enumerate(quarters)
        ]

    for copy in chunk_copies(0, 0):
        copy.start()
    out_ref[...] = jnp.zeros_like(out_ref)
    grad_middle_ref[...] = jnp.zeros_like(grad_middle_ref)

    def chunk(k, carry):
        slot = lax.rem(k, 2)
        for copy in chunk_copies(k, slot):
            copy.wait()

        def weights(kind):
            return chunk_ref[slot, kind].reshape(width, len(quarters) * GROUP)

        for q in range(len(quarters)):
            cols = slice(q * GROUP, (q + 1) * GROUP)
            hidden = dot_plain(feed_ref[...], weights(0)[:, cols])
            grad_active = dot_plain(grad_ref[...], weights(1)[:, cols])
            share = 0.5 * (1.0 + lax.erf(hidden * 0.7071067811865476))
            active_ref[:, cols] = (hidden * share).astype(bf16)
            slope = share + hidden * (jnp.exp(-0.5 * hidden * hidden) * 0.3989422804014327)
            hidden_ref[:, cols] = (grad_active * slope).astype(bf16)
        for j in range(chunks - 1):

            @pl.when(k == j)
            def _(j=j):
                if j + 2 < chunks:
                    act(("ready", feed[j + 1]), ("step_three", feed[j + 2]))
                else:
                    act(("ready", feed[j + 1]))
                for copy in chunk_copies(j + 1, (j + 1) % 2):
                    copy.start()

        out_ref[...] += dot_last(active_ref[...], weights(1))
        grad_middle_ref[...] += dot_last(hidden_ref[...], weights(0))

        @pl.when(k > 0)
        def _():
            for copy in stage_copies(k - 1):
                copy.wait()

        for kind, (left, right) in enumerate(((feed_ref, hidden_ref), (grad_ref, active_ref))):
            stage_ref[kind] = dot_first(left[...], right[...]).reshape(stage_ref.shape[1:]).astype(bf16)
        for copy in stage_copies(k):
            copy.start()
        return carry

    lax.fori_loop(0, chunks, chunk, 0)

    for i in range(total // BLOCK):
        rows = pl.ds(i * BLOCK, BLOCK)
        middle, out, back = middle_ref[rows, :], out_ref[rows, :], grad_middle_ref[rows, :]
        result_ref[rows, :] = (middle + out).astype(bf16)
        unit, inv = unit_of(middle)
        grad_middle_ref[rows, :] = grad_ref[rows, :].astype(f32) + unit_back(back, unit, inv, gains_ref[1:2, :])
        set_row(sums_ref, 3, jnp.sum(out * out * valid_of(i * BLOCK, BLOCK, ends), axis=0, keepdims=True))
        set_row(sums_ref, 0, jnp.sum(back * unit, axis=0, keepdims=True))
        for j, (ref, target) in enumerate(((result_ref, result_hbm), (grad_middle_ref, grad_middle_hbm))):
            outs.append(pltpu.make_async_copy(ref.at[rows], target.at[rows], store_sem.at[3 + 2 * i + j]))
            outs[-1].start()
    for copy in outs:
        copy.wait()
    for copy in stage_copies(chunks - 1):
        copy.wait()
    for pair in att + feed:
        for piece in pair:
            piece.drain()


def run_fused_forward(net, clip, tokens, out_grad, weights, gain_tile, w_expand, w_reduce):
    total, width = tokens.shape
    rows, rows_feed = width // net.count, w_expand.shape[0]
    lanes, hid = 4 * width + LANES, w_expand.shape[1]
    flip = BOTH[::-1]
    ff = (*net.dims(flip), rows_feed, 2 * hid)
    wide = GROUP * int(np.prod(net.dims(("tp",))))
    inner = tuple(net.size[n] for n in net.names(("dp",))) + (rows_feed, wide)
    count = 2 * (len(att_spans(width)) + hid // GROUP) * copies_of(net)
    dma = pltpu.SemaphoreType.DMA
    return pl.pallas_call(
        lambda *refs: fused_forward_kernel(net, *refs),
        name="layer_forward_feed",
        out_shape=(
            shape(*net.dims(BOTH), rows, lanes), shape(*ff), shape(total, 3 * width), shape(total, width),
            shape(16, total, kind=f32), shape(total, width), shape(*ff), shape(total, width),
            shape(total, width, kind=f32), shape(8, width, kind=f32), shape(8, width, kind=f32),
        ),
        in_specs=[SM, VM, VM] + [ANY] * 7,
        out_specs=(ANY, ANY, ANY, ANY, VM, ANY, ANY, ANY, ANY, VM, VM),
        scratch_shapes=[
            pltpu.VMEM((total, 3 * width), bf16), pltpu.VMEM((total, width), bf16), pltpu.VMEM((total, width), bf16),
            pltpu.VMEM((total, width), bf16), pltpu.VMEM((total, width), f32), dma((3 + 2 * total // BLOCK,)),
            pltpu.VMEM((rows, lanes), bf16), pltpu.VMEM((rows_feed, 2 * hid), bf16), pltpu.VMEM((*net.dims(BOTH), rows, LANES), bf16),
            pltpu.VMEM((2, *net.dims(BOTH), rows, 3 * GROUP), bf16), pltpu.VMEM((total, width), bf16),
            pltpu.VMEM((total, width), f32), pltpu.VMEM((total, width), bf16), pltpu.VMEM((total, wide), bf16),
            pltpu.VMEM((total, wide), bf16), pltpu.VMEM((total, width), f32), pltpu.VMEM((2, 2, *inner), bf16),
            pltpu.VMEM((2, *inner), bf16), pltpu.VMEM((total, LANES), f32),
            pltpu.VMEM((WIDE, static_windows(total)[1]), f32),
            dma((count,)), dma((count,)),
            dma((4 + 3 * (width // GROUP) + hid // GROUP,)), dma((2, 2, wide // GROUP)), dma((2, wide // GROUP)),
        ],
        compiler_params=params(collective_id=1, has_side_effects=True),
    )(clip, tokens, w_reduce, out_grad, *weights, gain_tile, w_expand)


def store_at(ref, index, lanes, value):
    ref[tuple(index) + (slice(None), lanes)] = value


def each(dims, body):
    count = 1
    for s in dims:
        count *= s

    def step(i, carry):
        index, left = [], i
        for s in dims[::-1]:
            index.append(lax.rem(left, s))
            left = lax.div(left, s)
        body(tuple(index[::-1]))
        return carry

    lax.fori_loop(0, count, step, 0)


class Fold:
    def __init__(self, net, sems, ref, order, lanes, along, bufs, out, own=None):
        self.net, self.lanes, self.along, self.bufs, self.out = net, lanes, along, bufs, out
        names = net.names(order)
        self.names = [[n for n in names if n not in along[:k]] for k in range(5)]
        self.start = ref if own is None else None
        self.own = own
        self.copies = []
        for k, dim in enumerate(along):
            source, cols = (ref, lanes) if k == 0 else (bufs[k - 1].at[0], (0, lanes[1]))
            copies = []
            for o, v in enumerate(net.peers(dim)):
                index = tuple(v if n == dim else slice(None) for n in self.names[k])
                s, r = sems.take()
                copies.append(
                    pltpu.make_async_remote_copy(
                        src_ref=source.at[index + (slice(None), pl.ds(*cols))], dst_ref=bufs[k].at[o],
                        send_sem=s, recv_sem=r, device_id=net.device(dim, v), device_id_type=MESH,
                    )
                )
            self.copies.append(copies)

    @staticmethod
    def buffers(net, order, rows, lanes, along):
        names, out = net.names(order), []
        for k, dim in enumerate(along):
            left = [net.size[n] for n in names if n not in along[: k + 1]]
            out.append(pltpu.VMEM((net.size[dim] - 1, *left, rows, lanes[1]), bf16))
        return out

    def send(self, k):
        for copy in self.copies[k]:
            copy.start()

    def add(self, k):
        arrive(self.copies[k])
        dim, buf, cols = self.along[k], self.bufs[k], slice(0, self.lanes[1])
        here = self.net.place[dim]
        wide = pl.ds(*self.lanes)

        def one(index):
            at = dict(zip(self.names[k + 1], index))
            full = tuple(at.get(n, here) for n in self.names[k])
            if k > 0:
                total = self.bufs[k - 1][(0,) + full + (slice(None), cols)].astype(f32)
            elif self.own is not None:
                total = self.own[index + (slice(None), wide)].astype(f32)
            else:
                total = self.start[full + (slice(None), wide)].astype(f32)
            terms = [total] + [buf[(o,) + index].astype(f32) for o in range(self.net.size[dim] - 1)]
            if len(terms) > 2:
                size = len(terms)
                total = 0.0
                for v in range(size):
                    back = lax.rem(here - v + size, size)
                    term = terms[0]
                    for o in range(1, size):
                        term = jnp.where(back == o, terms[o], term)
                    total = total + term
            else:
                total = terms[0] + terms[1]
            if k == 3:
                self.out[:, wide] = total
            else:
                buf[(0,) + index] = total.astype(bf16)

        each([self.net.size[n] for n in self.names[k + 1]], one)

    def drain(self):
        for copies in self.copies:
            for copy in copies:
                copy.wait_send()


ALONG = (("c", "x", "y", "z"), ("c", "y", "x", "z"))


def feed_folds(width):
    return [(lanes, ALONG[i % 2]) for i, lanes in enumerate(lane_parts(width, width // GROUP))]


def att_folds(width):
    out = []
    spans = [(0, width + LANES)] + [(width + LANES + g * 3 * GROUP, 3 * GROUP) for g in range(width // GROUP)]
    for start, size in spans:
        for i, (at, take) in enumerate(lane_parts(size, 2)):
            out.append(((start + at, take), ALONG[i % 2]))
    return out


def run_backward(net, clip, grad_middle, mixed, qkv, lse, normed, tokens, weights, gains, *more_args):
    total, width = tokens.shape
    lanes = weights.shape[1]
    scratch = [
        pltpu.VMEM((total, width), bf16), pltpu.VMEM((total, width), bf16), pltpu.VMEM((total, 3 * GROUP), bf16),
        pltpu.VMEM((total, GROUP), f32), pltpu.VMEM((total, LANES), f32), pltpu.VMEM((16, total), f32),
        pltpu.VMEM((WIDE, static_windows(total)[1]), f32),
    ]
    operands = [clip, grad_middle, mixed, qkv, lse, normed, tokens, weights, gains]
    in_specs = [SM, VM, VM, ANY, VM, ANY, ANY, ANY, VM]
    out_shape = (shape(width, lanes), shape(total, width, kind=f32))
    more = {}
    if net is not None:
        feed_grads = more_args[1]
        rows, rows_feed = width // net.count, feed_grads.shape[-2]
        hid = feed_grads.shape[-1] // 2
        flip = BOTH[::-1]
        operands += more_args
        in_specs += [VM, ANY] + [VM] * 4
        out_shape = (
            *(shape(rows, width, kind=f32) for _ in range(4)), shape(rows_feed, hid, kind=f32),
            shape(hid, rows_feed, kind=f32), shape(rows, LANES, kind=f32), out_shape[1],
        )
        scratch.append(pltpu.VMEM((*net.dims(BOTH), rows, lanes), bf16))
        scratch.append(pltpu.VMEM(tuple(net.size[n] for n in net.names(flip) if n != "c") + feed_grads.shape[-2:], bf16))
        scratch += [pltpu.VMEM((rows, lanes), f32), pltpu.VMEM((rows_feed, 2 * hid), f32)]
        folds = [(flip, rows_feed, *f) for f in feed_folds(feed_grads.shape[-1])]
        folds += [(BOTH, rows, *f) for f in att_folds(width)]
        count = len(folds) * sum(net.size[n] - 1 for n in "zyxc")
        scratch += [pltpu.SemaphoreType.DMA((count,)), pltpu.SemaphoreType.DMA((count,)), pltpu.SemaphoreType.DMA]
        for f in folds:
            scratch += Fold.buffers(net, *f)
        more = dict(collective_id=2, has_side_effects=True)
    scratch += [
        pltpu.VMEM((total, 3 * width), bf16), pltpu.VMEM((total, width), bf16),
        pltpu.VMEM((2, width, 3 * GROUP), bf16), pltpu.VMEM((total, width), f32),
        pltpu.SemaphoreType.DMA((5,)), pltpu.SemaphoreType.DMA((total // BLOCK,)),
    ]
    return pl.pallas_call(
        lambda *refs: backward_kernel(net, *refs),
        name="layer_backward",
        out_shape=out_shape,
        in_specs=in_specs,
        out_specs=(VM,) * (len(out_shape) - 1) + (ANY,),
        scratch_shapes=scratch,
        compiler_params=params(**more),
        cost_estimate=pl.CostEstimate(flops=22 * 10**9, bytes_accessed=30 << 20, transcendentals=0),
    )(*operands)


def on_device(
    net,
    tokens, clip_lengths, out_grad, w_query, w_key, w_value, w_output, gain_attention, gain_feed, w_expand, w_reduce,
):
    _, total, width = tokens.shape
    rows = tokens.reshape(total, width)
    out_grad = out_grad.reshape(total, width)
    gain_tile = jnp.pad(jnp.stack([gain_attention, gain_feed], axis=1), ((0, 0), (0, LANES - 2)))
    hid = w_expand.shape[1]
    if net is not None:
        weights, _, qkv, mixed, lse, normed, feed_grads, result, grad_middle, sums, gains = run_fused_forward(
            net, clip_lengths, rows, out_grad, (w_query, w_key, w_value, w_output), gain_tile, w_expand, w_reduce
        )
        weights = weights.reshape(width, -1)
        query, key, value, output, expand, reduce, tile, grad_tokens = run_backward(
            net, clip_lengths, grad_middle, mixed, qkv, lse, normed, rows, weights, gains, sums, feed_grads,
            w_query, w_key, w_value, gain_tile,
        )
        gain_one, gain_two, means = tile[:, LANES - 1], tile[:, 0], tile[0, 1:4]
    else:
        mine = [w_output, gain_tile]
        for g in range(width // GROUP):
            mine += [w[:, g * GROUP : (g + 1) * GROUP] for w in (w_query, w_key, w_value)]
        weights = lax.all_gather(jnp.concatenate(mine, axis=1), BOTH, axis=0, tiled=True)
        both = jnp.concatenate([w_expand, w_reduce.T], axis=1)
        feed_weights = lax.all_gather(both, BOTH[::-1], axis=0, tiled=True).reshape(-1, width, 2 * hid)
        gains = jnp.pad(weights[:, width : width + 2].T.astype(f32), ((0, 6), (0, 0)))
        qkv, mixed, lse, middle, feed, normed, sums_one = run_forward(clip_lengths, rows, weights, gains)
        feed_grads, result, grad_middle, sums_two = run_feed(
            clip_lengths, feed, out_grad, middle, gains, feed_weights
        )
        count = jnp.sum(clip_lengths[:, : SLOTS - 1]).astype(f32)
        squares = jnp.stack([jnp.sum(sums_one[0]), jnp.sum(sums_one[1]), jnp.sum(sums_two[0]), count])
        grads, grad_tokens = run_backward(
            None, clip_lengths, grad_middle, mixed, qkv, lse, normed, rows, weights, gains
        )
        shard = lax.psum_scatter(grads, BOTH, scatter_dimension=0, tiled=True).astype(f32)
        shard_feed = lax.psum_scatter(
            feed_grads.reshape(-1, 2 * hid), BOTH[::-1], scatter_dimension=0, tiled=True
        ).astype(f32)
        stats = lax.psum(squares, BOTH)
        gain_two = lax.psum_scatter(sums_two[1], BOTH, scatter_dimension=0, tiled=True)
        means = jnp.sqrt(stats[:3] / (stats[3] * width))
        parts = shard[:, width + LANES :].reshape(-1, width // GROUP, 3, GROUP)
        query, key, value = (parts[:, :, j].reshape(-1, width) for j in range(3))
        pairs = ((w_query, query), (w_key, key), (w_value, value))
        gain_one = sum(jnp.sum(w.astype(f32) * g, axis=1) for w, g in pairs) / gain_attention.astype(f32)
        output, expand, reduce = shard[:, :width], shard_feed[:, :hid], shard_feed[:, hid:].T
    return (
        result.reshape(1, total, width),
        grad_tokens.reshape(1, total, width),
        query,
        key,
        value,
        output,
        gain_one,
        gain_two,
        expand,
        reduce,
        means,
    )


def solution(mesh):
    row, flat = P(BOTH, None), P(BOTH)
    whole = P(BOTH, None, None)
    in_specs = (whole, row, whole, row, row, row, row, flat, flat, P("dp", "tp"), P("tp", "dp"))
    out_specs = (whole, whole, row, row, row, row, flat, flat, P("dp", "tp"), P("tp", "dp"), P())
    factors = FACTORS.get((mesh.shape["dp"], mesh.shape["tp"]))
    net = Net(factors) if factors else None
    return jax.shard_map(
        lambda *args: on_device(net, *args), mesh=mesh, in_specs=in_specs, out_specs=out_specs, check_vma=False
    )
```

```python
import jax
import jax.numpy as jnp
import numpy as np
from jax import lax
from jax.experimental import pallas as pl
from jax.experimental.pallas import tpu as pltpu
from jax.sharding import PartitionSpec as P

HEADS = 12
HEAD_DIM = 64
SLOTS = 4
LANES = 128
BLOCK = 256
WIDE = 512
MAXCLIP = 384
GROUP = 256
NEG = -1e30
f32 = jnp.float32
bf16 = jnp.bfloat16
BOTH = ("dp", "tp")
VM = pl.BlockSpec(memory_space=pltpu.VMEM)
SM = pl.BlockSpec(memory_space=pltpu.SMEM)


def dot_plain(left, right):
    return jnp.dot(left, right, preferred_element_type=f32)


def dot_first(left, right):
    return lax.dot_general(left, right, (((0,), (0,)), ((), ())), preferred_element_type=f32)


def dot_last(left, right):
    return lax.dot_general(left, right, (((1,), (1,)), ((), ())), preferred_element_type=f32)


def unit_of(rows):
    centred = rows - jnp.mean(rows, axis=-1, keepdims=True)
    inv = lax.rsqrt(jnp.mean(centred * centred, axis=-1, keepdims=True) + 1e-06)
    return centred * inv, inv


def unit_back(grad, unit, inv, gain):
    scaled = grad * gain
    inner = (
        scaled
        - jnp.mean(scaled, axis=-1, keepdims=True)
        - unit * jnp.mean(scaled * unit, axis=-1, keepdims=True)
    )
    return inv * inner


def clip_ends(clip_ref):
    ends, total = [], jnp.int32(0)
    for j in range(SLOTS - 1):
        total = total + clip_ref[0, j]
        ends.append(total)
    return ends


def segment_of(position, ends):
    return sum((position >= e).astype(jnp.int32) for e in ends)


def valid_of(start, count, ends):
    position = start + lax.broadcasted_iota(jnp.int32, (count, 1), 0)
    return (position < ends[-1]).astype(f32)


def window_of(low, high, ends, total):
    start, stop = jnp.int32(0), jnp.int32(total)
    for e in ends:
        start = jnp.where(low >= e, e, start)
    for e in ends[::-1]:
        stop = jnp.where(high < e, e, stop)
    block = start // LANES
    return block, (stop + LANES - 1) // LANES - block


def by_width(block, count, total, run):
    most = total // LANES
    widths = [w for w in range(2, most + 1) if w != most - 1]
    before = 0
    for w in widths:

        @pl.when((count > before) & (count <= w))
        def _(w=w):
            run(pl.multiple_of(jnp.minimum(block, most - w) * LANES, LANES), w * LANES)

        before = w


def row_loop(total, size, body):
    def step(i, carry):
        body(pl.multiple_of(i * size, size))
        return carry

    lax.fori_loop(0, total // size, step, 0)


def head_masks(scale):
    lane = lax.broadcasted_iota(jnp.int32, (1, LANES), 1)
    low = lane < HEAD_DIM
    return lane, low, (jnp.where(low, scale, 0.0).astype(bf16), jnp.where(low, 0.0, scale).astype(bf16))


def set_bias(bias_ref, row_start, rows, col_start, cols, ends):
    row_seg = segment_of(row_start + lax.broadcasted_iota(jnp.int32, (rows, 1), 0), ends)
    col_seg = segment_of(col_start + lax.broadcasted_iota(jnp.int32, (1, cols), 1), ends)
    bias_ref[:, :cols] = jnp.where(row_seg == col_seg, 0.0, NEG)


def attend(qkv_ref, ends, mixed_ref, stat_ref, bias_ref):
    total, width = mixed_ref.shape
    lane, low, scaled = head_masks(0.125)

    def block(r0):
        rows = pl.ds(r0, BLOCK)

        def run(k0, cols):
            win = pl.ds(k0, cols)
            set_bias(bias_ref, r0, BLOCK, k0, cols, ends)

            def pair(p, carry):
                c = pl.multiple_of(p * LANES, LANES)
                at = pl.multiple_of(p // 2 * (3 * GROUP) + p % 2 * LANES, LANES)
                query = qkv_ref[rows, pl.ds(at, LANES)]
                keys = qkv_ref[win, pl.ds(at + GROUP, LANES)]
                values = qkv_ref[win, pl.ds(at + 2 * GROUP, LANES)]
                values = jnp.concatenate([values, jnp.ones_like(values)], axis=1)
                stats, outs = stat_ref[rows, :], []
                for h, mask in enumerate(scaled):
                    scores = dot_last(query * mask, keys) + bias_ref[:, :cols]
                    top = jnp.max(scores, axis=1, keepdims=True)
                    mixed = dot_plain(jnp.exp(scores - top).astype(bf16), values)
                    row_sum = mixed[:, LANES:]
                    outs.append(mixed[:, :LANES] / row_sum)
                    stats = jnp.where(lane == 2 * p + h, top + jnp.log(row_sum), stats)
                stat_ref[rows, :] = stats
                mixed_ref[rows, pl.ds(c, LANES)] = jnp.where(low, outs[0], outs[1]).astype(bf16)
                return carry

            lax.fori_loop(0, width // LANES, pair, 0)

        by_width(*window_of(r0, r0 + BLOCK - 1, ends, total), total, run)

    row_loop(total, BLOCK, block)


def inner_sums(grad_ref, mixed_ref, stat_ref):
    total, width = mixed_ref.shape
    lane, low, _ = head_masks(1.0)

    def block(r0):
        rows = pl.ds(r0, LANES)
        sums = jnp.zeros((LANES, LANES), f32)
        for p in range(width // LANES):
            cols = slice(p * LANES, (p + 1) * LANES)
            both = grad_ref[rows, cols].astype(f32) * mixed_ref[rows, cols].astype(f32)
            first = jnp.sum(jnp.where(low, both, 0.0), axis=1, keepdims=True)
            second = jnp.sum(jnp.where(low, 0.0, both), axis=1, keepdims=True)
            sums = jnp.where(lane == 2 * p, first, jnp.where(lane == 2 * p + 1, second, sums))
        stat_ref[rows, :] = sums

    row_loop(total, LANES, block)


def group_lanes(width, g):
    start = width + LANES + g * 3 * GROUP
    return slice(start, start + 3 * GROUP)


def set_row(ref, row, value):
    at = lax.broadcasted_iota(jnp.int32, ref.shape, 0) == row
    ref[...] += jnp.where(at, value, 0.0)


def forward_kernel(
    clip_ref, tokens_ref, weights_ref, gains_ref,
    qkv_ref, mixed_ref, lse_ref, middle_ref, feed_ref, normed_ref, sums_ref,
    stat_ref, bias_ref,
):
    total, width = tokens_ref.shape
    ends = clip_ends(clip_ref)
    sums_ref[...] = jnp.zeros_like(sums_ref)

    def norm(r0):
        rows = pl.ds(r0, BLOCK)
        x = tokens_ref[rows, :].astype(f32)
        normed_ref[rows, :] = (unit_of(x)[0] * gains_ref[0:1, :]).astype(bf16)
        set_row(sums_ref, 0, jnp.sum(x * x * valid_of(r0, BLOCK, ends), axis=0, keepdims=True))

    row_loop(total, BLOCK, norm)
    for g in range(width // GROUP):
        cols = slice(g * 3 * GROUP, (g + 1) * 3 * GROUP)
        qkv_ref[:, cols] = dot_plain(normed_ref[...], weights_ref[:, group_lanes(width, g)]).astype(bf16)
    attend(qkv_ref, ends, mixed_ref, stat_ref, bias_ref)
    lse_ref[...] = stat_ref[...].T[: lse_ref.shape[0]]
    middle_ref[...] = dot_plain(mixed_ref[...], weights_ref[:, :width])

    def second(r0):
        rows = pl.ds(r0, BLOCK)
        branch = middle_ref[rows, :]
        middle = tokens_ref[rows, :].astype(f32) + branch
        middle_ref[rows, :] = middle
        feed_ref[rows, :] = (unit_of(middle)[0] * gains_ref[1:2, :]).astype(bf16)
        set_row(sums_ref, 1, jnp.sum(branch * branch * valid_of(r0, BLOCK, ends), axis=0, keepdims=True))

    row_loop(total, BLOCK, second)


def feed_kernel(
    clip_ref, feed_ref, out_grad_ref, middle_ref, gains_ref, weights_ref,
    grads_ref, result_ref, grad_middle_ref, sums_ref,
    grad_ref, active_ref, hidden_ref, out_ref, back_ref,
):
    total, width = feed_ref.shape
    ends = clip_ends(clip_ref)
    step = pl.program_id(0)

    @pl.when(step == 0)
    def _():
        def mask(r0):
            rows = pl.ds(r0, BLOCK)
            grad_ref[rows, :] = (out_grad_ref[rows, :].astype(f32) * valid_of(r0, BLOCK, ends)).astype(bf16)

        row_loop(total, BLOCK, mask)
        out_ref[...] = jnp.zeros_like(out_ref)
        back_ref[...] = jnp.zeros_like(back_ref)
        sums_ref[...] = jnp.zeros_like(sums_ref)

    hid = weights_ref.shape[2] - width
    part = 256
    for n in range(hid // part):
        cols = slice(n * part, (n + 1) * part)
        late = slice(hid + n * part, hid + (n + 1) * part)
        hidden = dot_plain(feed_ref[...], weights_ref[0, :, cols])
        grad_active = dot_plain(grad_ref[...], weights_ref[0, :, late])
        share = 0.5 * (1.0 + lax.erf(hidden * 0.7071067811865476))
        active_ref[:, cols] = (hidden * share).astype(bf16)
        slope = share + hidden * (jnp.exp(-0.5 * hidden * hidden) * 0.3989422804014327)
        hidden_ref[:, cols] = (grad_active * slope).astype(bf16)
    expand, reduce = weights_ref[0, :, :hid], weights_ref[0, :, hid:]
    out_ref[...] += dot_last(active_ref[...], reduce)
    back_ref[...] += dot_last(hidden_ref[...], expand)
    grads_ref[0, :, :hid] = dot_first(feed_ref[...], hidden_ref[...]).astype(bf16)
    grads_ref[0, :, hid:] = dot_first(grad_ref[...], active_ref[...]).astype(bf16)

    @pl.when(step == pl.num_programs(0) - 1)
    def _():
        def finish(r0):
            rows = pl.ds(r0, BLOCK)
            valid = valid_of(r0, BLOCK, ends)
            middle, out, back = middle_ref[rows, :], out_ref[rows, :], back_ref[rows, :]
            result_ref[rows, :] = (middle + out).astype(bf16)
            unit, inv = unit_of(middle)
            grad_middle_ref[rows, :] = (
                grad_ref[rows, :].astype(f32) + unit_back(back, unit, inv, gains_ref[1:2, :])
            )
            set_row(sums_ref, 0, jnp.sum(out * out * valid, axis=0, keepdims=True))
            set_row(sums_ref, 1, jnp.sum(back * unit, axis=0, keepdims=True))

        row_loop(total, BLOCK, finish)


def static_windows(total):
    spans = []
    for r0 in range(0, total, WIDE):
        low = max(0, r0 - MAXCLIP + 1) // LANES * LANES
        high = min(total, -(-(r0 + WIDE + MAXCLIP - 1) // LANES) * LANES)
        spans.append((low, high))
    width = max(high - low for low, high in spans)
    return [min(low, total - width) for low, _ in spans], width


def start_of(starts, block):
    at = jnp.int32(starts[0])
    for i, s in enumerate(starts):
        at = jnp.where(block == i, s, at)
    return pl.multiple_of(at, LANES)


def pair_forward(g, block, pair, total, qkv_ref, ends, mixed_ref, stat_ref, bias_ref):
    starts, cols = static_windows(total)
    lane, low, scaled = head_masks(0.125)
    r0 = pl.multiple_of(block * WIDE, WIDE)
    k0 = start_of(starts, block)
    rows, win = pl.ds(r0, WIDE), pl.ds(k0, cols)

    @pl.when(pair == 0)
    def _():
        set_bias(bias_ref, r0, WIDE, k0, cols, ends)

    c = pl.multiple_of(pair * LANES, LANES)
    at = pl.multiple_of(g * 3 * GROUP + c, LANES)
    query = qkv_ref[rows, pl.ds(at, LANES)]
    keys = qkv_ref[win, pl.ds(at + GROUP, LANES)]
    values = qkv_ref[win, pl.ds(at + 2 * GROUP, LANES)]
    values = jnp.concatenate([values, jnp.ones_like(values)], axis=1)
    stats, outs = stat_ref[rows, :], []
    for h, mask in enumerate(scaled):
        scores = dot_last(query * mask, keys) + bias_ref[:, :cols]
        top = jnp.max(scores, axis=1, keepdims=True)
        mixed = dot_plain(jnp.exp(scores - top).astype(bf16), values)
        row_sum = mixed[:, LANES:]
        outs.append(mixed[:, :LANES] / row_sum)
        stats = jnp.where(lane == 4 * g + 2 * pair + h, top + jnp.log(row_sum), stats)
    stat_ref[rows, :] = stats
    mixed_ref[rows, pl.ds(pl.multiple_of(g * GROUP + c, LANES), LANES)] = jnp.where(low, outs[0], outs[1]).astype(bf16)


def pair_back(g, block, pair, total, qkv_ref, ends, grad_ref, lse_ref, inner_ref, dqkv_ref, bias_ref, dq_ref):
    starts, cols = static_windows(total)
    _, low, scaled = head_masks(0.125)
    _, _, plain = head_masks(1.0)
    r0 = pl.multiple_of(block * WIDE, WIDE)
    q0 = start_of(starts, block)
    rows, win = pl.ds(r0, WIDE), pl.ds(q0, cols)

    @pl.when(pair == 0)
    def _():
        set_bias(bias_ref, r0, WIDE, q0, cols, ends)

    c = pl.multiple_of(pair * LANES, LANES)
    at = pl.multiple_of(g * 3 * GROUP + c, LANES)
    keys = qkv_ref[rows, pl.ds(at + GROUP, LANES)]
    values = qkv_ref[rows, pl.ds(at + 2 * GROUP, LANES)]
    query = qkv_ref[win, pl.ds(at, LANES)]
    grad = grad_ref[win, pl.ds(pl.multiple_of(g * GROUP + c, LANES), LANES)]
    dk, dv, dq = [], [], 0.0
    for h in range(2):
        one = pl.ds(4 * g + 2 * pair + h, 1)
        key = keys * scaled[h]
        scores = dot_last(key, query) + bias_ref[:, :cols]
        probs = jnp.exp(scores - lse_ref[one, win])
        dv.append(dot_plain(probs.astype(bf16), grad))
        grad_probs = dot_last(values * plain[h], grad)
        ds = (probs * (grad_probs - inner_ref[one, win])).astype(bf16)
        dk.append(dot_plain(ds, query))
        dq = dq + dot_first(ds, key)
    dq_ref[win, pl.ds(c, LANES)] += dq
    dqkv_ref[rows, pl.ds(GROUP + c, LANES)] = (jnp.where(low, dk[0], dk[1]) * 0.125).astype(bf16)
    dqkv_ref[rows, pl.ds(2 * GROUP + c, LANES)] = jnp.where(low, dv[0], dv[1]).astype(bf16)


def backward_kernel(
    net,
    clip_ref, grad_middle_ref, mixed_ref, qkv_hbm, lse_ref, normed_hbm, tokens_hbm, weights_hbm, gains_ref,
    *refs,
):
    total, width = mixed_ref.shape
    ends = clip_ends(clip_ref)
    refs, load_sem, store_sem = refs[:-2], *refs[-2:]
    refs, (qkv_ref, normed_ref, group_ref, sum_ref) = refs[:-4], refs[-4:]

    def load(slot, start, size):
        return pltpu.make_async_copy(
            weights_hbm.at[:, pl.ds(start, size)], group_ref.at[slot, :, pl.ds(0, size)], load_sem.at[slot]
        )

    weight = load(0, 0, width)
    weight.start()
    inputs = [
        pltpu.make_async_copy(qkv_hbm, qkv_ref, load_sem.at[2]),
        pltpu.make_async_copy(normed_hbm, normed_ref, load_sem.at[3]),
    ]
    for copy in inputs:
        copy.start()
    if net is None:
        grads_ref, grad_tokens_ref, low_ref, grad_ref, dqkv_ref, dq_ref, stat_ref, inner_ref, bias_ref = refs
        plan = {}
    else:
        sums_ref, feed_grads_ref, *owned = refs[:6]
        early, refs = refs[6 : 6 + 2 * EARLY], refs[2 * EARLY :]
        *outs, grad_tokens_ref = refs[6:14]
        low_ref, grad_ref, dqkv_ref, dq_ref, stat_ref, inner_ref, bias_ref, grads_ref, own_ref = refs[14:23]
        shard_ref, shard_feed_ref, send, recv, local, *bufs = refs[23:]
        net.locate()
        net.enter()
        sems = Sems(send, recv)
        feed, att = [], []
        flip = BOTH[::-1]
        for k in range(EARLY):
            for lanes, along in feed_folds(k):
                slots, bufs = [None, early[len(feed)], *bufs[:2]], bufs[2:]
                feed.append(Fold(net, sems, None, flip, lanes, along, slots, shard_feed_ref, steps=(2, 3)))
        span = 2 * GROUP * EARLY
        for k in range(EARLY, feed_grads_ref.shape[-1] // (2 * GROUP)):
            for lanes, along in feed_folds(k):

                def kept(index, start=lanes[0] - span):
                    return own_ref[index + (slice(None), pl.ds(start, GROUP))]

                feed.append(
                    Fold(net, sems, feed_grads_ref, flip, lanes, along, bufs[:4], shard_feed_ref, own=kept)
                )
                bufs = bufs[4:]
        for lanes, along in att_folds(width):
            att.append(Fold(net, sems, grads_ref, BOTH, lanes, along, bufs[:4], shard_ref))
            bufs = bufs[4:]
        early, late = feed[: 2 * EARLY], feed[2 * EARLY :]
        for p in late:
            p.send(0)
        for p in early:
            p.send(2)
        mine = tuple(net.place["c"] if n == "c" else slice(None) for n in net.names(flip))
        own = pltpu.make_async_copy(
            feed_grads_ref.at[mine + (slice(None), pl.ds(span, feed_grads_ref.shape[-1] - span))], own_ref, local
        )
        own.start()
        tall = jnp.concatenate([sums_ref[...], jnp.zeros((LANES - 8, width), f32)], axis=0).T
        lane = lax.broadcasted_iota(jnp.int32, (1, LANES), 1)
        for j in range(1, 4):
            tall = jnp.where(lane == j, jnp.sum(sums_ref[j : j + 1, :], axis=1, keepdims=True), tall)
        extras = jnp.where(lane == 4, ends[-1].astype(f32), tall)

    def advance(*moves):
        for piece, step in moves:
            piece.add(step)
            if step < 3:
                piece.send(step + 1)

    def store(lanes, value):
        if net is None:
            grads_ref[:, lanes] = value.astype(bf16)
        else:
            rows = grads_ref.shape[-2]
            for i, index in enumerate(np.ndindex(*net.dims(BOTH))):
                grads_ref[index + (slice(None), lanes)] = value[i * rows : (i + 1) * rows].astype(bf16)

    if net is not None:
        store(slice(width, width + LANES), extras)
    low_ref[...] = grad_middle_ref[...].astype(bf16)
    store(slice(0, width), dot_first(mixed_ref[...], low_ref[...]))
    weight.wait()
    grad_ref[...] = dot_last(low_ref[...], group_ref[0]).astype(bf16)
    weight = load(1, group_lanes(width, 0).start, 3 * GROUP)
    weight.start()
    tokens_ref = low_ref
    tokens = pltpu.make_async_copy(tokens_hbm, tokens_ref, load_sem.at[4])
    tokens.start()
    inner_sums(grad_ref, mixed_ref, stat_ref)
    inner_ref[...] = stat_ref[...].T[: inner_ref.shape[0]]
    if net is not None:
        for p in att[:2]:
            p.send(0)
        own.wait()
        plan = {
            (0, 0): [(p, 0) for p in late] + [(p, 2) for p in early],
            (0, 1): [(p, 0) for p in att[0:2]],
            (1, 0): [(p, 1) for p in late] + [(p, 1) for p in att[0:2]],
            (1, 1): [(p, 0) for p in att[2:4]],
            (1, 3): [(p, 2) for p in late] + [(p, 2) for p in att[0:2]] + [(p, 1) for p in att[2:4]],
            (2, 0): [(p, 3) for p in early],
            (2, 1): [(p, 0) for p in att[4:6]] + [(p, 2) for p in att[2:4]],
            (2, 3): [(p, 1) for p in att[4:6]] + [(p, 3) for p in late] + [(p, 3) for p in att[0:2]],
        }
    for copy in inputs:
        copy.wait()
    sum_ref[...] = jnp.zeros_like(sum_ref)
    groups = width // GROUP

    def group(g, carry):
        dq_ref[...] = jnp.zeros_like(dq_ref)

        def step(i, carry):
            for (a, b), moves in plan.items():
                pl.when((g == a) & (i == b))(lambda moves=moves: advance(*moves))
            pair_back(
                g, i // 2, i % 2, total, qkv_ref, ends, grad_ref, lse_ref, inner_ref, dqkv_ref, bias_ref, dq_ref
            )
            return carry

        lax.fori_loop(0, 2 * total // WIDE, step, 0)
        dqkv_ref[:, :GROUP] = dq_ref[...].astype(bf16)
        start = width + LANES + g * 3 * GROUP
        store(pl.ds(pl.multiple_of(start, LANES), 3 * GROUP), dot_first(normed_ref[...], dqkv_ref[...]))
        if net is not None:
            for k in range(groups):

                @pl.when(g == k)
                def _(k=k):
                    for p in att[2 + 2 * k : 4 + 2 * k]:
                        p.send(0)

        slot = 1 - lax.rem(g, 2)
        load(slot, 0, 3 * GROUP).wait()
        sum_ref[...] += dot_last(dqkv_ref[...], group_ref[slot])

        @pl.when(g + 1 < groups)
        def _():
            load(1 - slot, pl.multiple_of(start + 3 * GROUP, LANES), 3 * GROUP).start()

        return carry

    lax.fori_loop(0, groups, group, 0)
    if net is not None:
        advance((att[6], 0), (att[7], 0))
    tokens.wait()
    finals = []
    for b in range(total // BLOCK):
        rows = pl.ds(b * BLOCK, BLOCK)
        unit, inv = unit_of(tokens_ref[rows, :].astype(f32))
        sum_ref[rows, :] = grad_middle_ref[rows, :] + unit_back(sum_ref[rows, :], unit, inv, gains_ref[0:1, :])
        finals.append(pltpu.make_async_copy(sum_ref.at[rows], grad_tokens_ref.at[rows], store_sem.at[b]))
        finals[-1].start()
    if net is not None:
        advance((att[6], 1), (att[7], 1), (att[4], 2), (att[5], 2), (att[2], 3), (att[3], 3))
        advance((att[6], 2), (att[7], 2), (att[4], 3), (att[5], 3))
        query_ref, key_ref, value_ref, output_ref, expand_ref, reduce_ref, tile_ref = outs
        output_ref[...] = shard_ref[:, :width]
        for k in range(expand_ref.shape[1] // GROUP):
            cols = slice(k * GROUP, (k + 1) * GROUP)
            expand_ref[:, cols] = shard_feed_ref[:, 2 * k * GROUP : (2 * k + 1) * GROUP]
            reduce_ref[cols, :] = shard_feed_ref[:, (2 * k + 1) * GROUP : (2 * k + 2) * GROUP].T
        advance((att[6], 3), (att[7], 3))
        gain = 0.0
        for j, (out, weight) in enumerate(zip((query_ref, key_ref, value_ref), owned)):
            for g in range(width // GROUP):
                at = width + LANES + (3 * g + j) * GROUP
                out[:, g * GROUP : (g + 1) * GROUP] = shard_ref[:, at : at + GROUP]
            gain = gain + jnp.sum(weight[...].astype(f32) * out[...], axis=1, keepdims=True)
        gain = gain / owned[3][:, :1].astype(f32)
        lane = lax.broadcasted_iota(jnp.int32, (1, LANES), 1)
        tile = shard_ref[:, width : width + LANES]
        means = jnp.sqrt(tile / (tile[:, 4:5] * width))
        tile_ref[...] = jnp.where(lane == LANES - 1, gain, jnp.where(lane == 0, tile, means))
        for p in feed + att:
            p.drain()
    for copy in finals:
        copy.wait()


def params(**more):
    return pltpu.CompilerParams(vmem_limit_bytes=58 << 20, **more)


def shape(*dims, kind=bf16):
    return jax.ShapeDtypeStruct(dims, kind)


def run_forward(clip, tokens, weights, gains):
    total, width = tokens.shape
    return pl.pallas_call(
        forward_kernel,
        name="layer_forward",
        out_shape=(
            shape(total, 3 * width), shape(total, width), shape(16, total, kind=f32),
            shape(total, width, kind=f32), shape(total, width), shape(total, width), shape(8, width, kind=f32),
        ),
        in_specs=[SM, VM, VM, VM],
        out_specs=(VM,) * 7,
        scratch_shapes=[pltpu.VMEM((total, LANES), f32), pltpu.VMEM((BLOCK, total), f32)],
        compiler_params=params(),
        cost_estimate=pl.CostEstimate(flops=12 * 10**9, bytes_accessed=20 << 20, transcendentals=0),
    )(clip, tokens, weights, gains)


def run_feed(clip, feed, out_grad, middle, gains, weights):
    total, width = feed.shape
    parts, _, both = weights.shape
    one = pl.BlockSpec((1, width, both), lambda t: (t, 0, 0))
    return pl.pallas_call(
        feed_kernel,
        name="feed_both",
        grid=(parts,),
        out_shape=(
            shape(parts, width, both), shape(total, width), shape(total, width, kind=f32), shape(8, width, kind=f32),
        ),
        in_specs=[SM, VM, VM, VM, VM, one],
        out_specs=(one, VM, VM, VM),
        scratch_shapes=[
            pltpu.VMEM((total, width), bf16), pltpu.VMEM((total, both - width), bf16),
            pltpu.VMEM((total, both - width), bf16), pltpu.VMEM((total, width), f32), pltpu.VMEM((total, width), f32),
        ],
        compiler_params=params(),
        cost_estimate=pl.CostEstimate(flops=30 * 10**9, bytes_accessed=30 << 20, transcendentals=0),
    )(clip, feed, out_grad, middle, gains, weights)


MESH = pl.DeviceIdType.MESH
ANY = pl.BlockSpec(memory_space=pl.ANY)
FACTORS = {
    (8, 4): ((("z", 4), ("y", 2)), (("x", 2), ("c", 2))),
}


class Net:
    def __init__(self, factors):
        self.factors = factors
        self.size = {n: s for axis in factors for n, s in axis}
        self.count = 1
        for s in self.size.values():
            self.count *= s

    def locate(self):
        self.place = {}
        for name, axis in zip(BOTH, self.factors):
            left = lax.axis_index(name)
            for n, s in axis[::-1]:
                self.place[n] = lax.rem(left, s)
                left = lax.div(left, s)

    def device(self, dim, value):
        out = []
        for axis in self.factors:
            index = 0
            for n, s in axis:
                index = index * s + (value if n == dim else self.place[n])
            out.append(index)
        return tuple(out)

    def names(self, order):
        axes = dict(zip(BOTH, self.factors))
        return [n for a in order for n, _ in axes[a]]

    def dims(self, order):
        return tuple(self.size[n] for n in self.names(order))

    def view(self, ref, order, lanes, **fixed):
        index = tuple(fixed.get(n, slice(None)) for n in self.names(order))
        return ref.at[index + (slice(None), pl.ds(*lanes))]

    def peers(self, dim):
        s = self.size[dim]
        return [lax.rem(self.place[dim] + o, s) for o in range(1, s)]

    def enter(self):
        barrier, count = pltpu.get_barrier_semaphore(), 0
        for dim in self.size:
            for v in self.peers(dim):
                pl.semaphore_signal(barrier, inc=1, device_id=self.device(dim, v), device_id_type=MESH)
                count += 1
        pl.semaphore_wait(barrier, count)


class Sems:
    def __init__(self, send, recv):
        self.send, self.recv, self.used = send, recv, 0

    def take(self):
        self.used += 1
        return self.send.at[self.used - 1], self.recv.at[self.used - 1]


def spread(net, sems, dim, source, target):
    out = []
    for v in net.peers(dim):
        send, recv = sems.take()
        out.append(
            pltpu.make_async_remote_copy(
                src_ref=source, dst_ref=target, send_sem=send, recv_sem=recv,
                device_id=net.device(dim, v), device_id_type=MESH,
            )
        )
    return out


def begin(copies):
    for copy in copies:
        copy.start()


def arrive(copies):
    for copy in copies:
        copy.wait_recv()


class Piece:
    def __init__(self, net, sems, mine, ref, order, lanes, first, second):
        def block(free, **other):
            fixed = {n: v for n, v in net.place.items() if n not in free}
            return net.view(ref, order, lanes, **{**fixed, **other})

        def pass_on(dim, part):
            return spread(net, sems, dim, part, part)

        self.z = spread(net, sems, "z", mine.at[:, pl.ds(*lanes)], block(()))
        self.one = pass_on(first, block(("z",)))
        self.two = pass_on(second, block(("z", first)))
        self.twins = [
            pass_on("c", block(("z",))),
            sum((pass_on("c", block(("z",), **{first: v})) for v in net.peers(first)), []),
            sum((pass_on("c", block(("z", first), **{second: v})) for v in net.peers(second)), []),
        ]

    def start(self):
        begin(self.z)

    def step_one(self):
        arrive(self.z)
        begin(self.one + self.twins[0])

    def step_two(self):
        arrive(self.one)
        begin(self.two + self.twins[1])

    def step_three(self):
        arrive(self.two)
        begin(self.twins[2])

    def ready(self):
        arrive(sum(self.twins, []))

    def drain(self):
        for copy in self.z + self.one + self.two + sum(self.twins, []):
            copy.wait_send()


def copies_of(net):
    z, y, x, c = (net.size[n] - 1 for n in "zyxc")
    return z + y + x + c * (1 + y + x)


def lane_parts(width, count):
    tiles, out, at = width // LANES, [], 0
    for i in range(count):
        take = (tiles - at) // (count - i)
        out.append((at * LANES, take * LANES))
        at += take
    return out


ORDERS = (("y", "x"), ("x", "y"))


def att_spans(width):
    start = width + LANES
    spans = [(width, LANES + 3 * GROUP)]
    spans += [(start + g * 3 * GROUP, 3 * GROUP) for g in range(1, width // GROUP)]
    return spans + [(0, width)]


def halves(start, size):
    return [(start + at, take) for at, take in lane_parts(size, 2)]


def fused_forward_kernel(
    net,
    clip_ref, tokens_ref, w_reduce_ref, out_grad_ref, w_query_ref, w_key_ref, w_value_ref, w_output_ref, gain_ref,
    w_expand_ref,
    att_all, feed_all, qkv_hbm, mixed_hbm, lse_ref, normed_hbm, grads_ref, result_hbm, grad_middle_hbm, sums_ref,
    gains_ref, half_0, half_1, half_2, half_3, qkv_ref, mixed_ref, normed_ref, result_ref, grad_middle_ref, store_sem, mine_ref, both_ref, gain_tile_ref, group_ref, grad_ref, middle_ref, feed_ref, active_ref, hidden_ref, out_ref,
    chunk_ref, stage_ref, stat_ref, bias_ref, send, recv, local, chunk_sem, stage_sem, *early,
):
    total, width = tokens_ref.shape
    groups = width // GROUP
    hid = w_expand_ref.shape[1]
    chunks = hid // GROUP
    ends = clip_ends(clip_ref)
    flip = BOTH[::-1]
    net.locate()

    moves = [(w_output_ref, mine_ref.at[:, pl.ds(0, width)]), (gain_ref, mine_ref.at[:, pl.ds(width, LANES)])]
    for g in range(groups):
        for j, ref in enumerate((w_query_ref, w_key_ref, w_value_ref)):
            at = width + LANES + (3 * g + j) * GROUP
            moves.append((ref.at[:, pl.ds(g * GROUP, GROUP)], mine_ref.at[:, pl.ds(at, GROUP)]))
    for k in range(chunks):
        moves.append((w_expand_ref.at[:, pl.ds(k * GROUP, GROUP)], both_ref.at[:, pl.ds(2 * k * GROUP, GROUP)]))
    copies = [pltpu.make_async_copy(src, dst, local.at[i]) for i, (src, dst) in enumerate(moves)]
    used = len(copies)
    copies.append(pltpu.make_async_copy(out_grad_ref, grad_ref, local.at[used]))
    for copy in copies:
        copy.start()
    turned = w_reduce_ref[...].T
    for k in range(chunks):
        both_ref[:, (2 * k + 1) * GROUP : (2 * k + 2) * GROUP] = turned[:, k * GROUP : (k + 1) * GROUP]
    for copy in copies[:used]:
        copy.wait()
    net.enter()
    sems = Sems(send, recv)
    att = [
        [Piece(net, sems, mine_ref, att_all, BOTH, lanes, *ORDERS[i]) for i, lanes in enumerate(halves(*span))]
        for span in att_spans(width)
    ]
    feed = [
        [
            Piece(net, sems, both_ref, feed_all, flip, lanes, *ORDERS[i])
            for i, lanes in enumerate(halves(2 * k * GROUP, 2 * GROUP))
        ]
        for k in range(chunks)
    ]
    folds = []
    for k in range(EARLY):
        for kind, (lanes, along) in enumerate(feed_folds(k)):

            def staged(index, kind=kind):
                at = dict(zip([n for n in net.names(flip) if n != "c"], index))
                q = at["x"] * net.size["c"] + net.place["c"]
                return stage_ref[kind, at["z"], at["y"], :, pl.ds(pl.multiple_of(q * GROUP, GROUP), GROUP)]

            bufs, early = early[:2], early[2:]
            folds.append(Fold(net, sems, grads_ref, flip, lanes, along, bufs, own=staged, steps=(0, 1)))
    own = [
        pltpu.make_async_copy(mine_ref, net.view(att_all, BOTH, (0, mine_ref.shape[1]), **net.place), local.at[0]),
        pltpu.make_async_copy(both_ref, net.view(feed_all, flip, (0, both_ref.shape[1]), **net.place), local.at[1]),
    ]
    for copy in own:
        copy.start()

    def act(*moves):
        for name, pair in moves:
            for piece in pair:
                getattr(piece, name)()

    first, *others, last = att
    act(("start", first), ("start", others[0]))
    sums_ref[...] = jnp.zeros_like(sums_ref)
    copies[used].wait()
    for copy in own:
        copy.wait()

    def norm(r0):
        rows = pl.ds(r0, BLOCK)
        x = tokens_ref[rows, :].astype(f32)
        valid = valid_of(r0, BLOCK, ends)
        middle_ref[rows, :] = unit_of(x)[0]
        grad_ref[rows, :] = (grad_ref[rows, :].astype(f32) * valid).astype(bf16)
        set_row(sums_ref, 1, jnp.sum(x * x * valid, axis=0, keepdims=True))

    row_loop(total, BLOCK, norm)
    act(("step_one", first), ("start", others[1]), ("start", last))
    act(("step_one", others[0]), ("step_two", first), ("start", feed[0]))
    act(("step_one", others[1]), ("step_two", others[0]), ("step_three", first), ("ready", first))

    def fetch(lanes, target, sem):
        return pltpu.make_async_copy(net.view(att_all, BOTH, lanes), target, sem)

    def flat(value):
        return value.reshape(width, value.shape[-1])

    tile = fetch((width, LANES), gain_tile_ref, local.at[0])
    tile.start()
    weight = fetch((width + LANES, 3 * GROUP), group_ref.at[0], local.at[1])
    weight.start()
    tile.wait()
    gains_ref[...] = flat(gain_tile_ref[...].astype(f32)).T[:8]

    def scale(r0):
        rows = pl.ds(r0, BLOCK)
        normed_ref[rows, :] = (middle_ref[rows, :] * gains_ref[0:1, :]).astype(bf16)

    row_loop(total, BLOCK, scale)
    plan = {
        (0, 0): [("step_one", last), ("step_two", others[1]), ("step_three", others[0])],
        (0, 2): [("step_two", last), ("step_one", feed[0]), ("start", feed[1]), ("ready", others[0])],
        (0, 3): [("step_three", others[1])],
        (1, 0): [("step_three", last), ("step_two", feed[0]), ("ready", others[1])],
        (1, 2): [("step_one", feed[1]), ("start", feed[2]), ("ready", last)],
        (2, 0): [("step_three", feed[0]), ("step_two", feed[1])],
        (2, 2): [("step_one", feed[2])],
    }
    def group(g, carry):
        slot = lax.rem(g, 2)
        fetch((0, 3 * GROUP), group_ref.at[slot], local.at[1]).wait()
        at = pl.multiple_of(g * 3 * GROUP, LANES)
        qkv_ref[:, pl.ds(at, 3 * GROUP)] = dot_plain(normed_ref[...], flat(group_ref[slot])).astype(bf16)

        def step(i, carry):
            for (a, b), todo in plan.items():
                pl.when((g == a) & (i == b))(lambda todo=todo: act(*todo))
            pair_forward(g, i // 2, i % 2, total, qkv_ref, ends, mixed_ref, stat_ref, bias_ref)
            return carry

        lax.fori_loop(0, 2 * total // WIDE, step, 0)
        start = pl.multiple_of(jnp.where(g + 1 < groups, width + LANES + (g + 1) * 3 * GROUP, 0), LANES)
        fetch((start, 3 * GROUP), group_ref.at[1 - slot], local.at[1]).start()
        return carry

    lax.fori_loop(0, groups, group, 0)
    outs = [
        pltpu.make_async_copy(ref, target, store_sem.at[i])
        for i, (ref, target) in enumerate(((qkv_ref, qkv_hbm), (mixed_ref, mixed_hbm), (normed_ref, normed_hbm)))
    ]
    for copy in outs:
        copy.start()
    lse_ref[...] = stat_ref[...].T[: lse_ref.shape[0]]
    fetch((0, 3 * GROUP), group_ref.at[groups % 2], local.at[1]).wait()
    middle_ref[...] = dot_plain(mixed_ref[...], flat(group_ref[groups % 2]))

    def second(r0):
        rows = pl.ds(r0, BLOCK)
        branch = middle_ref[rows, :]
        middle = tokens_ref[rows, :].astype(f32) + branch
        middle_ref[rows, :] = middle
        feed_ref[rows, :] = (unit_of(middle)[0] * gains_ref[1:2, :]).astype(bf16)
        set_row(sums_ref, 2, jnp.sum(branch * branch * valid_of(r0, BLOCK, ends), axis=0, keepdims=True))

    row_loop(total, BLOCK, second)
    act(("ready", feed[0]), ("step_three", feed[1]), ("step_two", feed[2]))

    tp = net.names(("tp",))
    quarters = list(np.ndindex(*(net.size[n] for n in tp)))
    both_kinds = range(2)

    def place(ref, quarter, kind, k):
        at = (2 * k + kind) * GROUP
        at = at if isinstance(at, int) else pl.multiple_of(at, GROUP)
        return ref.at[quarter + (slice(None),) * (len(ref.shape) - len(quarter) - 1) + (pl.ds(at, GROUP),)]

    def part(ref, q):
        return ref.at[(slice(None),) * (len(ref.shape) - 1) + (pl.ds(q * GROUP, GROUP),)]

    def chunk_copies(k, slot):
        return [
            pltpu.make_async_copy(
                place(feed_all, quarter, kind, k), part(chunk_ref.at[slot, kind], q), chunk_sem.at[slot, kind, q]
            )
            for kind in both_kinds
            for q, quarter in enumerate(quarters)
        ]

    def stage_copies(k):
        return [
            pltpu.make_async_copy(part(stage_ref.at[kind], q), place(grads_ref, quarter, kind, k), stage_sem.at[kind, q])
            for kind in both_kinds
            for q, quarter in enumerate(quarters)
        ]

    for copy in chunk_copies(0, 0):
        copy.start()
    out_ref[...] = jnp.zeros_like(out_ref)
    grad_middle_ref[...] = jnp.zeros_like(grad_middle_ref)

    def chunk(k, carry):
        slot = lax.rem(k, 2)
        for copy in chunk_copies(k, slot):
            copy.wait()

        def weights(kind):
            return chunk_ref[slot, kind].reshape(width, len(quarters) * GROUP)

        for q in range(len(quarters)):
            cols = slice(q * GROUP, (q + 1) * GROUP)
            hidden = dot_plain(feed_ref[...], weights(0)[:, cols])
            grad_active = dot_plain(grad_ref[...], weights(1)[:, cols])
            share = 0.5 * (1.0 + lax.erf(hidden * 0.7071067811865476))
            active_ref[:, cols] = (hidden * share).astype(bf16)
            slope = share + hidden * (jnp.exp(-0.5 * hidden * hidden) * 0.3989422804014327)
            hidden_ref[:, cols] = (grad_active * slope).astype(bf16)
        for j in range(chunks - 1):

            @pl.when(k == j)
            def _(j=j):
                if j + 2 < chunks:
                    act(("ready", feed[j + 1]), ("step_three", feed[j + 2]))
                else:
                    act(("ready", feed[j + 1]))
                for copy in chunk_copies(j + 1, (j + 1) % 2):
                    copy.start()

        @pl.when(k > 0)
        def _():
            for copy in stage_copies(k - 1):
                copy.wait()

        for j in range(EARLY):

            @pl.when(k == j + 1)
            def _(j=j):
                for p in folds[2 * j : 2 * j + 2]:
                    p.send(0)

        out_ref[...] += dot_last(active_ref[...], weights(1))
        grad_middle_ref[...] += dot_last(hidden_ref[...], weights(0))
        for j in range(EARLY):

            @pl.when(k == j + 1)
            def _(j=j):
                for p in folds[2 * j : 2 * j + 2]:
                    p.add(0)
                    p.send(1)

        for kind, (left, right) in enumerate(((feed_ref, hidden_ref), (grad_ref, active_ref))):
            stage_ref[kind] = dot_first(left[...], right[...]).reshape(stage_ref.shape[1:]).astype(bf16)
        for copy in stage_copies(k):
            copy.start()
        return carry

    lax.fori_loop(0, chunks, chunk, 0)

    for i in range(total // BLOCK):
        rows = pl.ds(i * BLOCK, BLOCK)
        middle, out, back = middle_ref[rows, :], out_ref[rows, :], grad_middle_ref[rows, :]
        result_ref[rows, :] = (middle + out).astype(bf16)
        unit, inv = unit_of(middle)
        grad_middle_ref[rows, :] = grad_ref[rows, :].astype(f32) + unit_back(back, unit, inv, gains_ref[1:2, :])
        set_row(sums_ref, 3, jnp.sum(out * out * valid_of(i * BLOCK, BLOCK, ends), axis=0, keepdims=True))
        set_row(sums_ref, 0, jnp.sum(back * unit, axis=0, keepdims=True))
        for j, (ref, target) in enumerate(((result_ref, result_hbm), (grad_middle_ref, grad_middle_hbm))):
            outs.append(pltpu.make_async_copy(ref.at[rows], target.at[rows], store_sem.at[3 + 2 * i + j]))
            outs[-1].start()
    for i, (p, target) in enumerate(zip(folds, (half_0, half_1, half_2, half_3))):
        p.add(1)
        outs.append(pltpu.make_async_copy(p.bufs[1].at[pl.ds(0, 1)], target, local.at[i]))
        outs[-1].start()
    for copy in outs:
        copy.wait()
    for copy in stage_copies(chunks - 1):
        copy.wait()
    for p in folds:
        p.drain()
    for pair in att + feed:
        for piece in pair:
            piece.drain()


def run_fused_forward(net, clip, tokens, out_grad, weights, gain_tile, w_expand, w_reduce):
    total, width = tokens.shape
    rows, rows_feed = width // net.count, w_expand.shape[0]
    lanes, hid = 4 * width + LANES, w_expand.shape[1]
    flip = BOTH[::-1]
    ff = (*net.dims(flip), rows_feed, 2 * hid)
    wide = GROUP * int(np.prod(net.dims(("tp",))))
    inner = tuple(net.size[n] for n in net.names(("dp",))) + (rows_feed, wide)
    count = 2 * (len(att_spans(width)) + hid // GROUP) * copies_of(net) + 4 * EARLY * max(net.size.values())
    dma = pltpu.SemaphoreType.DMA
    early, halves_out = [], []
    for k in range(EARLY):
        for fold in feed_folds(k):
            shapes = Fold.shapes(net, flip, rows_feed, *fold)[:2]
            early += [pltpu.VMEM(dims, bf16) for dims in shapes]
            halves_out.append(shape(1, *shapes[1][1:]))
    return pl.pallas_call(
        lambda *refs: fused_forward_kernel(net, *refs),
        name="layer_forward_feed",
        out_shape=(
            shape(*net.dims(BOTH), rows, lanes), shape(*ff), shape(total, 3 * width), shape(total, width),
            shape(16, total, kind=f32), shape(total, width), shape(*ff), shape(total, width),
            shape(total, width, kind=f32), shape(8, width, kind=f32), shape(8, width, kind=f32), *halves_out,
        ),
        in_specs=[SM, VM, VM] + [ANY] * 7,
        out_specs=(ANY, ANY, ANY, ANY, VM, ANY, ANY, ANY, ANY, VM, VM) + (ANY,) * len(halves_out),
        scratch_shapes=[
            pltpu.VMEM((total, 3 * width), bf16), pltpu.VMEM((total, width), bf16), pltpu.VMEM((total, width), bf16),
            pltpu.VMEM((total, width), bf16), pltpu.VMEM((total, width), f32), dma((3 + 2 * total // BLOCK,)),
            pltpu.VMEM((rows, lanes), bf16), pltpu.VMEM((rows_feed, 2 * hid), bf16), pltpu.VMEM((*net.dims(BOTH), rows, LANES), bf16),
            pltpu.VMEM((2, *net.dims(BOTH), rows, 3 * GROUP), bf16), pltpu.VMEM((total, width), bf16),
            pltpu.VMEM((total, width), f32), pltpu.VMEM((total, width), bf16), pltpu.VMEM((total, wide), bf16),
            pltpu.VMEM((total, wide), bf16), pltpu.VMEM((total, width), f32), pltpu.VMEM((2, 2, *inner), bf16),
            pltpu.VMEM((2, *inner), bf16), pltpu.VMEM((total, LANES), f32),
            pltpu.VMEM((WIDE, static_windows(total)[1]), f32),
            dma((count,)), dma((count,)),
            dma((4 + 3 * (width // GROUP) + hid // GROUP,)), dma((2, 2, wide // GROUP)), dma((2, wide // GROUP)),
            *early,
        ],
        compiler_params=params(collective_id=1, has_side_effects=True),
    )(clip, tokens, w_reduce, out_grad, *weights, gain_tile, w_expand)


def store_at(ref, index, lanes, value):
    ref[tuple(index) + (slice(None), lanes)] = value


def each(dims, body, index=()):
    count = 1
    for size in dims:
        count *= size
    if count <= 4:
        for tail in np.ndindex(*dims):
            body(index + tail)
    else:

        def step(i, carry):
            each(dims[1:], body, index + (i,))
            return carry

        lax.fori_loop(0, dims[0], step, 0)


class Fold:
    def __init__(self, net, sems, ref, order, lanes, along, bufs, out=None, own=None, steps=(0, 1, 2, 3)):
        self.net, self.lanes, self.along, self.bufs, self.out, self.steps = net, lanes, along, bufs, out, steps
        names = net.names(order)
        self.names = [[n for n in names if n not in along[:k]] for k in range(5)]
        self.ref, self.own = ref, own
        self.copies = {}
        for k in steps:
            dim = along[k]
            source, cols = (ref, lanes) if k == 0 else (bufs[k - 1].at[0], (0, lanes[1]))
            self.copies[k] = []
            for o, v in enumerate(net.peers(dim)):
                index = tuple(v if n == dim else slice(None) for n in self.names[k])
                s, r = sems.take()
                self.copies[k].append(
                    pltpu.make_async_remote_copy(
                        src_ref=source.at[index + (slice(None), pl.ds(*cols))], dst_ref=bufs[k].at[o],
                        send_sem=s, recv_sem=r, device_id=net.device(dim, v), device_id_type=MESH,
                    )
                )

    @staticmethod
    def shapes(net, order, rows, lanes, along):
        names, out = net.names(order), []
        for k, dim in enumerate(along):
            left = [net.size[n] for n in names if n not in along[: k + 1]]
            out.append((net.size[dim] - 1, *left, rows, lanes[1]))
        return out

    def send(self, k):
        begin(self.copies[k])

    def add(self, k):
        arrive(self.copies[k])
        dim, buf, cols = self.along[k], self.bufs[k], slice(0, self.lanes[1])
        here = self.net.place[dim]
        wide = pl.ds(*self.lanes)

        def one(index):
            at = dict(zip(self.names[k + 1], index))
            full = tuple(at.get(n, here) for n in self.names[k])
            if k > 0:
                total = self.bufs[k - 1][(0,) + full + (slice(None), cols)].astype(f32)
            elif self.own is not None:
                total = self.own(index).astype(f32)
            else:
                total = self.ref[full + (slice(None), wide)].astype(f32)
            terms = [total] + [buf[(o,) + index].astype(f32) for o in range(self.net.size[dim] - 1)]
            if len(terms) > 2:
                size = len(terms)
                total = 0.0
                for v in range(size):
                    back = lax.rem(here - v + size, size)
                    term = terms[0]
                    for o in range(1, size):
                        term = jnp.where(back == o, terms[o], term)
                    total = total + term
            else:
                total = terms[0] + terms[1]
            if k == 3:
                self.out[:, wide] = total
            else:
                buf[(0,) + index] = total.astype(bf16)

        each([self.net.size[n] for n in self.names[k + 1]], one)

    def drain(self):
        for copies in self.copies.values():
            for copy in copies:
                copy.wait_send()


ALONG = (("c", "x", "y", "z"), ("c", "y", "x", "z"))


def feed_folds(k):
    return [((2 * GROUP * k + GROUP * i, GROUP), ALONG[i]) for i in range(2)]


EARLY = 2


def att_folds(width):
    out = []
    spans = [(0, width + LANES)] + [(width + LANES + g * 3 * GROUP, 3 * GROUP) for g in range(width // GROUP)]
    for start, size in spans:
        for i, (at, take) in enumerate(lane_parts(size, 2)):
            out.append(((start + at, take), ALONG[i % 2]))
    return out


def run_backward(net, clip, grad_middle, mixed, qkv, lse, normed, tokens, weights, gains, *more_args):
    total, width = tokens.shape
    lanes = weights.shape[1]
    scratch = [
        pltpu.VMEM((total, width), bf16), pltpu.VMEM((total, width), bf16), pltpu.VMEM((total, 3 * GROUP), bf16),
        pltpu.VMEM((total, GROUP), f32), pltpu.VMEM((total, LANES), f32), pltpu.VMEM((16, total), f32),
        pltpu.VMEM((WIDE, static_windows(total)[1]), f32),
    ]
    operands = [clip, grad_middle, mixed, qkv, lse, normed, tokens, weights, gains]
    in_specs = [SM, VM, VM, ANY, VM, ANY, ANY, ANY, VM]
    out_shape = (shape(width, lanes), shape(total, width, kind=f32))
    more = {}
    if net is not None:
        feed_grads = more_args[1]
        rows, rows_feed = width // net.count, feed_grads.shape[-2]
        hid = feed_grads.shape[-1] // 2
        flip = BOTH[::-1]
        operands += more_args
        in_specs += [VM, ANY] + [VM] * (4 + 2 * EARLY)
        out_shape = (
            *(shape(rows, width, kind=f32) for _ in range(4)), shape(rows_feed, hid, kind=f32),
            shape(hid, rows_feed, kind=f32), shape(rows, LANES, kind=f32), out_shape[1],
        )
        scratch.append(pltpu.VMEM((*net.dims(BOTH), rows, lanes), bf16))
        kept = tuple(net.size[n] for n in net.names(flip) if n != "c")
        scratch.append(pltpu.VMEM((*kept, rows_feed, 2 * hid - 2 * GROUP * EARLY), bf16))
        scratch += [pltpu.VMEM((rows, lanes), f32), pltpu.VMEM((rows_feed, 2 * hid), f32)]
        bufs = []
        for k in range(hid // GROUP):
            for f in feed_folds(k):
                bufs += Fold.shapes(net, flip, rows_feed, *f)[2 if k < EARLY else 0 :]
        for f in att_folds(width):
            bufs += Fold.shapes(net, BOTH, rows, *f)
        count = sum(dims[0] for dims in bufs)
        scratch += [pltpu.SemaphoreType.DMA((count,)), pltpu.SemaphoreType.DMA((count,)), pltpu.SemaphoreType.DMA]
        scratch += [pltpu.VMEM(dims, bf16) for dims in bufs]
        more = dict(collective_id=2, has_side_effects=True)
    scratch += [
        pltpu.VMEM((total, 3 * width), bf16), pltpu.VMEM((total, width), bf16),
        pltpu.VMEM((2, width, 3 * GROUP), bf16), pltpu.VMEM((total, width), f32),
        pltpu.SemaphoreType.DMA((5,)), pltpu.SemaphoreType.DMA((total // BLOCK,)),
    ]
    return pl.pallas_call(
        lambda *refs: backward_kernel(net, *refs),
        name="layer_backward",
        out_shape=out_shape,
        in_specs=in_specs,
        out_specs=(VM,) * (len(out_shape) - 1) + (ANY,),
        scratch_shapes=scratch,
        compiler_params=params(**more),
        cost_estimate=pl.CostEstimate(flops=22 * 10**9, bytes_accessed=30 << 20, transcendentals=0),
    )(*operands)


def on_device(
    net,
    tokens, clip_lengths, out_grad, w_query, w_key, w_value, w_output, gain_attention, gain_feed, w_expand, w_reduce,
):
    _, total, width = tokens.shape
    rows = tokens.reshape(total, width)
    out_grad = out_grad.reshape(total, width)
    gain_tile = jnp.pad(jnp.stack([gain_attention, gain_feed], axis=1), ((0, 0), (0, LANES - 2)))
    hid = w_expand.shape[1]
    if net is not None:
        weights, _, qkv, mixed, lse, normed, feed_grads, result, grad_middle, sums, gains, *early = run_fused_forward(
            net, clip_lengths, rows, out_grad, (w_query, w_key, w_value, w_output), gain_tile, w_expand, w_reduce
        )
        weights = weights.reshape(width, -1)
        query, key, value, output, expand, reduce, tile, grad_tokens = run_backward(
            net, clip_lengths, grad_middle, mixed, qkv, lse, normed, rows, weights, gains, sums, feed_grads,
            w_query, w_key, w_value, gain_tile, *early,
        )
        gain_one, gain_two, means = tile[:, LANES - 1], tile[:, 0], tile[0, 1:4]
    else:
        mine = [w_output, gain_tile]
        for g in range(width // GROUP):
            mine += [w[:, g * GROUP : (g + 1) * GROUP] for w in (w_query, w_key, w_value)]
        weights = lax.all_gather(jnp.concatenate(mine, axis=1), BOTH, axis=0, tiled=True)
        both = jnp.concatenate([w_expand, w_reduce.T], axis=1)
        feed_weights = lax.all_gather(both, BOTH[::-1], axis=0, tiled=True).reshape(-1, width, 2 * hid)
        gains = jnp.pad(weights[:, width : width + 2].T.astype(f32), ((0, 6), (0, 0)))
        qkv, mixed, lse, middle, feed, normed, sums_one = run_forward(clip_lengths, rows, weights, gains)
        feed_grads, result, grad_middle, sums_two = run_feed(
            clip_lengths, feed, out_grad, middle, gains, feed_weights
        )
        count = jnp.sum(clip_lengths[:, : SLOTS - 1]).astype(f32)
        squares = jnp.stack([jnp.sum(sums_one[0]), jnp.sum(sums_one[1]), jnp.sum(sums_two[0]), count])
        grads, grad_tokens = run_backward(
            None, clip_lengths, grad_middle, mixed, qkv, lse, normed, rows, weights, gains
        )
        shard = lax.psum_scatter(grads, BOTH, scatter_dimension=0, tiled=True).astype(f32)
        shard_feed = lax.psum_scatter(
            feed_grads.reshape(-1, 2 * hid), BOTH[::-1], scatter_dimension=0, tiled=True
        ).astype(f32)
        stats = lax.psum(squares, BOTH)
        gain_two = lax.psum_scatter(sums_two[1], BOTH, scatter_dimension=0, tiled=True)
        means = jnp.sqrt(stats[:3] / (stats[3] * width))
        parts = shard[:, width + LANES :].reshape(-1, width // GROUP, 3, GROUP)
        query, key, value = (parts[:, :, j].reshape(-1, width) for j in range(3))
        pairs = ((w_query, query), (w_key, key), (w_value, value))
        gain_one = sum(jnp.sum(w.astype(f32) * g, axis=1) for w, g in pairs) / gain_attention.astype(f32)
        output, expand, reduce = shard[:, :width], shard_feed[:, :hid], shard_feed[:, hid:].T
    return (
        result.reshape(1, total, width),
        grad_tokens.reshape(1, total, width),
        query,
        key,
        value,
        output,
        gain_one,
        gain_two,
        expand,
        reduce,
        means,
    )


def solution(mesh):
    row, flat = P(BOTH, None), P(BOTH)
    whole = P(BOTH, None, None)
    in_specs = (whole, row, whole, row, row, row, row, flat, flat, P("dp", "tp"), P("tp", "dp"))
    out_specs = (whole, whole, row, row, row, row, flat, flat, P("dp", "tp"), P("tp", "dp"), P())
    factors = FACTORS.get((mesh.shape["dp"], mesh.shape["tp"]))
    net = Net(factors) if factors else None
    return jax.shard_map(
        lambda *args: on_device(net, *args), mesh=mesh, in_specs=in_specs, out_specs=out_specs, check_vma=False
    )
```

```python
import jax
import jax.numpy as jnp
import numpy as np
from jax import lax
from jax.experimental import pallas as pl
from jax.experimental.pallas import tpu as pltpu
from jax.sharding import PartitionSpec as P

HEADS = 12
HEAD_DIM = 64
SLOTS = 4
LANES = 128
BLOCK = 256
WIDE = 512
MAXCLIP = 384
GROUP = 256
TRIO = 3 * LANES
NEG = -1e30
LOG2E = 1.4426950408889634
LN2 = 0.6931471805599453
f32 = jnp.float32
bf16 = jnp.bfloat16
BOTH = ("dp", "tp")
VM = pl.BlockSpec(memory_space=pltpu.VMEM)
SM = pl.BlockSpec(memory_space=pltpu.SMEM)


def dot_plain(left, right):
    return jnp.dot(left, right, preferred_element_type=f32)


def dot_first(left, right):
    return lax.dot_general(left, right, (((0,), (0,)), ((), ())), preferred_element_type=f32)


def dot_last(left, right):
    return lax.dot_general(left, right, (((1,), (1,)), ((), ())), preferred_element_type=f32)


def unit_of(rows):
    centred = rows - jnp.mean(rows, axis=-1, keepdims=True)
    inv = lax.rsqrt(jnp.mean(centred * centred, axis=-1, keepdims=True) + 1e-06)
    return centred * inv, inv


def unit_back(grad, unit, inv, gain):
    scaled = grad * gain
    inner = (
        scaled
        - jnp.mean(scaled, axis=-1, keepdims=True)
        - unit * jnp.mean(scaled * unit, axis=-1, keepdims=True)
    )
    return inv * inner


def clip_ends(clip_ref):
    ends, total = [], jnp.int32(0)
    for j in range(SLOTS - 1):
        total = total + clip_ref[0, j]
        ends.append(total)
    return ends


def segment_of(position, ends):
    return sum((position >= e).astype(jnp.int32) for e in ends)


def valid_of(start, count, ends):
    position = start + lax.broadcasted_iota(jnp.int32, (count, 1), 0)
    return (position < ends[-1]).astype(f32)


def row_loop(total, size, body):
    def step(i, carry):
        body(pl.multiple_of(i * size, size))
        return carry

    lax.fori_loop(0, total // size, step, 0)


def head_masks(scale):
    lane = lax.broadcasted_iota(jnp.int32, (1, LANES), 1)
    low = lane < HEAD_DIM
    return lane, low, (jnp.where(low, scale, 0.0).astype(bf16), jnp.where(low, 0.0, scale).astype(bf16))


def lane_index():
    lane = lax.broadcasted_iota(jnp.int32, (1, LANES), 1)
    return lane, lax.rem(lane, HEAD_DIM)


def split_three(value):
    high = value.astype(bf16)
    rest = value - high.astype(f32)
    middle = rest.astype(bf16)
    return high, middle, (rest - middle.astype(f32)).astype(bf16)


def in_lanes(at, first, terms, other):
    out = other
    for i, term in enumerate(terms):
        out = jnp.where(at == first + i, term.astype(f32), out)
    return out


def set_codes(query_ref, key_ref, ends):
    _, at = lane_index()

    def block(r0):
        rows = pl.ds(r0, BLOCK)
        seg = segment_of(r0 + lax.broadcasted_iota(jnp.int32, (BLOCK, 1), 0), ends)
        own = at == seg
        if query_ref is not None:
            query_ref[rows, :] = jnp.where(own, NEG, 0.0).astype(bf16)
        key_ref[rows, :] = jnp.where((at < SLOTS + 3) & jnp.logical_not(own), 1.0, 0.0).astype(bf16)

    row_loop(key_ref.shape[0], BLOCK, block)


def inner_codes(grad_ref, mixed_ref, out_ref):
    total, width = mixed_ref.shape
    _, at = lane_index()
    _, low, _ = head_masks(1.0)

    def block(r0):
        rows = pl.ds(r0, LANES)
        for p in range(width // LANES):
            cols = slice(p * LANES, (p + 1) * LANES)
            both = grad_ref[rows, cols].astype(f32) * mixed_ref[rows, cols].astype(f32)
            sums = (
                jnp.sum(jnp.where(low, both, 0.0), axis=1, keepdims=True),
                jnp.sum(jnp.where(low, 0.0, both), axis=1, keepdims=True),
            )
            first, second = (in_lanes(at, 0, split_three(-x), 0.0) for x in sums)
            out_ref[rows, cols] = jnp.where(low, second, first).astype(bf16)

    row_loop(total, LANES, block)


def set_row(ref, row, value):
    at = lax.broadcasted_iota(jnp.int32, ref.shape, 0) == row
    ref[...] += jnp.where(at, value, 0.0)


def forward_kernel(
    clip_ref, tokens_ref, weights_ref, gains_ref,
    qkv_ref, mixed_ref, extra_ref, middle_ref, feed_ref, normed_ref, sums_ref,
    code_q_ref, code_k_ref,
):
    total, width = tokens_ref.shape
    ends = clip_ends(clip_ref)
    sums_ref[...] = jnp.zeros_like(sums_ref)

    def norm(r0):
        rows = pl.ds(r0, BLOCK)
        x = tokens_ref[rows, :].astype(f32)
        normed_ref[rows, :] = (unit_of(x)[0] * gains_ref[0:1, :]).astype(bf16)
        set_row(sums_ref, 0, jnp.sum(x * x * valid_of(r0, BLOCK, ends), axis=0, keepdims=True))

    row_loop(total, BLOCK, norm)
    set_codes(code_q_ref, code_k_ref, ends)
    for p in range(width // LANES):
        weight = weights_ref[:, width + LANES + p * TRIO : width + LANES + (p + 1) * TRIO]
        project(normed_ref, pl.ds(0, total), weight, qkv_ref, p)

    def pair_block(i, carry):
        blocks = total // WIDE
        pair_forward(
            lax.div(i, blocks), lax.rem(i, blocks), total, qkv_ref, mixed_ref, extra_ref, code_q_ref, code_k_ref
        )
        return carry

    lax.fori_loop(0, width // LANES * (total // WIDE), pair_block, 0)
    middle_ref[...] = dot_plain(mixed_ref[...], weights_ref[:, :width])

    def second(r0):
        rows = pl.ds(r0, BLOCK)
        branch = middle_ref[rows, :]
        middle = tokens_ref[rows, :].astype(f32) + branch
        middle_ref[rows, :] = middle
        feed_ref[rows, :] = (unit_of(middle)[0] * gains_ref[1:2, :]).astype(bf16)
        set_row(sums_ref, 1, jnp.sum(branch * branch * valid_of(r0, BLOCK, ends), axis=0, keepdims=True))

    row_loop(total, BLOCK, second)


def feed_kernel(
    clip_ref, feed_ref, out_grad_ref, middle_ref, gains_ref, weights_ref,
    grads_ref, result_ref, grad_middle_ref, sums_ref,
    grad_ref, active_ref, hidden_ref, out_ref, back_ref,
):
    total, width = feed_ref.shape
    ends = clip_ends(clip_ref)
    step = pl.program_id(0)

    @pl.when(step == 0)
    def _():
        def mask(r0):
            rows = pl.ds(r0, BLOCK)
            grad_ref[rows, :] = (out_grad_ref[rows, :].astype(f32) * valid_of(r0, BLOCK, ends)).astype(bf16)

        row_loop(total, BLOCK, mask)
        out_ref[...] = jnp.zeros_like(out_ref)
        back_ref[...] = jnp.zeros_like(back_ref)
        sums_ref[...] = jnp.zeros_like(sums_ref)

    hid = weights_ref.shape[2] - width
    part = 256
    for n in range(hid // part):
        cols = slice(n * part, (n + 1) * part)
        late = slice(hid + n * part, hid + (n + 1) * part)
        hidden = dot_plain(feed_ref[...], weights_ref[0, :, cols])
        grad_active = dot_plain(grad_ref[...], weights_ref[0, :, late])
        share = 0.5 * (1.0 + lax.erf(hidden * 0.7071067811865476))
        active_ref[:, cols] = (hidden * share).astype(bf16)
        slope = share + hidden * (jnp.exp(-0.5 * hidden * hidden) * 0.3989422804014327)
        hidden_ref[:, cols] = (grad_active * slope).astype(bf16)
    expand, reduce = weights_ref[0, :, :hid], weights_ref[0, :, hid:]
    out_ref[...] += dot_last(active_ref[...], reduce)
    back_ref[...] += dot_last(hidden_ref[...], expand)
    grads_ref[0, :, :hid] = dot_first(feed_ref[...], hidden_ref[...]).astype(bf16)
    grads_ref[0, :, hid:] = dot_first(grad_ref[...], active_ref[...]).astype(bf16)

    @pl.when(step == pl.num_programs(0) - 1)
    def _():
        def finish(r0):
            rows = pl.ds(r0, BLOCK)
            valid = valid_of(r0, BLOCK, ends)
            middle, out, back = middle_ref[rows, :], out_ref[rows, :], back_ref[rows, :]
            result_ref[rows, :] = (middle + out).astype(bf16)
            unit, inv = unit_of(middle)
            grad_middle_ref[rows, :] = (
                grad_ref[rows, :].astype(f32) + unit_back(back, unit, inv, gains_ref[1:2, :])
            )
            set_row(sums_ref, 0, jnp.sum(out * out * valid, axis=0, keepdims=True))
            set_row(sums_ref, 1, jnp.sum(back * unit, axis=0, keepdims=True))

        row_loop(total, BLOCK, finish)


def static_windows(total):
    spans = []
    for r0 in range(0, total, WIDE):
        low = max(0, r0 - MAXCLIP + 1) // LANES * LANES
        high = min(total, -(-(r0 + WIDE + MAXCLIP - 1) // LANES) * LANES)
        spans.append((low, high))
    width = max(high - low for low, high in spans)
    return [min(low, total - width) for low, _ in spans], width


def start_of(starts, block):
    at = jnp.int32(starts[0])
    for i, s in enumerate(starts):
        at = jnp.where(block == i, s, at)
    return pl.multiple_of(at, LANES)


def pair_parts(p, block, total):
    starts, cols = static_windows(total)
    rows = pl.ds(pl.multiple_of(block * WIDE, WIDE), WIDE)
    win = pl.ds(start_of(starts, block), cols)
    return rows, win, [pl.ds(pl.multiple_of(p * TRIO + j * LANES, LANES), LANES) for j in range(3)]


def with_codes(value, code, plain):
    return value * plain[0] + code * plain[1], value * plain[1] + code * plain[0]


def pair_forward(p, block, total, qkv_ref, mixed_ref, extra_ref, code_q_ref, code_k_ref):
    _, at = lane_index()
    _, low, plain = head_masks(1.0)
    rows, win, (at_q, at_k, at_v) = pair_parts(p, block, total)
    query, keys, values = qkv_ref[rows, at_q], qkv_ref[win, at_k], qkv_ref[win, at_v]
    values = jnp.concatenate([values, jnp.ones_like(values)], axis=1)
    code = code_q_ref[rows, :]
    queries, keys = with_codes(query, code, plain), with_codes(keys, code_k_ref[win, :], plain)
    outs, extras = [], []
    for h in range(2):
        scores = dot_last(queries[h], keys[h])
        top = jnp.max(scores, axis=1, keepdims=True)
        mixed = dot_plain(jnp.exp2(scores - top).astype(bf16), values)
        row_sum = mixed[:, LANES:]
        outs.append(mixed[:, :LANES] / row_sum)
        extras.append(in_lanes(at, SLOTS, split_three(-(top + LOG2E * jnp.log(row_sum))), code.astype(f32)))
    lanes = pl.ds(pl.multiple_of(p * LANES, LANES), LANES)
    mixed_ref[rows, lanes] = jnp.where(low, outs[0], outs[1]).astype(bf16)
    extra_ref[rows, lanes] = jnp.where(low, extras[1], extras[0]).astype(bf16)


def pair_back(p, block, total, qkv_ref, grad_ref, extra_ref, inner_ref, code_k_ref, dqkv_ref, dq_ref):
    _, at = lane_index()
    _, low, scaled = head_masks(0.125)
    _, _, plain = head_masks(1.0)
    rows, win, (at_q, at_k, at_v) = pair_parts(p, block, total)
    lanes = pl.ds(pl.multiple_of(p * LANES, LANES), LANES)
    keys, values, query, grad = qkv_ref[rows, at_k], qkv_ref[rows, at_v], qkv_ref[win, at_q], grad_ref[win, lanes]
    ones = jnp.where(at < 3, 1.0, 0.0).astype(bf16)
    key_codes, query_codes = with_codes(keys, code_k_ref[rows, :], plain), with_codes(query, extra_ref[win, lanes], plain)
    value_codes, grad_codes = with_codes(values, ones, plain), with_codes(grad, inner_ref[win, lanes], plain)
    dk, dv, dq = [], [], 0.0
    for h in range(2):
        probs = jnp.exp2(dot_last(key_codes[h], query_codes[h]))
        dv.append(dot_plain(probs.astype(bf16), grad))
        ds = (probs * dot_last(value_codes[h], grad_codes[h])).astype(bf16)
        dk.append(dot_plain(ds, query))
        dq = dq + dot_first(ds, keys * scaled[h])
    dq_ref[win, :] += dq
    dqkv_ref[rows, at_k] = (jnp.where(low, dk[0], dk[1]) * LN2).astype(bf16)
    dqkv_ref[rows, at_v] = jnp.where(low, dv[0], dv[1]).astype(bf16)


def project(normed_ref, rows, weight, qkv_ref, p):
    lane = lax.broadcasted_iota(jnp.int32, (1, TRIO), 1)
    scale = jnp.where(lane < LANES, 0.125 * LOG2E, 1.0)
    at = pl.multiple_of(p * TRIO, LANES)
    qkv_ref[rows, pl.ds(at, TRIO)] = (dot_plain(normed_ref[rows, :], weight) * scale).astype(bf16)


def backward_kernel(
    net,
    clip_ref, grad_middle_ref, mixed_ref, qkv_hbm, extra_hbm, normed_hbm, tokens_hbm, weights_hbm, gains_ref,
    *refs,
):
    total, width = mixed_ref.shape
    ends = clip_ends(clip_ref)
    refs, load_sem, store_sem = refs[:-2], *refs[-2:]
    refs, (qkv_ref, extra_ref, normed_ref, output_weight_ref, weight_ref, sum_ref) = refs[:-6], refs[-6:]
    pairs = width // LANES
    loads = [
        pltpu.make_async_copy(source, target, load_sem.at[i])
        for i, (source, target) in enumerate(
            (
                (weights_hbm.at[:, pl.ds(0, width)], output_weight_ref),
                (qkv_hbm, qkv_ref),
                (extra_hbm, extra_ref),
                (normed_hbm, normed_ref),
                (weights_hbm.at[:, pl.ds(width + LANES, pairs * TRIO)], weight_ref),
            )
        )
    ]
    begin(loads)
    if net is None:
        grads_ref, grad_tokens_ref, low_ref, grad_ref, dqkv_ref, dq_ref, inner_ref, code_k_ref = refs
        plan = {}
    else:
        sums_ref, feed_grads_ref, *refs = refs
        early, refs = refs[: 2 * EARLY], refs[2 * EARLY :]
        shard_ref, shard_feed_ref, grad_tokens_ref, low_ref, grad_ref, dqkv_ref, dq_ref, inner_ref, *refs = refs
        code_k_ref, grads_ref, own_ref, send, recv, local, *bufs = refs
        net.locate()
        net.announce()
        net.meet()
        sems = Sems(send, recv)
        feed, att = [], []
        flip = BOTH[::-1]
        for k in range(EARLY):
            for lanes, along in feed_folds(k):
                slots, bufs = [None, early[len(feed)], *bufs[:2]], bufs[2:]
                feed.append(Fold(net, sems, None, flip, lanes, along, slots, shard_feed_ref, steps=(2, 3)))
        span = 2 * GROUP * EARLY
        for k in range(EARLY, feed_grads_ref.shape[-1] // (2 * GROUP)):
            for lanes, along in feed_folds(k):

                def kept(index, start=lanes[0] - span):
                    return own_ref[index + (slice(None), pl.ds(start, GROUP))]

                feed.append(
                    Fold(net, sems, feed_grads_ref, flip, lanes, along, bufs[:4], shard_feed_ref, own=kept)
                )
                bufs = bufs[4:]
        for lanes, along in att_folds(width):
            att.append(Fold(net, sems, grads_ref, BOTH, lanes, along, bufs[:4], shard_ref))
            bufs = bufs[4:]
        early, late = feed[: 2 * EARLY], feed[2 * EARLY :]
        for p in late:
            p.send(0)
        for p in early:
            p.send(2)
        mine = tuple(net.place["c"] if n == "c" else slice(None) for n in net.names(flip))
        own = pltpu.make_async_copy(
            feed_grads_ref.at[mine + (slice(None), pl.ds(span, feed_grads_ref.shape[-1] - span))], own_ref, local
        )
        own.start()
        tall = jnp.concatenate([sums_ref[...], jnp.zeros((LANES - 8, width), f32)], axis=0).T
        lane = lax.broadcasted_iota(jnp.int32, (1, LANES), 1)
        for j in range(1, 4):
            tall = jnp.where(lane == j, jnp.sum(sums_ref[j : j + 1, :], axis=1, keepdims=True), tall)
        extras = jnp.where(lane == 4, ends[-1].astype(f32), tall)

    def advance(*todo):
        for pieces, step in todo:
            for piece in pieces:
                piece.add(step)
                if step < 3:
                    piece.send(step + 1)

    def store(lanes, value):
        if net is None:
            grads_ref[:, lanes] = value.astype(bf16)
        else:
            rows = grads_ref.shape[-2]
            for i, index in enumerate(np.ndindex(*net.dims(BOTH))):
                grads_ref[index + (slice(None), lanes)] = value[i * rows : (i + 1) * rows].astype(bf16)

    if net is not None:
        store(slice(width, width + LANES), extras)
    low_ref[...] = grad_middle_ref[...].astype(bf16)
    store(slice(0, width), dot_first(mixed_ref[...], low_ref[...]))
    if net is not None:
        for p in att[:2]:
            p.send(0)
    loads[0].wait()
    grad_ref[...] = dot_last(low_ref[...], output_weight_ref[...]).astype(bf16)
    tokens_ref = low_ref
    tokens = pltpu.make_async_copy(tokens_hbm, tokens_ref, load_sem.at[5])
    tokens.start()
    set_codes(None, code_k_ref, ends)
    inner_codes(grad_ref, mixed_ref, inner_ref)
    moves, ending = {}, {}
    if net is not None:
        own.wait()
        output, pair = att[:2], [att[2 + 2 * p : 4 + 2 * p] for p in range(pairs)]
        moves = {
            0: [(late, 0)],
            1: [(output, 0)],
            2: [(early, 2)],
            3: [(pair[0], 0)],
            4: [(late, 1), (output, 1)],
            5: [(pair[1], 0), (pair[0], 1)],
            6: [(output, 2)],
            7: [(pair[2], 0), (pair[1], 1), (late, 2), (pair[0], 2)],
            8: [(early, 3)],
            9: [(pair[3], 0), (pair[2], 1), (pair[1], 2)],
            10: [(output, 3), (pair[0], 3)],
            11: [(pair[4], 0), (pair[3], 1), (pair[2], 2), (late, 3)],
        }
        ending = {
            0: [(pair[4], 1), (pair[3], 2), (pair[1], 3)],
            1: [(pair[5], 0)],
            2: [(pair[2], 3)],
            4: [(pair[4], 2)],
            6: [(pair[5], 1), (pair[3], 3)],
        }
    for copy in loads[1:]:
        copy.wait()
    blocks = total // WIDE

    def per_pair(p, carry):
        dq_ref[...] = jnp.zeros_like(dq_ref)

        def step(b, carry):
            for i, todo in moves.items():
                pl.when(p * blocks + b == i)(lambda todo=todo: advance(*todo))
            pair_back(p, b, total, qkv_ref, grad_ref, extra_ref, inner_ref, code_k_ref, dqkv_ref, dq_ref)
            return carry

        lax.fori_loop(0, blocks, step, 0)
        at = pl.multiple_of(p * TRIO, LANES)
        dqkv_ref[:, pl.ds(at, LANES)] = dq_ref[...].astype(bf16)
        lanes = pl.ds(pl.multiple_of(width + LANES + at, LANES), TRIO)
        store(lanes, dot_first(normed_ref[...], dqkv_ref[:, pl.ds(at, TRIO)]))
        if net is not None:
            for k in range(pairs):

                @pl.when(p == k)
                def _(k=k):
                    for piece in pair[k]:
                        piece.send(0)

        return carry

    lax.fori_loop(0, pairs, per_pair, 0)
    third = pairs * TRIO // 3
    for j in range(3):
        cols = slice(j * third, (j + 1) * third)
        back = dot_last(dqkv_ref[:, cols], weight_ref[:, cols])
        if j == 0:
            sum_ref[...] = back
        else:
            sum_ref[...] += back
        advance(*ending.get(j, ()))
    tokens.wait()
    finals = []
    for b in range(total // BLOCK):
        rows = pl.ds(b * BLOCK, BLOCK)
        unit, inv = unit_of(tokens_ref[rows, :].astype(f32))
        sum_ref[rows, :] = grad_middle_ref[rows, :] + unit_back(sum_ref[rows, :], unit, inv, gains_ref[0:1, :])
        finals.append(pltpu.make_async_copy(sum_ref.at[rows], grad_tokens_ref.at[rows], store_sem.at[b]))
        finals[-1].start()
        advance(*ending.get(3 + b, ()))
    if net is not None:
        advance((pair[5], 2), (pair[4], 3))
        advance((pair[5], 3))
        for p in feed + att:
            p.drain()
    for copy in finals:
        copy.wait()


def params(**more):
    return pltpu.CompilerParams(vmem_limit_bytes=58 << 20, **more)


def shape(*dims, kind=bf16):
    return jax.ShapeDtypeStruct(dims, kind)


def run_forward(clip, tokens, weights, gains):
    total, width = tokens.shape
    return pl.pallas_call(
        forward_kernel,
        name="layer_forward",
        out_shape=(
            shape(total, 3 * width), shape(total, width), shape(total, width),
            shape(total, width, kind=f32), shape(total, width), shape(total, width), shape(8, width, kind=f32),
        ),
        in_specs=[SM, VM, VM, VM],
        out_specs=(VM,) * 7,
        scratch_shapes=[pltpu.VMEM((total, LANES), bf16), pltpu.VMEM((total, LANES), bf16)],
        compiler_params=params(),
        cost_estimate=pl.CostEstimate(flops=12 * 10**9, bytes_accessed=20 << 20, transcendentals=0),
    )(clip, tokens, weights, gains)


def run_feed(clip, feed, out_grad, middle, gains, weights):
    total, width = feed.shape
    parts, _, both = weights.shape
    one = pl.BlockSpec((1, width, both), lambda t: (t, 0, 0))
    return pl.pallas_call(
        feed_kernel,
        name="feed_both",
        grid=(parts,),
        out_shape=(
            shape(parts, width, both), shape(total, width), shape(total, width, kind=f32), shape(8, width, kind=f32),
        ),
        in_specs=[SM, VM, VM, VM, VM, one],
        out_specs=(one, VM, VM, VM),
        scratch_shapes=[
            pltpu.VMEM((total, width), bf16), pltpu.VMEM((total, both - width), bf16),
            pltpu.VMEM((total, both - width), bf16), pltpu.VMEM((total, width), f32), pltpu.VMEM((total, width), f32),
        ],
        compiler_params=params(),
        cost_estimate=pl.CostEstimate(flops=30 * 10**9, bytes_accessed=30 << 20, transcendentals=0),
    )(clip, feed, out_grad, middle, gains, weights)


MESH = pl.DeviceIdType.MESH
ANY = pl.BlockSpec(memory_space=pl.ANY)
FACTORS = {
    (8, 4): ((("z", 4), ("y", 2)), (("x", 2), ("c", 2))),
}


class Net:
    def __init__(self, factors):
        self.factors = factors
        self.size = {n: s for axis in factors for n, s in axis}
        self.count = 1
        for s in self.size.values():
            self.count *= s

    def locate(self):
        self.place = {}
        for name, axis in zip(BOTH, self.factors):
            left = lax.axis_index(name)
            for n, s in axis[::-1]:
                self.place[n] = lax.rem(left, s)
                left = lax.div(left, s)

    def device(self, dim, value):
        out = []
        for axis in self.factors:
            index = 0
            for n, s in axis:
                index = index * s + (value if n == dim else self.place[n])
            out.append(index)
        return tuple(out)

    def names(self, order):
        axes = dict(zip(BOTH, self.factors))
        return [n for a in order for n, _ in axes[a]]

    def dims(self, order):
        return tuple(self.size[n] for n in self.names(order))

    def view(self, ref, order, lanes, **fixed):
        index = tuple(fixed.get(n, slice(None)) for n in self.names(order))
        return ref.at[index + (slice(None), pl.ds(*lanes))]

    def peers(self, dim):
        s = self.size[dim]
        return [lax.rem(self.place[dim] + o, s) for o in range(1, s)]

    def announce(self):
        barrier = pltpu.get_barrier_semaphore()
        for dim in self.size:
            for v in self.peers(dim):
                pl.semaphore_signal(barrier, inc=1, device_id=self.device(dim, v), device_id_type=MESH)

    def meet(self):
        pl.semaphore_wait(pltpu.get_barrier_semaphore(), sum(s - 1 for s in self.size.values()))


class Sems:
    def __init__(self, send, recv):
        self.send, self.recv, self.used = send, recv, 0

    def take(self):
        self.used += 1
        return self.send.at[self.used - 1], self.recv.at[self.used - 1]


def spread(net, sems, dim, source, target):
    out = []
    for v in net.peers(dim):
        send, recv = sems.take()
        out.append(
            pltpu.make_async_remote_copy(
                src_ref=source, dst_ref=target, send_sem=send, recv_sem=recv,
                device_id=net.device(dim, v), device_id_type=MESH,
            )
        )
    return out


def begin(copies):
    for copy in copies:
        copy.start()


def arrive(copies):
    for copy in copies:
        copy.wait_recv()


class Piece:
    def __init__(self, net, sems, mine, ref, order, lanes, first, second):
        def block(free, **other):
            fixed = {n: v for n, v in net.place.items() if n not in free}
            return net.view(ref, order, lanes, **{**fixed, **other})

        def pass_on(dim, part):
            return spread(net, sems, dim, part, part)

        self.left = False
        self.z = spread(net, sems, "z", mine.at[:, pl.ds(*lanes)], block(()))
        self.one = pass_on(first, block(("z",)))
        self.two = pass_on(second, block(("z", first)))
        self.twins = [
            pass_on("c", block(("z",))),
            sum((pass_on("c", block(("z",), **{first: v})) for v in net.peers(first)), []),
            sum((pass_on("c", block(("z", first), **{second: v})) for v in net.peers(second)), []),
        ]

    def start(self):
        begin(self.z)

    def leave(self):
        for copy in self.z:
            copy.wait_send()
        self.left = True

    def step_one(self):
        arrive(self.z)
        begin(self.one + self.twins[0])

    def step_two(self):
        arrive(self.one)
        begin(self.two + self.twins[1])

    def step_three(self):
        arrive(self.two)
        begin(self.twins[2])

    def ready(self):
        arrive(sum(self.twins, []))

    def drain(self):
        for copy in ([] if self.left else self.z) + self.one + self.two + sum(self.twins, []):
            copy.wait_send()


def copies_of(net):
    z, y, x, c = (net.size[n] - 1 for n in "zyxc")
    return z + y + x + c * (1 + y + x)


def lane_parts(width, count):
    tiles, out, at = width // LANES, [], 0
    for i in range(count):
        take = (tiles - at) // (count - i)
        out.append((at * LANES, take * LANES))
        at += take
    return out


ORDERS = (("y", "x"), ("x", "y"))


def att_spans(width):
    start = width + LANES
    spans = [(width, LANES + TRIO)] + [(start + p * TRIO, TRIO) for p in range(1, width // LANES)]
    return spans + [(0, width)]


def halves(start, size):
    return [(start + at, take) for at, take in lane_parts(size, 2)]


def fused_forward_kernel(
    net,
    clip_ref, tokens_ref, w_reduce_ref, out_grad_ref, w_query_ref, w_key_ref, w_value_ref, w_output_ref, gain_ref,
    w_expand_ref,
    att_all, feed_all, qkv_hbm, mixed_hbm, extra_hbm, normed_hbm, grads_ref, result_hbm, grad_middle_hbm, sums_ref,
    gains_ref, half_0, half_1, half_2, half_3, qkv_ref, mixed_ref, extra_ref, normed_ref, result_ref, grad_middle_ref, store_sem, mine_ref, both_ref, gain_tile_ref, group_ref, output_weight_ref, grad_ref, middle_ref, feed_ref, active_ref, hidden_ref, out_ref,
    chunk_ref, stage_ref, code_q_ref, code_k_ref, send, recv, local, chunk_sem, stage_sem, *early,
):
    total, width = tokens_ref.shape
    pairs = width // LANES
    hid = w_expand_ref.shape[1]
    chunks = hid // GROUP
    ends = clip_ends(clip_ref)
    flip = BOTH[::-1]
    net.locate()
    net.announce()

    moves = [(w_output_ref, mine_ref.at[:, pl.ds(0, width)]), (gain_ref, mine_ref.at[:, pl.ds(width, LANES)])]
    for p in range(pairs):
        for j, ref in enumerate((w_query_ref, w_key_ref, w_value_ref)):
            at = width + LANES + p * TRIO + j * LANES
            moves.append((ref.at[:, pl.ds(p * LANES, LANES)], mine_ref.at[:, pl.ds(at, LANES)]))
    for k in range(chunks):
        for kind, ref in enumerate((w_expand_ref, w_reduce_ref)):
            moves.append((ref.at[:, pl.ds(k * GROUP, GROUP)], both_ref.at[:, pl.ds((2 * k + kind) * GROUP, GROUP)]))
    copies = [pltpu.make_async_copy(src, dst, local.at[i]) for i, (src, dst) in enumerate(moves)]
    used = len(copies)
    copies.append(pltpu.make_async_copy(out_grad_ref, grad_ref, local.at[used]))
    for copy in copies:
        copy.start()
    for copy in copies[:used]:
        copy.wait()
    net.meet()
    sems = Sems(send, recv)
    att = [
        [Piece(net, sems, mine_ref, att_all, BOTH, lanes, *ORDERS[i]) for i, lanes in enumerate(halves(*span))]
        for span in att_spans(width)
    ]
    feed = [
        [
            Piece(net, sems, both_ref, feed_all, flip, lanes, *ORDERS[i])
            for i, lanes in enumerate(halves(2 * k * GROUP, 2 * GROUP))
        ]
        for k in range(chunks)
    ]
    folds = []
    for k in range(EARLY):
        for kind, (lanes, along) in enumerate(feed_folds(k)):

            def staged(index, kind=kind):
                at = dict(zip([n for n in net.names(flip) if n != "c"], index))
                q = at["x"] * net.size["c"] + net.place["c"]
                return stage_ref[kind, at["z"], at["y"], :, pl.ds(pl.multiple_of(q * GROUP, GROUP), GROUP)]

            bufs, early = early[:2], early[2:]
            folds.append(Fold(net, sems, grads_ref, flip, lanes, along, bufs, own=staged, steps=(0, 1)))
    own = [
        pltpu.make_async_copy(mine_ref, net.view(att_all, BOTH, (0, mine_ref.shape[1]), **net.place), local.at[0]),
        pltpu.make_async_copy(both_ref, net.view(feed_all, flip, (0, both_ref.shape[1]), **net.place), local.at[1]),
    ]
    for copy in own:
        copy.start()

    def act(*moves):
        for name, pair in moves:
            for piece in pair:
                getattr(piece, name)()

    pair, output = att[:-1], att[-1]
    act(("start", pair[0]))
    sums_ref[...] = jnp.zeros_like(sums_ref)
    copies[used].wait()
    for copy in own:
        copy.wait()

    def norm(r0):
        rows = pl.ds(r0, BLOCK)
        x = tokens_ref[rows, :].astype(f32)
        valid = valid_of(r0, BLOCK, ends)
        middle_ref[rows, :] = unit_of(x)[0]
        grad_ref[rows, :] = (grad_ref[rows, :].astype(f32) * valid).astype(bf16)
        set_row(sums_ref, 1, jnp.sum(x * x * valid, axis=0, keepdims=True))

    row_loop(total, BLOCK, norm)
    set_codes(code_q_ref, code_k_ref, ends)
    for p in range(pairs):
        act(("leave", pair[p]), ("start", pair[p + 1] if p + 1 < pairs else feed[0]), ("step_one", pair[p]))
        if p >= 2:
            act(("step_two", pair[p - 2]))
        if p >= 4:
            act(("step_three", pair[p - 4]))
    act(("ready", pair[0]))

    def fetch(lanes, target, sem):
        return pltpu.make_async_copy(net.view(att_all, BOTH, lanes), target, sem)

    def flat(value):
        return value.reshape(width, value.shape[-1])

    tile = fetch((width, LANES), gain_tile_ref, local.at[0])
    tile.start()
    fetch((width + LANES, TRIO), group_ref.at[0], local.at[1]).start()
    tile.wait()
    gains_ref[...] = flat(gain_tile_ref[...].astype(f32)).T[:8]

    def scale(r0):
        rows = pl.ds(r0, BLOCK)
        normed_ref[rows, :] = (middle_ref[rows, :] * gains_ref[0:1, :]).astype(bf16)

    row_loop(total, BLOCK, scale)
    plan = {
        0: [("step_two", pair[4]), ("step_three", pair[2]), ("ready", pair[1])],
        1: [("step_two", pair[5]), ("step_three", pair[3]), ("start", output)],
        2: [("start", feed[1]), ("step_three", pair[4]), ("ready", pair[2])],
        3: [("step_one", feed[0]), ("step_three", pair[5])],
        4: [("step_one", output), ("ready", pair[3])],
        6: [("step_two", output), ("step_two", feed[0]), ("start", feed[2]), ("ready", pair[4])],
        8: [("step_one", feed[1]), ("ready", pair[5])],
        9: [("step_three", output)],
        11: [("step_three", feed[0])],
    }
    blocks = total // WIDE

    def per_pair(p, carry):
        slot = lax.rem(p, 2)
        fetch((0, TRIO), group_ref.at[slot], local.at[1]).wait()
        project(normed_ref, pl.ds(0, total), flat(group_ref[slot]), qkv_ref, p)

        def step(b, carry):
            for i, todo in plan.items():
                pl.when(p * blocks + b == i)(lambda todo=todo: act(*todo))

            @pl.when((b == 1) & (p + 1 < pairs))
            def _():
                start = pl.multiple_of(width + LANES + (p + 1) * TRIO, LANES)
                fetch((start, TRIO), group_ref.at[1 - slot], local.at[1]).start()

            pair_forward(p, b, total, qkv_ref, mixed_ref, extra_ref, code_q_ref, code_k_ref)
            return carry

        lax.fori_loop(0, blocks, step, 0)
        return carry

    lax.fori_loop(0, pairs, per_pair, 0)
    act(("ready", output))
    fetch((0, width), output_weight_ref, local.at[1]).start()
    outs = [
        pltpu.make_async_copy(ref, target, store_sem.at[i])
        for i, (ref, target) in enumerate(
            ((qkv_ref, qkv_hbm), (mixed_ref, mixed_hbm), (normed_ref, normed_hbm), (extra_ref, extra_hbm))
        )
    ]
    for copy in outs:
        copy.start()
    fetch((0, width), output_weight_ref, local.at[1]).wait()
    middle_ref[...] = dot_plain(mixed_ref[...], flat(output_weight_ref[...]))
    act(("step_two", feed[1]), ("step_one", feed[2]))

    def second(r0):
        rows = pl.ds(r0, BLOCK)
        branch = middle_ref[rows, :]
        middle = tokens_ref[rows, :].astype(f32) + branch
        middle_ref[rows, :] = middle
        feed_ref[rows, :] = (unit_of(middle)[0] * gains_ref[1:2, :]).astype(bf16)
        set_row(sums_ref, 2, jnp.sum(branch * branch * valid_of(r0, BLOCK, ends), axis=0, keepdims=True))

    row_loop(total, BLOCK, second)
    act(("ready", feed[0]))
    feed_plan = {(0, 3): [("step_three", feed[1]), ("step_two", feed[2])], (1, 3): [("step_three", feed[2])]}

    tp = net.names(("tp",))
    quarters = list(np.ndindex(*(net.size[n] for n in tp)))
    both_kinds = range(2)

    def place(ref, quarter, kind, k):
        at = (2 * k + kind) * GROUP
        at = at if isinstance(at, int) else pl.multiple_of(at, GROUP)
        return ref.at[quarter + (slice(None),) * (len(ref.shape) - len(quarter) - 1) + (pl.ds(at, GROUP),)]

    def part(ref, q):
        return ref.at[(slice(None),) * (len(ref.shape) - 1) + (pl.ds(q * GROUP, GROUP),)]

    def chunk_copies(k, slot):
        return [
            pltpu.make_async_copy(
                place(feed_all, quarter, kind, k), part(chunk_ref.at[slot, kind], q), chunk_sem.at[slot, kind, q]
            )
            for kind in both_kinds
            for q, quarter in enumerate(quarters)
        ]

    def stage_copies(k):
        return [
            pltpu.make_async_copy(part(stage_ref.at[kind], q), place(grads_ref, quarter, kind, k), stage_sem.at[kind, q])
            for kind in both_kinds
            for q, quarter in enumerate(quarters)
        ]

    for copy in chunk_copies(0, 0):
        copy.start()
    out_ref[...] = jnp.zeros_like(out_ref)
    grad_middle_ref[...] = jnp.zeros_like(grad_middle_ref)

    def chunk(k, carry):
        slot = lax.rem(k, 2)
        for copy in chunk_copies(k, slot):
            copy.wait()

        def weights(kind):
            return chunk_ref[slot, kind].reshape(width, len(quarters) * GROUP)

        for q in range(len(quarters)):
            for (a, b), todo in feed_plan.items():
                if q == b:
                    pl.when(k == a)(lambda todo=todo: act(*todo))
            if q == 1:

                @pl.when(k > 0)
                def _():
                    for copy in stage_copies(k - 1):
                        copy.wait()

                for j in range(EARLY):

                    @pl.when(k == j + 1)
                    def _(j=j):
                        for p in folds[2 * j : 2 * j + 2]:
                            p.send(0)

            cols = slice(q * GROUP, (q + 1) * GROUP)
            hidden = dot_plain(feed_ref[...], weights(0)[:, cols])
            grad_active = dot_plain(grad_ref[...], weights(1)[:, cols])
            share = 0.5 * (1.0 + lax.erf(hidden * 0.7071067811865476))
            active_ref[:, cols] = (hidden * share).astype(bf16)
            slope = share + hidden * (jnp.exp(-0.5 * hidden * hidden) * 0.3989422804014327)
            hidden_ref[:, cols] = (grad_active * slope).astype(bf16)
        for j in range(chunks - 1):

            @pl.when(k == j)
            def _(j=j):
                act(("ready", feed[j + 1]))
                for copy in chunk_copies(j + 1, (j + 1) % 2):
                    copy.start()

        for j in range(EARLY):

            @pl.when(k == j + 1)
            def _(j=j):
                for p in folds[2 * j : 2 * j + 2]:
                    p.add(0)
                    p.send(1)

        out_ref[...] += dot_last(active_ref[...], weights(1))
        grad_middle_ref[...] += dot_last(hidden_ref[...], weights(0))
        for kind, (left, right) in enumerate(((feed_ref, hidden_ref), (grad_ref, active_ref))):
            stage_ref[kind] = dot_first(left[...], right[...]).reshape(stage_ref.shape[1:]).astype(bf16)
        for copy in stage_copies(k):
            copy.start()
        return carry

    lax.fori_loop(0, chunks, chunk, 0)

    for i in range(total // BLOCK):
        rows = pl.ds(i * BLOCK, BLOCK)
        middle, out, back = middle_ref[rows, :], out_ref[rows, :], grad_middle_ref[rows, :]
        result_ref[rows, :] = (middle + out).astype(bf16)
        unit, inv = unit_of(middle)
        grad_middle_ref[rows, :] = grad_ref[rows, :].astype(f32) + unit_back(back, unit, inv, gains_ref[1:2, :])
        set_row(sums_ref, 3, jnp.sum(out * out * valid_of(i * BLOCK, BLOCK, ends), axis=0, keepdims=True))
        set_row(sums_ref, 0, jnp.sum(back * unit, axis=0, keepdims=True))
        for j, (ref, target) in enumerate(((result_ref, result_hbm), (grad_middle_ref, grad_middle_hbm))):
            outs.append(pltpu.make_async_copy(ref.at[rows], target.at[rows], store_sem.at[4 + 2 * i + j]))
            outs[-1].start()
    for i, (p, target) in enumerate(zip(folds, (half_0, half_1, half_2, half_3))):
        p.add(1)
        outs.append(pltpu.make_async_copy(p.bufs[1].at[pl.ds(0, 1)], target, local.at[i]))
        outs[-1].start()
    for copy in outs:
        copy.wait()
    for copy in stage_copies(chunks - 1):
        copy.wait()
    for p in folds:
        p.drain()
    for pair in att + feed:
        for piece in pair:
            piece.drain()


def run_fused_forward(net, clip, tokens, out_grad, weights, gain_tile, w_expand, w_reduce):
    total, width = tokens.shape
    rows, rows_feed = width // net.count, w_expand.shape[0]
    lanes, hid = 4 * width + LANES, w_expand.shape[1]
    flip = BOTH[::-1]
    ff = (*net.dims(flip), rows_feed, 2 * hid)
    wide = GROUP * int(np.prod(net.dims(("tp",))))
    inner = tuple(net.size[n] for n in net.names(("dp",))) + (rows_feed, wide)
    count = 2 * (len(att_spans(width)) + hid // GROUP) * copies_of(net) + 4 * EARLY * max(net.size.values())
    dma = pltpu.SemaphoreType.DMA
    early, halves_out = [], []
    for k in range(EARLY):
        for fold in feed_folds(k):
            shapes = Fold.shapes(net, flip, rows_feed, *fold)[:2]
            early += [pltpu.VMEM(dims, bf16) for dims in shapes]
            halves_out.append(shape(1, *shapes[1][1:]))
    return pl.pallas_call(
        lambda *refs: fused_forward_kernel(net, *refs),
        name="layer_forward_feed",
        out_shape=(
            shape(*net.dims(BOTH), rows, lanes), shape(*ff), shape(total, 3 * width), shape(total, width),
            shape(total, width), shape(total, width), shape(*ff), shape(total, width),
            shape(total, width, kind=f32), shape(8, width, kind=f32), shape(8, width, kind=f32), *halves_out,
        ),
        in_specs=[SM, VM] + [ANY] * 8,
        out_specs=(ANY, ANY, ANY, ANY, ANY, ANY, ANY, ANY, ANY, VM, VM) + (ANY,) * len(halves_out),
        scratch_shapes=[
            pltpu.VMEM((total, 3 * width), bf16), pltpu.VMEM((total, width), bf16), pltpu.VMEM((total, width), bf16),
            pltpu.VMEM((total, width), bf16), pltpu.VMEM((total, width), bf16), pltpu.VMEM((total, width), f32), dma((4 + 2 * total // BLOCK,)),
            pltpu.VMEM((rows, lanes), bf16), pltpu.VMEM((rows_feed, 2 * hid), bf16), pltpu.VMEM((*net.dims(BOTH), rows, LANES), bf16),
            pltpu.VMEM((2, *net.dims(BOTH), rows, TRIO), bf16), pltpu.VMEM((*net.dims(BOTH), rows, width), bf16),
            pltpu.VMEM((total, width), bf16),
            pltpu.VMEM((total, width), f32), pltpu.VMEM((total, width), bf16), pltpu.VMEM((total, wide), bf16),
            pltpu.VMEM((total, wide), bf16), pltpu.VMEM((total, width), f32), pltpu.VMEM((2, 2, *inner), bf16),
            pltpu.VMEM((2, *inner), bf16), pltpu.VMEM((total, LANES), bf16), pltpu.VMEM((total, LANES), bf16),
            dma((count,)), dma((count,)),
            dma((4 + 3 * (width // LANES) + 2 * hid // GROUP,)), dma((2, 2, wide // GROUP)), dma((2, wide // GROUP)),
            *early,
        ],
        compiler_params=params(collective_id=1, has_side_effects=True),
    )(clip, tokens, w_reduce, out_grad, *weights, gain_tile, w_expand)


def store_at(ref, index, lanes, value):
    ref[tuple(index) + (slice(None), lanes)] = value


def each(dims, body, index=()):
    count = 1
    for size in dims:
        count *= size
    if count <= 4:
        for tail in np.ndindex(*dims):
            body(index + tail)
    else:

        def step(i, carry):
            each(dims[1:], body, index + (i,))
            return carry

        lax.fori_loop(0, dims[0], step, 0)


class Fold:
    def __init__(self, net, sems, ref, order, lanes, along, bufs, out=None, own=None, steps=(0, 1, 2, 3)):
        self.net, self.lanes, self.along, self.bufs, self.out, self.steps = net, lanes, along, bufs, out, steps
        names = net.names(order)
        self.names = [[n for n in names if n not in along[:k]] for k in range(5)]
        self.ref, self.own = ref, own
        self.copies = {}
        for k in steps:
            dim = along[k]
            source, cols = (ref, lanes) if k == 0 else (bufs[k - 1].at[0], (0, lanes[1]))
            self.copies[k] = []
            for o, v in enumerate(net.peers(dim)):
                index = tuple(v if n == dim else slice(None) for n in self.names[k])
                s, r = sems.take()
                self.copies[k].append(
                    pltpu.make_async_remote_copy(
                        src_ref=source.at[index + (slice(None), pl.ds(*cols))], dst_ref=bufs[k].at[o],
                        send_sem=s, recv_sem=r, device_id=net.device(dim, v), device_id_type=MESH,
                    )
                )

    @staticmethod
    def shapes(net, order, rows, lanes, along):
        names, out = net.names(order), []
        for k, dim in enumerate(along):
            left = [net.size[n] for n in names if n not in along[: k + 1]]
            out.append((net.size[dim] - 1, *left, rows, lanes[1]))
        return out

    def send(self, k):
        begin(self.copies[k])

    def add(self, k):
        arrive(self.copies[k])
        dim, buf, cols = self.along[k], self.bufs[k], slice(0, self.lanes[1])
        here = self.net.place[dim]
        wide = pl.ds(*self.lanes)

        def one(index):
            at = dict(zip(self.names[k + 1], index))
            full = tuple(at.get(n, here) for n in self.names[k])
            if k > 0:
                total = self.bufs[k - 1][(0,) + full + (slice(None), cols)].astype(f32)
            elif self.own is not None:
                total = self.own(index).astype(f32)
            else:
                total = self.ref[full + (slice(None), wide)].astype(f32)
            terms = [total] + [buf[(o,) + index].astype(f32) for o in range(self.net.size[dim] - 1)]
            if len(terms) > 2:
                size = len(terms)
                total = 0.0
                for v in range(size):
                    back = lax.rem(here - v + size, size)
                    term = terms[0]
                    for o in range(1, size):
                        term = jnp.where(back == o, terms[o], term)
                    total = total + term
            else:
                total = terms[0] + terms[1]
            if k == 3:
                self.out[:, wide] = total
            else:
                buf[(0,) + index] = total.astype(bf16)

        each([self.net.size[n] for n in self.names[k + 1]], one)

    def drain(self):
        for copies in self.copies.values():
            for copy in copies:
                copy.wait_send()


ALONG = (("c", "x", "y", "z"), ("c", "y", "x", "z"))


def feed_folds(k):
    return [((2 * GROUP * k + GROUP * i, GROUP), ALONG[i]) for i in range(2)]


EARLY = 2


def att_folds(width):
    out = []
    spans = [(0, width + LANES)] + [(width + LANES + p * TRIO, TRIO) for p in range(width // LANES)]
    for start, size in spans:
        for i, (at, take) in enumerate(lane_parts(size, 2)):
            out.append(((start + at, take), ALONG[i % 2]))
    return out


def run_backward(net, clip, grad_middle, mixed, qkv, extra, normed, tokens, weights, gains, *more_args):
    total, width = tokens.shape
    lanes = weights.shape[1]
    scratch = [
        pltpu.VMEM((total, width), bf16), pltpu.VMEM((total, width), bf16), pltpu.VMEM((total, 3 * width), bf16),
        pltpu.VMEM((total, LANES), f32), pltpu.VMEM((total, width), bf16), pltpu.VMEM((total, LANES), bf16),
    ]
    operands = [clip, grad_middle, mixed, qkv, extra, normed, tokens, weights, gains]
    in_specs = [SM, VM, VM, ANY, ANY, ANY, ANY, ANY, VM]
    out_shape = (shape(width, lanes), shape(total, width, kind=f32))
    more = {}
    if net is not None:
        feed_grads = more_args[1]
        rows, rows_feed = width // net.count, feed_grads.shape[-2]
        hid = feed_grads.shape[-1] // 2
        flip = BOTH[::-1]
        operands += more_args
        in_specs += [VM, ANY] + [VM] * (2 * EARLY)
        out_shape = (shape(rows, lanes, kind=f32), shape(rows_feed, 2 * hid, kind=f32), out_shape[1])
        scratch.append(pltpu.VMEM((*net.dims(BOTH), rows, lanes), bf16))
        kept = tuple(net.size[n] for n in net.names(flip) if n != "c")
        scratch.append(pltpu.VMEM((*kept, rows_feed, 2 * hid - 2 * GROUP * EARLY), bf16))
        bufs = []
        for k in range(hid // GROUP):
            for f in feed_folds(k):
                bufs += Fold.shapes(net, flip, rows_feed, *f)[2 if k < EARLY else 0 :]
        for f in att_folds(width):
            bufs += Fold.shapes(net, BOTH, rows, *f)
        count = sum(dims[0] for dims in bufs)
        scratch += [pltpu.SemaphoreType.DMA((count,)), pltpu.SemaphoreType.DMA((count,)), pltpu.SemaphoreType.DMA]
        scratch += [pltpu.VMEM(dims, bf16) for dims in bufs]
        more = dict(collective_id=2, has_side_effects=True)
    scratch += [
        pltpu.VMEM((total, 3 * width), bf16), pltpu.VMEM((total, width), bf16), pltpu.VMEM((total, width), bf16),
        pltpu.VMEM((width, width), bf16), pltpu.VMEM((width, 3 * width), bf16), pltpu.VMEM((total, width), f32),
        pltpu.SemaphoreType.DMA((6,)), pltpu.SemaphoreType.DMA((total // BLOCK,)),
    ]
    return pl.pallas_call(
        lambda *refs: backward_kernel(net, *refs),
        name="layer_backward",
        out_shape=out_shape,
        in_specs=in_specs,
        out_specs=(VM,) * (len(out_shape) - 1) + (ANY,),
        scratch_shapes=scratch,
        compiler_params=params(**more),
        cost_estimate=pl.CostEstimate(flops=22 * 10**9, bytes_accessed=30 << 20, transcendentals=0),
    )(*operands)


def unpack_kernel(
    shard_ref, feed_ref, w_query_ref, w_key_ref, w_value_ref, gain_ref, result_in, grad_in,
    query_ref, key_ref, value_ref, output_ref, expand_ref, reduce_ref, tile_ref, result_out, grad_out,
    result_ref, grad_ref, sem,
):
    width = output_ref.shape[1]
    parts = [
        (source.at[pl.ds(r0, BLOCK)], held.at[pl.ds(r0, BLOCK)], target.at[pl.ds(r0, BLOCK)])
        for r0 in range(0, result_ref.shape[0], BLOCK)
        for source, held, target in ((result_in, result_ref, result_out), (grad_in, grad_ref, grad_out))
    ]
    loads = [pltpu.make_async_copy(source, held, sem.at[i]) for i, (source, held, _) in enumerate(parts)]
    copies = [pltpu.make_async_copy(held, target, sem.at[i]) for i, (_, held, target) in enumerate(parts)]
    begin(loads)
    output_ref[...] = shard_ref[:, :width]
    for k in range(expand_ref.shape[1] // GROUP):
        cols = slice(k * GROUP, (k + 1) * GROUP)
        expand_ref[:, cols] = feed_ref[:, 2 * k * GROUP : (2 * k + 1) * GROUP]
        reduce_ref[:, cols] = feed_ref[:, (2 * k + 1) * GROUP : (2 * k + 2) * GROUP]
    gain = 0.0
    owned = (w_query_ref, w_key_ref, w_value_ref)
    for j, (out, weight) in enumerate(zip((query_ref, key_ref, value_ref), owned)):
        for p in range(width // LANES):
            at = width + LANES + p * TRIO + j * LANES
            out[:, p * LANES : (p + 1) * LANES] = shard_ref[:, at : at + LANES]
        gain = gain + jnp.sum(weight[...].astype(f32) * out[...], axis=1, keepdims=True)
    gain = gain / gain_ref[:, :1].astype(f32)
    lane = lax.broadcasted_iota(jnp.int32, (1, LANES), 1)
    tile = shard_ref[:, width : width + LANES]
    means = jnp.sqrt(tile / (tile[:, 4:5] * width))
    tile = jnp.where(lane == 5, gain, jnp.where(lane == 0, tile, means))
    tile = jnp.concatenate([tile, jnp.zeros((LANES - tile.shape[0], LANES), f32)], axis=0)
    tile_ref[...] = tile.T[:8]
    for load, copy in zip(loads, copies):
        load.wait()
        copy.start()
    for copy in copies:
        copy.wait()


def run_unpack(shard, shard_feed, weights, gain_tile, result, grad_tokens):
    rows, width = weights[0].shape
    rows_feed, both = shard_feed.shape
    return pl.pallas_call(
        unpack_kernel,
        name="unpack_outputs",
        out_shape=(
            *(shape(rows, width, kind=f32) for _ in range(4)), shape(rows_feed, both // 2, kind=f32),
            shape(rows_feed, both // 2, kind=f32), shape(8, LANES, kind=f32),
            shape(*result.shape), shape(*grad_tokens.shape, kind=f32),
        ),
        in_specs=[VM] * 6 + [ANY] * 2,
        out_specs=(VM,) * 7 + (ANY,) * 2,
        scratch_shapes=[
            pltpu.VMEM(result.shape, bf16), pltpu.VMEM(grad_tokens.shape, f32),
            pltpu.SemaphoreType.DMA((2 * result.shape[0] // BLOCK,)),
        ],
        compiler_params=params(),
    )(shard, shard_feed, *weights, gain_tile, result, grad_tokens)


def on_device(
    net,
    tokens, clip_lengths, out_grad, w_query, w_key, w_value, w_output, gain_attention, gain_feed, w_expand, w_reduce,
):
    _, total, width = tokens.shape
    rows = tokens.reshape(total, width)
    out_grad = out_grad.reshape(total, width)
    lane = lax.broadcasted_iota(jnp.int32, (1, LANES), 1)
    gain_tile = jnp.where(lane == 0, gain_attention[:, None], jnp.where(lane == 1, gain_feed[:, None], 0))
    hid = w_expand.shape[1]
    if net is not None:
        weights, _, qkv, mixed, extra, normed, feed_grads, result, grad_middle, sums, gains, *early = run_fused_forward(
            net, clip_lengths, rows, out_grad, (w_query, w_key, w_value, w_output), gain_tile, w_expand, w_reduce.T
        )
        weights = weights.reshape(width, -1)
        shard, shard_feed, grad_tokens = run_backward(
            net, clip_lengths, grad_middle, mixed, qkv, extra, normed, rows, weights, gains, sums, feed_grads, *early
        )
        query, key, value, output, expand, reduce, tile, result, grad_tokens = run_unpack(
            shard, shard_feed, (w_query, w_key, w_value), gain_tile, result, grad_tokens
        )
        count = gain_feed.shape[0]
        gain_one, gain_two, means, reduce = tile[5, :count], tile[0, :count], tile[1:4, 0], reduce.T
    else:
        mine = [w_output, gain_tile]
        for p in range(width // LANES):
            mine += [w[:, p * LANES : (p + 1) * LANES] for w in (w_query, w_key, w_value)]
        weights = lax.all_gather(jnp.concatenate(mine, axis=1), BOTH, axis=0, tiled=True)
        both = jnp.concatenate([w_expand, w_reduce.T], axis=1)
        feed_weights = lax.all_gather(both, BOTH[::-1], axis=0, tiled=True).reshape(-1, width, 2 * hid)
        gains = jnp.pad(weights[:, width : width + 2].T.astype(f32), ((0, 6), (0, 0)))
        qkv, mixed, extra, middle, feed, normed, sums_one = run_forward(clip_lengths, rows, weights, gains)
        feed_grads, result, grad_middle, sums_two = run_feed(
            clip_lengths, feed, out_grad, middle, gains, feed_weights
        )
        count = jnp.sum(clip_lengths[:, : SLOTS - 1]).astype(f32)
        squares = jnp.stack([jnp.sum(sums_one[0]), jnp.sum(sums_one[1]), jnp.sum(sums_two[0]), count])
        grads, grad_tokens = run_backward(
            None, clip_lengths, grad_middle, mixed, qkv, extra, normed, rows, weights, gains
        )
        shard = lax.psum_scatter(grads, BOTH, scatter_dimension=0, tiled=True).astype(f32)
        shard_feed = lax.psum_scatter(
            feed_grads.reshape(-1, 2 * hid), BOTH[::-1], scatter_dimension=0, tiled=True
        ).astype(f32)
        stats = lax.psum(squares, BOTH)
        gain_two = lax.psum_scatter(sums_two[1], BOTH, scatter_dimension=0, tiled=True)
        means = jnp.sqrt(stats[:3] / (stats[3] * width))
        parts = shard[:, width + LANES :].reshape(-1, width // LANES, 3, LANES)
        query, key, value = (parts[:, :, j].reshape(-1, width) for j in range(3))
        pairs = ((w_query, query), (w_key, key), (w_value, value))
        gain_one = sum(jnp.sum(w.astype(f32) * g, axis=1) for w, g in pairs) / gain_attention.astype(f32)
        output, expand, reduce = shard[:, :width], shard_feed[:, :hid], shard_feed[:, hid:].T
    return (
        result.reshape(1, total, width),
        grad_tokens.reshape(1, total, width),
        query,
        key,
        value,
        output,
        gain_one,
        gain_two,
        expand,
        reduce,
        means,
    )


def solution(mesh):
    row, flat = P(BOTH, None), P(BOTH)
    whole = P(BOTH, None, None)
    in_specs = (whole, row, whole, row, row, row, row, flat, flat, P("dp", "tp"), P("tp", "dp"))
    out_specs = (whole, whole, row, row, row, row, flat, flat, P("dp", "tp"), P("tp", "dp"), P())
    factors = FACTORS.get((mesh.shape["dp"], mesh.shape["tp"]))
    net = Net(factors) if factors else None
    return jax.shard_map(
        lambda *args: on_device(net, *args), mesh=mesh, in_specs=in_specs, out_specs=out_specs, check_vma=False
    )
```

```python
import jax
import jax.numpy as jnp
import numpy as np
from jax import lax
from jax.experimental import pallas as pl
from jax.experimental.pallas import tpu as pltpu
from jax.sharding import PartitionSpec as P

HEADS = 12
HEAD_DIM = 64
SLOTS = 4
LANES = 128
BLOCK = 256
WIDE = 512
MAXCLIP = 384
GROUP = 256
TRIO = 3 * LANES
NEG = -1e30
LOG2E = 1.4426950408889634
LN2 = 0.6931471805599453
f32 = jnp.float32
bf16 = jnp.bfloat16
BOTH = ("dp", "tp")
VM = pl.BlockSpec(memory_space=pltpu.VMEM)
SM = pl.BlockSpec(memory_space=pltpu.SMEM)


def dot_plain(left, right):
    return jnp.dot(left, right, preferred_element_type=f32)


def dot_first(left, right):
    return lax.dot_general(left, right, (((0,), (0,)), ((), ())), preferred_element_type=f32)


def dot_last(left, right):
    return lax.dot_general(left, right, (((1,), (1,)), ((), ())), preferred_element_type=f32)


def unit_of(rows):
    centred = rows - jnp.mean(rows, axis=-1, keepdims=True)
    inv = lax.rsqrt(jnp.mean(centred * centred, axis=-1, keepdims=True) + 1e-06)
    return centred * inv, inv


def unit_back(grad, unit, inv, gain):
    scaled = grad * gain
    inner = (
        scaled
        - jnp.mean(scaled, axis=-1, keepdims=True)
        - unit * jnp.mean(scaled * unit, axis=-1, keepdims=True)
    )
    return inv * inner


def clip_ends(clip_ref):
    ends, total = [], jnp.int32(0)
    for j in range(SLOTS - 1):
        total = total + clip_ref[0, j]
        ends.append(total)
    return ends


def segment_of(position, ends):
    return sum((position >= e).astype(jnp.int32) for e in ends)


def valid_of(start, count, ends):
    position = start + lax.broadcasted_iota(jnp.int32, (count, 1), 0)
    return (position < ends[-1]).astype(f32)


def row_loop(total, size, body):
    def step(i, carry):
        body(pl.multiple_of(i * size, size))
        return carry

    lax.fori_loop(0, total // size, step, 0)


def head_masks(scale):
    lane = lax.broadcasted_iota(jnp.int32, (1, LANES), 1)
    low = lane < HEAD_DIM
    return lane, low, (jnp.where(low, scale, 0.0).astype(bf16), jnp.where(low, 0.0, scale).astype(bf16))


def lane_index():
    lane = lax.broadcasted_iota(jnp.int32, (1, LANES), 1)
    return lane, lax.rem(lane, HEAD_DIM)


def split_three(value):
    high = value.astype(bf16)
    rest = value - high.astype(f32)
    middle = rest.astype(bf16)
    return high, middle, (rest - middle.astype(f32)).astype(bf16)


def in_lanes(at, first, terms, other):
    out = other
    for i, term in enumerate(terms):
        out = jnp.where(at == first + i, term.astype(f32), out)
    return out


def set_codes(query_ref, key_ref, ends):
    _, at = lane_index()

    def block(r0):
        rows = pl.ds(r0, BLOCK)
        seg = segment_of(r0 + lax.broadcasted_iota(jnp.int32, (BLOCK, 1), 0), ends)
        own = at == seg
        if query_ref is not None:
            query_ref[rows, :] = jnp.where(own, NEG, 0.0).astype(bf16)
        key_ref[rows, :] = jnp.where((at < SLOTS + 3) & jnp.logical_not(own), 1.0, 0.0).astype(bf16)

    row_loop(key_ref.shape[0], BLOCK, block)


def inner_codes(grad_ref, mixed_ref, out_ref):
    total, width = mixed_ref.shape
    _, at = lane_index()
    _, low, _ = head_masks(1.0)

    def block(r0):
        rows = pl.ds(r0, LANES)
        for p in range(width // LANES):
            cols = slice(p * LANES, (p + 1) * LANES)
            both = grad_ref[rows, cols].astype(f32) * mixed_ref[rows, cols].astype(f32)
            sums = (
                jnp.sum(jnp.where(low, both, 0.0), axis=1, keepdims=True),
                jnp.sum(jnp.where(low, 0.0, both), axis=1, keepdims=True),
            )
            first, second = (in_lanes(at, 0, split_three(-x), 0.0) for x in sums)
            out_ref[rows, cols] = jnp.where(low, second, first).astype(bf16)

    row_loop(total, LANES, block)


def set_row(ref, row, value):
    at = lax.broadcasted_iota(jnp.int32, ref.shape, 0) == row
    ref[...] += jnp.where(at, value, 0.0)


def forward_kernel(
    clip_ref, tokens_ref, weights_ref, gains_ref,
    qkv_ref, mixed_ref, extra_ref, middle_ref, feed_ref, normed_ref, sums_ref,
    code_q_ref, code_k_ref,
):
    total, width = tokens_ref.shape
    ends = clip_ends(clip_ref)
    sums_ref[...] = jnp.zeros_like(sums_ref)

    def norm(r0):
        rows = pl.ds(r0, BLOCK)
        x = tokens_ref[rows, :].astype(f32)
        normed_ref[rows, :] = (unit_of(x)[0] * gains_ref[0:1, :]).astype(bf16)
        set_row(sums_ref, 0, jnp.sum(x * x * valid_of(r0, BLOCK, ends), axis=0, keepdims=True))

    row_loop(total, BLOCK, norm)
    set_codes(code_q_ref, code_k_ref, ends)
    for p in range(width // LANES):
        weight = weights_ref[:, width + LANES + p * TRIO : width + LANES + (p + 1) * TRIO]
        project(normed_ref, pl.ds(0, total), weight, qkv_ref, p)

    def pair_block(i, carry):
        blocks = total // WIDE
        pair_forward(
            lax.div(i, blocks), lax.rem(i, blocks), total, qkv_ref, mixed_ref, extra_ref, code_q_ref, code_k_ref
        )
        return carry

    lax.fori_loop(0, width // LANES * (total // WIDE), pair_block, 0)
    middle_ref[...] = dot_plain(mixed_ref[...], weights_ref[:, :width])

    def second(r0):
        rows = pl.ds(r0, BLOCK)
        branch = middle_ref[rows, :]
        middle = tokens_ref[rows, :].astype(f32) + branch
        middle_ref[rows, :] = middle
        feed_ref[rows, :] = (unit_of(middle)[0] * gains_ref[1:2, :]).astype(bf16)
        set_row(sums_ref, 1, jnp.sum(branch * branch * valid_of(r0, BLOCK, ends), axis=0, keepdims=True))

    row_loop(total, BLOCK, second)


def feed_kernel(
    clip_ref, feed_ref, out_grad_ref, middle_ref, gains_ref, weights_ref,
    grads_ref, result_ref, grad_middle_ref, sums_ref,
    grad_ref, active_ref, hidden_ref, out_ref, back_ref,
):
    total, width = feed_ref.shape
    ends = clip_ends(clip_ref)
    step = pl.program_id(0)

    @pl.when(step == 0)
    def _():
        def mask(r0):
            rows = pl.ds(r0, BLOCK)
            grad_ref[rows, :] = (out_grad_ref[rows, :].astype(f32) * valid_of(r0, BLOCK, ends)).astype(bf16)

        row_loop(total, BLOCK, mask)
        out_ref[...] = jnp.zeros_like(out_ref)
        back_ref[...] = jnp.zeros_like(back_ref)
        sums_ref[...] = jnp.zeros_like(sums_ref)

    hid = weights_ref.shape[2] - width
    part = 256
    for n in range(hid // part):
        cols = slice(n * part, (n + 1) * part)
        late = slice(hid + n * part, hid + (n + 1) * part)
        hidden = dot_plain(feed_ref[...], weights_ref[0, :, cols])
        grad_active = dot_plain(grad_ref[...], weights_ref[0, :, late])
        share = 0.5 * (1.0 + lax.erf(hidden * 0.7071067811865476))
        active_ref[:, cols] = (hidden * share).astype(bf16)
        slope = share + hidden * (jnp.exp(-0.5 * hidden * hidden) * 0.3989422804014327)
        hidden_ref[:, cols] = (grad_active * slope).astype(bf16)
    expand, reduce = weights_ref[0, :, :hid], weights_ref[0, :, hid:]
    out_ref[...] += dot_last(active_ref[...], reduce)
    back_ref[...] += dot_last(hidden_ref[...], expand)
    grads_ref[0, :, :hid] = dot_first(feed_ref[...], hidden_ref[...]).astype(bf16)
    grads_ref[0, :, hid:] = dot_first(grad_ref[...], active_ref[...]).astype(bf16)

    @pl.when(step == pl.num_programs(0) - 1)
    def _():
        def finish(r0):
            rows = pl.ds(r0, BLOCK)
            valid = valid_of(r0, BLOCK, ends)
            middle, out, back = middle_ref[rows, :], out_ref[rows, :], back_ref[rows, :]
            result_ref[rows, :] = (middle + out).astype(bf16)
            unit, inv = unit_of(middle)
            grad_middle_ref[rows, :] = (
                grad_ref[rows, :].astype(f32) + unit_back(back, unit, inv, gains_ref[1:2, :])
            )
            set_row(sums_ref, 0, jnp.sum(out * out * valid, axis=0, keepdims=True))
            set_row(sums_ref, 1, jnp.sum(back * unit, axis=0, keepdims=True))

        row_loop(total, BLOCK, finish)


def static_windows(total):
    spans = []
    for r0 in range(0, total, WIDE):
        low = max(0, r0 - MAXCLIP + 1) // LANES * LANES
        high = min(total, -(-(r0 + WIDE + MAXCLIP - 1) // LANES) * LANES)
        spans.append((low, high))
    width = max(high - low for low, high in spans)
    return [min(low, total - width) for low, _ in spans], width


def start_of(starts, block):
    at = jnp.int32(starts[0])
    for i, s in enumerate(starts):
        at = jnp.where(block == i, s, at)
    return pl.multiple_of(at, LANES)


def pair_parts(p, block, total):
    starts, cols = static_windows(total)
    rows = pl.ds(pl.multiple_of(block * WIDE, WIDE), WIDE)
    win = pl.ds(start_of(starts, block), cols)
    return rows, win, [pl.ds(pl.multiple_of(p * TRIO + j * LANES, LANES), LANES) for j in range(3)]


def with_codes(value, code, plain):
    return value * plain[0] + code * plain[1], value * plain[1] + code * plain[0]


def pair_forward(p, block, total, qkv_ref, mixed_ref, extra_ref, code_q_ref, code_k_ref):
    _, at = lane_index()
    _, low, plain = head_masks(1.0)
    rows, win, (at_q, at_k, at_v) = pair_parts(p, block, total)
    query, keys, values = qkv_ref[rows, at_q], qkv_ref[win, at_k], qkv_ref[win, at_v]
    values = jnp.concatenate([values, jnp.ones_like(values)], axis=1)
    code = code_q_ref[rows, :]
    queries, keys = with_codes(query, code, plain), with_codes(keys, code_k_ref[win, :], plain)
    outs, extras = [], []
    for h in range(2):
        scores = dot_last(queries[h], keys[h])
        top = jnp.max(scores, axis=1, keepdims=True)
        mixed = dot_plain(jnp.exp2(scores - top).astype(bf16), values)
        row_sum = mixed[:, LANES:]
        outs.append(mixed[:, :LANES] / row_sum)
        extras.append(in_lanes(at, SLOTS, split_three(-(top + LOG2E * jnp.log(row_sum))), code.astype(f32)))
    lanes = pl.ds(pl.multiple_of(p * LANES, LANES), LANES)
    mixed_ref[rows, lanes] = jnp.where(low, outs[0], outs[1]).astype(bf16)
    extra_ref[rows, lanes] = jnp.where(low, extras[1], extras[0]).astype(bf16)


def pair_back(p, block, total, qkv_ref, grad_ref, extra_ref, inner_ref, code_k_ref, dqkv_ref, dq_ref):
    _, at = lane_index()
    _, low, scaled = head_masks(0.125)
    _, _, plain = head_masks(1.0)
    rows, win, (at_q, at_k, at_v) = pair_parts(p, block, total)
    lanes = pl.ds(pl.multiple_of(p * LANES, LANES), LANES)
    keys, values, query, grad = qkv_ref[rows, at_k], qkv_ref[rows, at_v], qkv_ref[win, at_q], grad_ref[win, lanes]
    ones = jnp.where(at < 3, 1.0, 0.0).astype(bf16)
    key_codes, query_codes = with_codes(keys, code_k_ref[rows, :], plain), with_codes(query, extra_ref[win, lanes], plain)
    value_codes, grad_codes = with_codes(values, ones, plain), with_codes(grad, inner_ref[win, lanes], plain)
    dk, dv, dq = [], [], 0.0
    for h in range(2):
        probs = jnp.exp2(dot_last(key_codes[h], query_codes[h]))
        dv.append(dot_plain(probs.astype(bf16), grad))
        ds = (probs * dot_last(value_codes[h], grad_codes[h])).astype(bf16)
        dk.append(dot_plain(ds, query))
        dq = dq + dot_first(ds, keys * scaled[h])
    dq_ref[win, :] += dq
    dqkv_ref[rows, at_k] = (jnp.where(low, dk[0], dk[1]) * LN2).astype(bf16)
    dqkv_ref[rows, at_v] = jnp.where(low, dv[0], dv[1]).astype(bf16)


def project(normed_ref, rows, weight, qkv_ref, p):
    lane = lax.broadcasted_iota(jnp.int32, (1, TRIO), 1)
    scale = jnp.where(lane < LANES, 0.125 * LOG2E, 1.0)
    at = pl.multiple_of(p * TRIO, LANES)
    qkv_ref[rows, pl.ds(at, TRIO)] = (dot_plain(normed_ref[rows, :], weight) * scale).astype(bf16)


def backward_kernel(
    net,
    clip_ref, grad_middle_hbm, mixed_hbm, qkv_hbm, extra_hbm, normed_hbm, tokens_hbm, weights_hbm, gains_ref,
    *refs,
):
    total, width = mixed_hbm.shape
    ends = clip_ends(clip_ref)
    refs, load_sem, store_sem = refs[:-2], *refs[-2:]
    refs, (qkv_ref, extra_ref, normed_ref, output_weight_ref, weight_ref, sum_ref) = refs[:-6], refs[-6:]
    refs, (grad_middle_ref, mixed_ref) = refs[:-2], refs[-2:]
    if net is not None:
        net.locate()
        net.announce()
    firsts = [
        pltpu.make_async_copy(grad_middle_hbm, grad_middle_ref, load_sem.at[6]),
        pltpu.make_async_copy(mixed_hbm, mixed_ref, load_sem.at[7]),
    ]
    begin(firsts)
    pairs = width // LANES
    loads = [
        pltpu.make_async_copy(source, target, load_sem.at[i])
        for i, (source, target) in enumerate(
            (
                (weights_hbm.at[:, pl.ds(0, width)], output_weight_ref),
                (qkv_hbm, qkv_ref),
                (extra_hbm, extra_ref),
                (normed_hbm, normed_ref),
                (weights_hbm.at[:, pl.ds(width + LANES, pairs * TRIO)], weight_ref),
            )
        )
    ]
    if net is None:
        begin(loads)
        grads_ref, grad_tokens_ref, low_ref, grad_ref, dqkv_ref, dq_ref, inner_ref, code_k_ref = refs
        plan = {}
    else:
        sums_ref, feed_grads_ref, *refs = refs
        early, refs = refs[: 2 * EARLY], refs[2 * EARLY :]
        shard_ref, shard_feed_ref, grad_tokens_ref, low_ref, grad_ref, dqkv_ref, dq_ref, inner_ref, *refs = refs
        code_k_ref, grads_ref, own_ref, send, recv, local, *bufs = refs
        held, bufs = bufs[: 2 * EARLY], bufs[2 * EARLY :]
        halves_in = [
            pltpu.make_async_copy(source, target, load_sem.at[8 + i])
            for i, (source, target) in enumerate(zip(early, held))
        ]
        begin(halves_in)
        begin(loads)
        early = held
        sems = Sems(send, recv)
        feed, att = [], []
        flip = BOTH[::-1]
        for k in range(EARLY):
            for lanes, along in feed_folds(k):
                slots, bufs = [None, early[len(feed)], *bufs[:2]], bufs[2:]
                feed.append(Fold(net, sems, None, flip, lanes, along, slots, shard_feed_ref, steps=(2, 3)))
        span = 2 * GROUP * EARLY
        for k in range(EARLY, feed_grads_ref.shape[-1] // (2 * GROUP)):
            for lanes, along in feed_folds(k):

                def kept(index, start=lanes[0] - span):
                    return own_ref[index + (slice(None), pl.ds(start, GROUP))]

                feed.append(
                    Fold(net, sems, feed_grads_ref, flip, lanes, along, bufs[:4], shard_feed_ref, own=kept)
                )
                bufs = bufs[4:]
        for lanes, along in att_folds(width):
            att.append(Fold(net, sems, grads_ref, BOTH, lanes, along, bufs[:4], shard_ref))
            bufs = bufs[4:]
        early, late = feed[: 2 * EARLY], feed[2 * EARLY :]
        net.meet()
        for p in late:
            p.send(0)
        for copy in halves_in:
            copy.wait()
        for p in early:
            p.send(2)
        mine = tuple(net.place["c"] if n == "c" else slice(None) for n in net.names(flip))
        own = pltpu.make_async_copy(
            feed_grads_ref.at[mine + (slice(None), pl.ds(span, feed_grads_ref.shape[-1] - span))], own_ref, local
        )
        own.start()
        tall = jnp.concatenate([sums_ref[...], jnp.zeros((LANES - 8, width), f32)], axis=0).T
        lane = lax.broadcasted_iota(jnp.int32, (1, LANES), 1)
        for j in range(1, 4):
            tall = jnp.where(lane == j, jnp.sum(sums_ref[j : j + 1, :], axis=1, keepdims=True), tall)
        extras = jnp.where(lane == 4, ends[-1].astype(f32), tall)

    def advance(*todo):
        for pieces, step in todo:
            for piece in pieces:
                piece.add(step)
                if step < 3:
                    piece.send(step + 1)

    def store(lanes, value):
        if net is None:
            grads_ref[:, lanes] = value.astype(bf16)
        else:
            rows = grads_ref.shape[-2]
            for i, index in enumerate(np.ndindex(*net.dims(BOTH))):
                grads_ref[index + (slice(None), lanes)] = value[i * rows : (i + 1) * rows].astype(bf16)

    if net is not None:
        store(slice(width, width + LANES), extras)
    for copy in firsts:
        copy.wait()
    low_ref[...] = grad_middle_ref[...].astype(bf16)
    store(slice(0, width), dot_first(mixed_ref[...], low_ref[...]))
    if net is not None:
        for p in att[:2]:
            p.send(0)
    loads[0].wait()
    grad_ref[...] = dot_last(low_ref[...], output_weight_ref[...]).astype(bf16)
    tokens_ref = low_ref
    tokens = pltpu.make_async_copy(tokens_hbm, tokens_ref, load_sem.at[5])
    tokens.start()
    set_codes(None, code_k_ref, ends)
    inner_codes(grad_ref, mixed_ref, inner_ref)
    moves, ending = {}, {}
    if net is not None:
        own.wait()
        output, pair = att[:2], [att[2 + 2 * p : 4 + 2 * p] for p in range(pairs)]
        moves = {
            0: [(late, 0)],
            1: [(output, 0)],
            2: [(early, 2)],
            3: [(pair[0], 0)],
            4: [(late, 1), (output, 1)],
            5: [(pair[1], 0), (pair[0], 1)],
            6: [(output, 2)],
            7: [(pair[2], 0), (pair[1], 1), (late, 2), (pair[0], 2)],
            8: [(early, 3)],
            9: [(pair[3], 0), (pair[2], 1), (pair[1], 2)],
            10: [(output, 3), (pair[0], 3)],
            11: [(pair[4], 0), (pair[3], 1), (pair[2], 2), (late, 3)],
        }
        ending = {
            0: [(pair[4], 1), (pair[3], 2), (pair[1], 3)],
            1: [(pair[5], 0)],
            2: [(pair[2], 3)],
            4: [(pair[4], 2)],
            6: [(pair[5], 1), (pair[3], 3)],
        }
    for copy in loads[1:]:
        copy.wait()
    blocks = total // WIDE

    def per_pair(p, carry):
        dq_ref[...] = jnp.zeros_like(dq_ref)

        def step(b, carry):
            for i, todo in moves.items():
                pl.when(p * blocks + b == i)(lambda todo=todo: advance(*todo))
            pair_back(p, b, total, qkv_ref, grad_ref, extra_ref, inner_ref, code_k_ref, dqkv_ref, dq_ref)
            return carry

        lax.fori_loop(0, blocks, step, 0)
        at = pl.multiple_of(p * TRIO, LANES)
        dqkv_ref[:, pl.ds(at, LANES)] = dq_ref[...].astype(bf16)
        lanes = pl.ds(pl.multiple_of(width + LANES + at, LANES), TRIO)
        store(lanes, dot_first(normed_ref[...], dqkv_ref[:, pl.ds(at, TRIO)]))
        if net is not None:
            for k in range(pairs):

                @pl.when(p == k)
                def _(k=k):
                    for piece in pair[k]:
                        piece.send(0)

        return carry

    lax.fori_loop(0, pairs, per_pair, 0)
    third = pairs * TRIO // 3
    for j in range(3):
        cols = slice(j * third, (j + 1) * third)
        back = dot_last(dqkv_ref[:, cols], weight_ref[:, cols])
        if j == 0:
            sum_ref[...] = back
        else:
            sum_ref[...] += back
        advance(*ending.get(j, ()))
    tokens.wait()
    finals = []
    for b in range(total // BLOCK):
        rows = pl.ds(b * BLOCK, BLOCK)
        unit, inv = unit_of(tokens_ref[rows, :].astype(f32))
        sum_ref[rows, :] = grad_middle_ref[rows, :] + unit_back(sum_ref[rows, :], unit, inv, gains_ref[0:1, :])
        finals.append(pltpu.make_async_copy(sum_ref.at[rows], grad_tokens_ref.at[rows], store_sem.at[b]))
        finals[-1].start()
        advance(*ending.get(3 + b, ()))
    if net is not None:
        advance((pair[5], 2), (pair[4], 3))
        advance((pair[5], 3))
        for p in feed + att:
            p.drain()
    for copy in finals:
        copy.wait()


def params(**more):
    return pltpu.CompilerParams(vmem_limit_bytes=58 << 20, **more)


def shape(*dims, kind=bf16):
    return jax.ShapeDtypeStruct(dims, kind)


def run_forward(clip, tokens, weights, gains):
    total, width = tokens.shape
    return pl.pallas_call(
        forward_kernel,
        name="layer_forward",
        out_shape=(
            shape(total, 3 * width), shape(total, width), shape(total, width),
            shape(total, width, kind=f32), shape(total, width), shape(total, width), shape(8, width, kind=f32),
        ),
        in_specs=[SM, VM, VM, VM],
        out_specs=(VM,) * 7,
        scratch_shapes=[pltpu.VMEM((total, LANES), bf16), pltpu.VMEM((total, LANES), bf16)],
        compiler_params=params(),
        cost_estimate=pl.CostEstimate(flops=12 * 10**9, bytes_accessed=20 << 20, transcendentals=0),
    )(clip, tokens, weights, gains)


def run_feed(clip, feed, out_grad, middle, gains, weights):
    total, width = feed.shape
    parts, _, both = weights.shape
    one = pl.BlockSpec((1, width, both), lambda t: (t, 0, 0))
    return pl.pallas_call(
        feed_kernel,
        name="feed_both",
        grid=(parts,),
        out_shape=(
            shape(parts, width, both), shape(total, width), shape(total, width, kind=f32), shape(8, width, kind=f32),
        ),
        in_specs=[SM, VM, VM, VM, VM, one],
        out_specs=(one, VM, VM, VM),
        scratch_shapes=[
            pltpu.VMEM((total, width), bf16), pltpu.VMEM((total, both - width), bf16),
            pltpu.VMEM((total, both - width), bf16), pltpu.VMEM((total, width), f32), pltpu.VMEM((total, width), f32),
        ],
        compiler_params=params(),
        cost_estimate=pl.CostEstimate(flops=30 * 10**9, bytes_accessed=30 << 20, transcendentals=0),
    )(clip, feed, out_grad, middle, gains, weights)


MESH = pl.DeviceIdType.MESH
ANY = pl.BlockSpec(memory_space=pl.ANY)
FACTORS = {
    (8, 4): ((("z", 4), ("y", 2)), (("x", 2), ("c", 2))),
}


class Net:
    def __init__(self, factors):
        self.factors = factors
        self.size = {n: s for axis in factors for n, s in axis}
        self.count = 1
        for s in self.size.values():
            self.count *= s

    def locate(self):
        self.place = {}
        for name, axis in zip(BOTH, self.factors):
            left = lax.axis_index(name)
            for n, s in axis[::-1]:
                self.place[n] = lax.rem(left, s)
                left = lax.div(left, s)

    def device(self, dim, value):
        out = []
        for axis in self.factors:
            index = 0
            for n, s in axis:
                index = index * s + (value if n == dim else self.place[n])
            out.append(index)
        return tuple(out)

    def names(self, order):
        axes = dict(zip(BOTH, self.factors))
        return [n for a in order for n, _ in axes[a]]

    def dims(self, order):
        return tuple(self.size[n] for n in self.names(order))

    def view(self, ref, order, lanes, **fixed):
        index = tuple(fixed.get(n, slice(None)) for n in self.names(order))
        return ref.at[index + (slice(None), pl.ds(*lanes))]

    def peers(self, dim):
        s = self.size[dim]
        return [lax.rem(self.place[dim] + o, s) for o in range(1, s)]

    def announce(self):
        barrier = pltpu.get_barrier_semaphore()
        for dim in self.size:
            for v in self.peers(dim):
                pl.semaphore_signal(barrier, inc=1, device_id=self.device(dim, v), device_id_type=MESH)

    def meet(self):
        pl.semaphore_wait(pltpu.get_barrier_semaphore(), sum(s - 1 for s in self.size.values()))


class Sems:
    def __init__(self, send, recv):
        self.send, self.recv, self.used = send, recv, 0

    def take(self):
        self.used += 1
        return self.send.at[self.used - 1], self.recv.at[self.used - 1]


def spread(net, sems, dim, source, target):
    out = []
    for v in net.peers(dim):
        send, recv = sems.take()
        out.append(
            pltpu.make_async_remote_copy(
                src_ref=source, dst_ref=target, send_sem=send, recv_sem=recv,
                device_id=net.device(dim, v), device_id_type=MESH,
            )
        )
    return out


def begin(copies):
    for copy in copies:
        copy.start()


def arrive(copies):
    for copy in copies:
        copy.wait_recv()


class Piece:
    def __init__(self, net, sems, mine, ref, order, lanes, first, second, third):
        def block(free, **other):
            fixed = {n: v for n, v in net.place.items() if n not in free}
            return net.view(ref, order, lanes, **{**fixed, **other})

        def pass_on(dim, part):
            return spread(net, sems, dim, part, part)

        self.left = False
        self.z = spread(net, sems, first, mine.at[:, pl.ds(*lanes)], block(()))
        self.one = pass_on(second, block((first,)))
        self.two = pass_on(third, block((first, second)))
        self.twins = [
            pass_on("c", block((first,))),
            sum((pass_on("c", block((first,), **{second: v})) for v in net.peers(second)), []),
            sum((pass_on("c", block((first, second), **{third: v})) for v in net.peers(third)), []),
        ]

    def start(self):
        begin(self.z)

    def leave(self):
        for copy in self.z:
            copy.wait_send()
        self.left = True

    def step_one(self):
        arrive(self.z)
        begin(self.one + self.twins[0])

    def step_two(self):
        arrive(self.one)
        begin(self.two + self.twins[1])

    def step_three(self):
        arrive(self.two)
        begin(self.twins[2])

    def ready(self):
        arrive(sum(self.twins, []))

    def drain(self):
        for copy in ([] if self.left else self.z) + self.one + self.two + sum(self.twins, []):
            copy.wait_send()


def copies_of(net):
    z, y, x, c = (net.size[n] - 1 for n in "zyxc")
    return z + y + x + c * (1 + z + y + x)


def lane_parts(width, count):
    tiles, out, at = width // LANES, [], 0
    for i in range(count):
        take = (tiles - at) // (count - i)
        out.append((at * LANES, take * LANES))
        at += take
    return out


ORDERS = (("z", "y", "x"), ("z", "x", "y"))
ORDERS_LATE = (("y", "z", "x"), ("x", "z", "y"))


def att_spans(width):
    start = width + LANES
    spans = [(width, LANES + TRIO)] + [(start + p * TRIO, TRIO) for p in range(1, width // LANES)]
    return spans + [(0, width)]


def halves(start, size):
    return [(start + at, take) for at, take in lane_parts(size, 2)]


def fused_forward_kernel(
    net,
    clip_ref, tokens_ref, w_reduce_ref, out_grad_ref, w_query_ref, w_key_ref, w_value_ref, w_output_ref, gain_ref,
    w_expand_ref,
    att_all, feed_all, qkv_hbm, mixed_hbm, extra_hbm, normed_hbm, grads_ref, result_hbm, grad_middle_hbm, sums_ref,
    gains_ref, half_0, half_1, half_2, half_3, qkv_ref, mixed_ref, extra_ref, normed_ref, result_ref, grad_middle_ref, store_sem, mine_ref, both_ref, gain_tile_ref, group_ref, output_weight_ref, grad_ref, middle_ref, feed_ref, active_ref, hidden_ref, out_ref,
    chunk_ref, stage_ref, code_q_ref, code_k_ref, send, recv, local, chunk_sem, stage_sem, *early,
):
    total, width = tokens_ref.shape
    pairs = width // LANES
    hid = w_expand_ref.shape[1]
    chunks = hid // GROUP
    ends = clip_ends(clip_ref)
    flip = BOTH[::-1]
    net.locate()
    net.announce()

    moves = [(w_output_ref, mine_ref.at[:, pl.ds(0, width)]), (gain_ref, mine_ref.at[:, pl.ds(width, LANES)])]
    for p in range(pairs):
        for j, ref in enumerate((w_query_ref, w_key_ref, w_value_ref)):
            at = width + LANES + p * TRIO + j * LANES
            moves.append((ref.at[:, pl.ds(p * LANES, LANES)], mine_ref.at[:, pl.ds(at, LANES)]))
    for k in range(chunks):
        for kind, ref in enumerate((w_expand_ref, w_reduce_ref)):
            moves.append((ref.at[:, pl.ds(k * GROUP, GROUP)], both_ref.at[:, pl.ds((2 * k + kind) * GROUP, GROUP)]))
    copies = [pltpu.make_async_copy(src, dst, local.at[i]) for i, (src, dst) in enumerate(moves)]
    used = len(copies)
    copies.append(pltpu.make_async_copy(out_grad_ref, grad_ref, local.at[used]))
    for copy in copies:
        copy.start()
    for copy in copies[:used]:
        copy.wait()
    net.meet()
    sems = Sems(send, recv)
    att = [
        [Piece(net, sems, mine_ref, att_all, BOTH, lanes, *ORDERS[i]) for i, lanes in enumerate(halves(*span))]
        for span in att_spans(width)
    ]
    feed = [
        [
            Piece(net, sems, both_ref, feed_all, flip, lanes, *(ORDERS_LATE if k >= LATE else ORDERS)[i])
            for i, lanes in enumerate(halves(2 * k * GROUP, 2 * GROUP))
        ]
        for k in range(chunks)
    ]
    folds = []
    for k in range(EARLY):
        for kind, (lanes, along) in enumerate(feed_folds(k)):

            def staged(index, kind=kind):
                at = dict(zip([n for n in net.names(flip) if n != "c"], index))
                q = at["x"] * net.size["c"] + net.place["c"]
                return stage_ref[kind, at["z"], at["y"], :, pl.ds(pl.multiple_of(q * GROUP, GROUP), GROUP)]

            bufs, early = early[:2], early[2:]
            folds.append(Fold(net, sems, grads_ref, flip, lanes, along, bufs, own=staged, steps=(0, 1)))
    own = [
        pltpu.make_async_copy(mine_ref, net.view(att_all, BOTH, (0, mine_ref.shape[1]), **net.place), local.at[0]),
        pltpu.make_async_copy(both_ref, net.view(feed_all, flip, (0, both_ref.shape[1]), **net.place), local.at[1]),
    ]
    for copy in own:
        copy.start()

    def act(*moves):
        for name, pair in moves:
            for piece in pair:
                getattr(piece, name)()

    pair, output = att[:-1], att[-1]
    act(("start", pair[0]))
    sums_ref[...] = jnp.zeros_like(sums_ref)
    copies[used].wait()
    for copy in own:
        copy.wait()

    def norm(r0):
        rows = pl.ds(r0, BLOCK)
        x = tokens_ref[rows, :].astype(f32)
        valid = valid_of(r0, BLOCK, ends)
        middle_ref[rows, :] = unit_of(x)[0]
        grad_ref[rows, :] = (grad_ref[rows, :].astype(f32) * valid).astype(bf16)
        set_row(sums_ref, 1, jnp.sum(x * x * valid, axis=0, keepdims=True))

    row_loop(total, BLOCK, norm)
    set_codes(code_q_ref, code_k_ref, ends)
    for p in range(pairs):
        act(("leave", pair[p]), ("start", pair[p + 1] if p + 1 < pairs else feed[0]), ("step_one", pair[p]))
        if p >= 2:
            act(("step_two", pair[p - 2]))
        if p >= 4:
            act(("step_three", pair[p - 4]))
    act(("ready", pair[0]))

    def fetch(lanes, target, sem):
        return pltpu.make_async_copy(net.view(att_all, BOTH, lanes), target, sem)

    def flat(value):
        return value.reshape(width, value.shape[-1])

    tile = fetch((width, LANES), gain_tile_ref, local.at[0])
    tile.start()
    fetch((width + LANES, TRIO), group_ref.at[0], local.at[1]).start()
    tile.wait()
    gains_ref[...] = flat(gain_tile_ref[...].astype(f32)).T[:8]

    def scale(r0):
        rows = pl.ds(r0, BLOCK)
        normed_ref[rows, :] = (middle_ref[rows, :] * gains_ref[0:1, :]).astype(bf16)

    row_loop(total, BLOCK, scale)
    plan = {
        0: [("step_two", pair[4]), ("step_three", pair[2]), ("ready", pair[1])],
        1: [("step_two", pair[5]), ("step_three", pair[3]), ("start", output)],
        2: [("start", feed[1]), ("step_three", pair[4]), ("ready", pair[2])],
        3: [("step_one", feed[0]), ("step_three", pair[5])],
        4: [("start", feed[2]), ("step_one", output), ("ready", pair[3])],
        6: [("step_one", feed[2]), ("step_two", output), ("step_two", feed[0]), ("ready", pair[4])],
        8: [("step_one", feed[1]), ("ready", pair[5])],
        9: [("step_three", output)],
        11: [("step_three", feed[0])],
    }
    blocks = total // WIDE

    def per_pair(p, carry):
        slot = lax.rem(p, 2)
        fetch((0, TRIO), group_ref.at[slot], local.at[1]).wait()
        project(normed_ref, pl.ds(0, total), flat(group_ref[slot]), qkv_ref, p)

        def step(b, carry):
            for i, todo in plan.items():
                pl.when(p * blocks + b == i)(lambda todo=todo: act(*todo))

            @pl.when((b == 1) & (p + 1 < pairs))
            def _():
                start = pl.multiple_of(width + LANES + (p + 1) * TRIO, LANES)
                fetch((start, TRIO), group_ref.at[1 - slot], local.at[1]).start()

            pair_forward(p, b, total, qkv_ref, mixed_ref, extra_ref, code_q_ref, code_k_ref)
            return carry

        lax.fori_loop(0, blocks, step, 0)
        return carry

    lax.fori_loop(0, pairs, per_pair, 0)
    act(("ready", output))
    fetch((0, width), output_weight_ref, local.at[1]).start()
    outs = [
        pltpu.make_async_copy(ref, target, store_sem.at[i])
        for i, (ref, target) in enumerate(
            ((qkv_ref, qkv_hbm), (mixed_ref, mixed_hbm), (normed_ref, normed_hbm), (extra_ref, extra_hbm))
        )
    ]
    for copy in outs:
        copy.start()
    fetch((0, width), output_weight_ref, local.at[1]).wait()
    middle_ref[...] = dot_plain(mixed_ref[...], flat(output_weight_ref[...]))
    act(("step_two", feed[1]))

    def second(r0):
        rows = pl.ds(r0, BLOCK)
        branch = middle_ref[rows, :]
        middle = tokens_ref[rows, :].astype(f32) + branch
        middle_ref[rows, :] = middle
        feed_ref[rows, :] = (unit_of(middle)[0] * gains_ref[1:2, :]).astype(bf16)
        set_row(sums_ref, 2, jnp.sum(branch * branch * valid_of(r0, BLOCK, ends), axis=0, keepdims=True))

    row_loop(total, BLOCK, second)
    act(("ready", feed[0]))
    feed_plan = {(0, 2): [("step_three", feed[1]), ("step_two", feed[2])], (1, 2): [("step_three", feed[2])]}

    tp = net.names(("tp",))
    quarters = list(np.ndindex(*(net.size[n] for n in tp)))
    both_kinds = range(2)

    def place(ref, quarter, kind, k):
        at = (2 * k + kind) * GROUP
        at = at if isinstance(at, int) else pl.multiple_of(at, GROUP)
        return ref.at[quarter + (slice(None),) * (len(ref.shape) - len(quarter) - 1) + (pl.ds(at, GROUP),)]

    def part(ref, q):
        return ref.at[(slice(None),) * (len(ref.shape) - 1) + (pl.ds(q * GROUP, GROUP),)]

    def chunk_copies(k, slot):
        return [
            pltpu.make_async_copy(
                place(feed_all, quarter, kind, k), part(chunk_ref.at[slot, kind], q), chunk_sem.at[slot, kind, q]
            )
            for kind in both_kinds
            for q, quarter in enumerate(quarters)
        ]

    def stage_copies(k):
        return [
            pltpu.make_async_copy(part(stage_ref.at[kind], q), place(grads_ref, quarter, kind, k), stage_sem.at[kind, q])
            for kind in both_kinds
            for q, quarter in enumerate(quarters)
        ]

    for copy in chunk_copies(0, 0):
        copy.start()
    out_ref[...] = jnp.zeros_like(out_ref)
    grad_middle_ref[...] = jnp.zeros_like(grad_middle_ref)

    def chunk(k, carry):
        slot = lax.rem(k, 2)
        for copy in chunk_copies(k, slot):
            copy.wait()

        def weights(kind):
            return chunk_ref[slot, kind].reshape(width, len(quarters) * GROUP)

        for q in range(len(quarters)):
            for (a, b), todo in feed_plan.items():
                if q == b:
                    pl.when(k == a)(lambda todo=todo: act(*todo))
            if q == 1:

                @pl.when(k > 0)
                def _():
                    for copy in stage_copies(k - 1):
                        copy.wait()

                for j in range(EARLY):

                    @pl.when(k == j + 1)
                    def _(j=j):
                        for p in folds[2 * j : 2 * j + 2]:
                            p.send(0)

            cols = slice(q * GROUP, (q + 1) * GROUP)
            hidden = dot_plain(feed_ref[...], weights(0)[:, cols])
            grad_active = dot_plain(grad_ref[...], weights(1)[:, cols])
            share = 0.5 * (1.0 + lax.erf(hidden * 0.7071067811865476))
            active_ref[:, cols] = (hidden * share).astype(bf16)
            slope = share + hidden * (jnp.exp(-0.5 * hidden * hidden) * 0.3989422804014327)
            hidden_ref[:, cols] = (grad_active * slope).astype(bf16)
        for j in range(chunks - 1):

            @pl.when(k == j)
            def _(j=j):
                act(("ready", feed[j + 1]))
                for copy in chunk_copies(j + 1, (j + 1) % 2):
                    copy.start()

        for j in range(EARLY):

            @pl.when(k == j + 1)
            def _(j=j):
                for p in folds[2 * j : 2 * j + 2]:
                    p.add(0)
                    p.send(1)

        out_ref[...] += dot_last(active_ref[...], weights(1))
        grad_middle_ref[...] += dot_last(hidden_ref[...], weights(0))
        for kind, (left, right) in enumerate(((feed_ref, hidden_ref), (grad_ref, active_ref))):
            stage_ref[kind] = dot_first(left[...], right[...]).reshape(stage_ref.shape[1:]).astype(bf16)
        for copy in stage_copies(k):
            copy.start()
        return carry

    lax.fori_loop(0, chunks, chunk, 0)

    for i in range(total // BLOCK):
        rows = pl.ds(i * BLOCK, BLOCK)
        middle, out, back = middle_ref[rows, :], out_ref[rows, :], grad_middle_ref[rows, :]
        result_ref[rows, :] = (middle + out).astype(bf16)
        unit, inv = unit_of(middle)
        grad_middle_ref[rows, :] = grad_ref[rows, :].astype(f32) + unit_back(back, unit, inv, gains_ref[1:2, :])
        set_row(sums_ref, 3, jnp.sum(out * out * valid_of(i * BLOCK, BLOCK, ends), axis=0, keepdims=True))
        set_row(sums_ref, 0, jnp.sum(back * unit, axis=0, keepdims=True))
        for j, (ref, target) in enumerate(((result_ref, result_hbm), (grad_middle_ref, grad_middle_hbm))):
            outs.append(pltpu.make_async_copy(ref.at[rows], target.at[rows], store_sem.at[4 + 2 * i + j]))
            outs[-1].start()
    for i, (p, target) in enumerate(zip(folds, (half_0, half_1, half_2, half_3))):
        p.add(1)
        outs.append(pltpu.make_async_copy(p.bufs[1].at[pl.ds(0, 1)], target, local.at[i]))
        outs[-1].start()
    for copy in outs:
        copy.wait()
    for copy in stage_copies(chunks - 1):
        copy.wait()
    for p in folds:
        p.drain()
    for pair in att + feed:
        for piece in pair:
            piece.drain()


def run_fused_forward(net, clip, tokens, out_grad, weights, gain_tile, w_expand, w_reduce):
    total, width = tokens.shape
    rows, rows_feed = width // net.count, w_expand.shape[0]
    lanes, hid = 4 * width + LANES, w_expand.shape[1]
    flip = BOTH[::-1]
    ff = (*net.dims(flip), rows_feed, 2 * hid)
    wide = GROUP * int(np.prod(net.dims(("tp",))))
    inner = tuple(net.size[n] for n in net.names(("dp",))) + (rows_feed, wide)
    count = 2 * (len(att_spans(width)) + hid // GROUP) * copies_of(net) + 4 * EARLY * max(net.size.values())
    dma = pltpu.SemaphoreType.DMA
    early, halves_out = [], []
    for k in range(EARLY):
        for fold in feed_folds(k):
            shapes = Fold.shapes(net, flip, rows_feed, *fold)[:2]
            early += [pltpu.VMEM(dims, bf16) for dims in shapes]
            halves_out.append(shape(1, *shapes[1][1:]))
    return pl.pallas_call(
        lambda *refs: fused_forward_kernel(net, *refs),
        name="layer_forward_feed",
        out_shape=(
            shape(*net.dims(BOTH), rows, lanes), shape(*ff), shape(total, 3 * width), shape(total, width),
            shape(total, width), shape(total, width), shape(*ff), shape(total, width),
            shape(total, width, kind=f32), shape(8, width, kind=f32), shape(8, width, kind=f32), *halves_out,
        ),
        in_specs=[SM, VM] + [ANY] * 8,
        out_specs=(ANY, ANY, ANY, ANY, ANY, ANY, ANY, ANY, ANY, VM, VM) + (ANY,) * len(halves_out),
        scratch_shapes=[
            pltpu.VMEM((total, 3 * width), bf16), pltpu.VMEM((total, width), bf16), pltpu.VMEM((total, width), bf16),
            pltpu.VMEM((total, width), bf16), pltpu.VMEM((total, width), bf16), pltpu.VMEM((total, width), f32), dma((4 + 2 * total // BLOCK,)),
            pltpu.VMEM((rows, lanes), bf16), pltpu.VMEM((rows_feed, 2 * hid), bf16), pltpu.VMEM((*net.dims(BOTH), rows, LANES), bf16),
            pltpu.VMEM((2, *net.dims(BOTH), rows, TRIO), bf16), pltpu.VMEM((*net.dims(BOTH), rows, width), bf16),
            pltpu.VMEM((total, width), bf16),
            pltpu.VMEM((total, width), f32), pltpu.VMEM((total, width), bf16), pltpu.VMEM((total, wide), bf16),
            pltpu.VMEM((total, wide), bf16), pltpu.VMEM((total, width), f32), pltpu.VMEM((2, 2, *inner), bf16),
            pltpu.VMEM((2, *inner), bf16), pltpu.VMEM((total, LANES), bf16), pltpu.VMEM((total, LANES), bf16),
            dma((count,)), dma((count,)),
            dma((4 + 3 * (width // LANES) + 2 * hid // GROUP,)), dma((2, 2, wide // GROUP)), dma((2, wide // GROUP)),
            *early,
        ],
        compiler_params=params(collective_id=1, has_side_effects=True),
    )(clip, tokens, w_reduce, out_grad, *weights, gain_tile, w_expand)


def store_at(ref, index, lanes, value):
    ref[tuple(index) + (slice(None), lanes)] = value


def each(dims, body, index=()):
    count = 1
    for size in dims:
        count *= size
    if count <= 4:
        for tail in np.ndindex(*dims):
            body(index + tail)
    else:

        def step(i, carry):
            each(dims[1:], body, index + (i,))
            return carry

        lax.fori_loop(0, dims[0], step, 0)


class Fold:
    def __init__(self, net, sems, ref, order, lanes, along, bufs, out=None, own=None, steps=(0, 1, 2, 3)):
        self.net, self.lanes, self.along, self.bufs, self.out, self.steps = net, lanes, along, bufs, out, steps
        names = net.names(order)
        self.names = [[n for n in names if n not in along[:k]] for k in range(5)]
        self.ref, self.own = ref, own
        self.copies = {}
        for k in steps:
            dim = along[k]
            source, cols = (ref, lanes) if k == 0 else (bufs[k - 1].at[0], (0, lanes[1]))
            self.copies[k] = []
            for o, v in enumerate(net.peers(dim)):
                index = tuple(v if n == dim else slice(None) for n in self.names[k])
                s, r = sems.take()
                self.copies[k].append(
                    pltpu.make_async_remote_copy(
                        src_ref=source.at[index + (slice(None), pl.ds(*cols))], dst_ref=bufs[k].at[o],
                        send_sem=s, recv_sem=r, device_id=net.device(dim, v), device_id_type=MESH,
                    )
                )

    @staticmethod
    def shapes(net, order, rows, lanes, along):
        names, out = net.names(order), []
        for k, dim in enumerate(along):
            left = [net.size[n] for n in names if n not in along[: k + 1]]
            out.append((net.size[dim] - 1, *left, rows, lanes[1]))
        return out

    def send(self, k):
        begin(self.copies[k])

    def add(self, k):
        arrive(self.copies[k])
        dim, buf, cols = self.along[k], self.bufs[k], slice(0, self.lanes[1])
        here = self.net.place[dim]
        wide = pl.ds(*self.lanes)

        def one(index):
            at = dict(zip(self.names[k + 1], index))
            full = tuple(at.get(n, here) for n in self.names[k])
            if k > 0:
                total = self.bufs[k - 1][(0,) + full + (slice(None), cols)].astype(f32)
            elif self.own is not None:
                total = self.own(index).astype(f32)
            else:
                total = self.ref[full + (slice(None), wide)].astype(f32)
            terms = [total] + [buf[(o,) + index].astype(f32) for o in range(self.net.size[dim] - 1)]
            if len(terms) > 2:
                size = len(terms)
                total = 0.0
                for v in range(size):
                    back = lax.rem(here - v + size, size)
                    term = terms[0]
                    for o in range(1, size):
                        term = jnp.where(back == o, terms[o], term)
                    total = total + term
            else:
                total = terms[0] + terms[1]
            if k == 3:
                self.out[:, wide] = total
            else:
                buf[(0,) + index] = total.astype(bf16)

        each([self.net.size[n] for n in self.names[k + 1]], one)

    def drain(self):
        for copies in self.copies.values():
            for copy in copies:
                copy.wait_send()


ALONG = (("c", "x", "y", "z"), ("c", "y", "x", "z"))


def feed_folds(k):
    return [((2 * GROUP * k + GROUP * i, GROUP), ALONG[i]) for i in range(2)]


EARLY = 2
LATE = 2


def att_folds(width):
    out = []
    spans = [(0, width + LANES)] + [(width + LANES + p * TRIO, TRIO) for p in range(width // LANES)]
    for start, size in spans:
        for i, (at, take) in enumerate(lane_parts(size, 2)):
            out.append(((start + at, take), ALONG[i % 2]))
    return out


def run_backward(net, clip, grad_middle, mixed, qkv, extra, normed, tokens, weights, gains, *more_args):
    total, width = tokens.shape
    lanes = weights.shape[1]
    scratch = [
        pltpu.VMEM((total, width), bf16), pltpu.VMEM((total, width), bf16), pltpu.VMEM((total, 3 * width), bf16),
        pltpu.VMEM((total, LANES), f32), pltpu.VMEM((total, width), bf16), pltpu.VMEM((total, LANES), bf16),
    ]
    operands = [clip, grad_middle, mixed, qkv, extra, normed, tokens, weights, gains]
    in_specs = [SM] + [ANY] * 7 + [VM]
    out_shape = (shape(width, lanes), shape(total, width, kind=f32))
    more = {}
    if net is not None:
        feed_grads = more_args[1]
        rows, rows_feed = width // net.count, feed_grads.shape[-2]
        hid = feed_grads.shape[-1] // 2
        flip = BOTH[::-1]
        operands += more_args
        in_specs += [VM, ANY] + [ANY] * (2 * EARLY)
        out_shape = (shape(rows, lanes, kind=f32), shape(rows_feed, 2 * hid, kind=f32), out_shape[1])
        scratch.append(pltpu.VMEM((*net.dims(BOTH), rows, lanes), bf16))
        kept = tuple(net.size[n] for n in net.names(flip) if n != "c")
        scratch.append(pltpu.VMEM((*kept, rows_feed, 2 * hid - 2 * GROUP * EARLY), bf16))
        bufs = []
        for k in range(hid // GROUP):
            for f in feed_folds(k):
                bufs += Fold.shapes(net, flip, rows_feed, *f)[2 if k < EARLY else 0 :]
        for f in att_folds(width):
            bufs += Fold.shapes(net, BOTH, rows, *f)
        count = sum(dims[0] for dims in bufs)
        scratch += [pltpu.SemaphoreType.DMA((count,)), pltpu.SemaphoreType.DMA((count,)), pltpu.SemaphoreType.DMA]
        scratch += [pltpu.VMEM(half.shape, bf16) for half in more_args[2:]]
        scratch += [pltpu.VMEM(dims, bf16) for dims in bufs]
        more = dict(collective_id=2, has_side_effects=True)
    scratch += [
        pltpu.VMEM((total, width), f32), pltpu.VMEM((total, width), bf16),
        pltpu.VMEM((total, 3 * width), bf16), pltpu.VMEM((total, width), bf16), pltpu.VMEM((total, width), bf16),
        pltpu.VMEM((width, width), bf16), pltpu.VMEM((width, 3 * width), bf16), pltpu.VMEM((total, width), f32),
        pltpu.SemaphoreType.DMA((8 + 2 * EARLY,)), pltpu.SemaphoreType.DMA((total // BLOCK,)),
    ]
    return pl.pallas_call(
        lambda *refs: backward_kernel(net, *refs),
        name="layer_backward",
        out_shape=out_shape,
        in_specs=in_specs,
        out_specs=(VM,) * (len(out_shape) - 1) + (ANY,),
        scratch_shapes=scratch,
        compiler_params=params(**more),
        cost_estimate=pl.CostEstimate(flops=22 * 10**9, bytes_accessed=30 << 20, transcendentals=0),
    )(*operands)


def unpack_kernel(
    shard_ref, feed_ref, w_query_ref, w_key_ref, w_value_ref, gain_ref, result_in, grad_in,
    query_ref, key_ref, value_ref, output_ref, expand_ref, reduce_ref, gain_one_ref, gain_two_ref, means_ref,
    result_out, grad_out, result_ref, grad_ref, sem,
):
    width = output_ref.shape[1]
    parts = [
        (source.at[pl.ds(r0, BLOCK)], held.at[pl.ds(r0, BLOCK)], target.at[pl.ds(r0, BLOCK)])
        for r0 in range(0, result_ref.shape[0], BLOCK)
        for source, held, target in ((result_in, result_ref, result_out), (grad_in, grad_ref, grad_out))
    ]
    loads = [pltpu.make_async_copy(source, held, sem.at[i]) for i, (source, held, _) in enumerate(parts)]
    copies = [pltpu.make_async_copy(held, target, sem.at[i]) for i, (_, held, target) in enumerate(parts)]
    begin(loads)
    output_ref[...] = shard_ref[:, :width]
    for k in range(expand_ref.shape[1] // GROUP):
        cols = slice(k * GROUP, (k + 1) * GROUP)
        expand_ref[:, cols] = feed_ref[:, 2 * k * GROUP : (2 * k + 1) * GROUP]
        reduce_ref[:, cols] = feed_ref[:, (2 * k + 1) * GROUP : (2 * k + 2) * GROUP]
    gain = 0.0
    owned = (w_query_ref, w_key_ref, w_value_ref)
    for j, (out, weight) in enumerate(zip((query_ref, key_ref, value_ref), owned)):
        for p in range(width // LANES):
            at = width + LANES + p * TRIO + j * LANES
            out[:, p * LANES : (p + 1) * LANES] = shard_ref[:, at : at + LANES]
        gain = gain + jnp.sum(weight[...].astype(f32) * out[...], axis=1, keepdims=True)
    gain = gain / gain_ref[:, :1].astype(f32)
    lane = lax.broadcasted_iota(jnp.int32, (1, LANES), 1)
    tile = shard_ref[:, width : width + LANES]
    means = jnp.sqrt(tile / (tile[:, 4:5] * width))
    tile = jnp.where(lane == 5, gain, jnp.where(lane == 0, tile, means))
    tile = jnp.concatenate([tile, jnp.zeros((LANES - tile.shape[0], LANES), f32)], axis=0)
    rows = tile.T
    count = gain_one_ref.shape[0]
    gain_one_ref[...] = rows[5, :count]
    gain_two_ref[...] = rows[0, :count]
    lane = lax.broadcasted_iota(jnp.int32, (1, LANES), 1)
    means_ref[...] = jnp.where(lane == 0, rows[1:2], jnp.where(lane == 1, rows[2:3], rows[3:4]))[0, :3]
    for load, copy in zip(loads, copies):
        load.wait()
        copy.start()
    for copy in copies:
        copy.wait()


def run_unpack(shard, shard_feed, weights, gain_tile, result, grad_tokens):
    rows, width = weights[0].shape
    rows_feed, both = shard_feed.shape
    return pl.pallas_call(
        unpack_kernel,
        name="unpack_outputs",
        out_shape=(
            *(shape(rows, width, kind=f32) for _ in range(4)), shape(rows_feed, both // 2, kind=f32),
            shape(rows_feed, both // 2, kind=f32), shape(rows, kind=f32), shape(rows, kind=f32), shape(3, kind=f32),
            shape(*result.shape), shape(*grad_tokens.shape, kind=f32),
        ),
        in_specs=[VM] * 6 + [ANY] * 2,
        out_specs=(VM,) * 9 + (ANY,) * 2,
        scratch_shapes=[
            pltpu.VMEM(result.shape, bf16), pltpu.VMEM(grad_tokens.shape, f32),
            pltpu.SemaphoreType.DMA((2 * result.shape[0] // BLOCK,)),
        ],
        compiler_params=params(),
    )(shard, shard_feed, *weights, gain_tile, result, grad_tokens)


def on_device(
    net,
    tokens, clip_lengths, out_grad, w_query, w_key, w_value, w_output, gain_attention, gain_feed, w_expand, w_reduce,
):
    _, total, width = tokens.shape
    rows = tokens.reshape(total, width)
    out_grad = out_grad.reshape(total, width)
    lane = lax.broadcasted_iota(jnp.int32, (1, LANES), 1)
    gain_tile = jnp.where(lane == 0, gain_attention[:, None], jnp.where(lane == 1, gain_feed[:, None], 0))
    hid = w_expand.shape[1]
    if net is not None:
        weights, _, qkv, mixed, extra, normed, feed_grads, result, grad_middle, sums, gains, *early = run_fused_forward(
            net, clip_lengths, rows, out_grad, (w_query, w_key, w_value, w_output), gain_tile, w_expand, w_reduce.T
        )
        weights = weights.reshape(width, -1)
        shard, shard_feed, grad_tokens = run_backward(
            net, clip_lengths, grad_middle, mixed, qkv, extra, normed, rows, weights, gains, sums, feed_grads, *early
        )
        query, key, value, output, expand, reduce, gain_one, gain_two, means, result, grad_tokens = run_unpack(
            shard, shard_feed, (w_query, w_key, w_value), gain_tile, result, grad_tokens
        )
        reduce = reduce.T
    else:
        mine = [w_output, gain_tile]
        for p in range(width // LANES):
            mine += [w[:, p * LANES : (p + 1) * LANES] for w in (w_query, w_key, w_value)]
        weights = lax.all_gather(jnp.concatenate(mine, axis=1), BOTH, axis=0, tiled=True)
        both = jnp.concatenate([w_expand, w_reduce.T], axis=1)
        feed_weights = lax.all_gather(both, BOTH[::-1], axis=0, tiled=True).reshape(-1, width, 2 * hid)
        gains = jnp.pad(weights[:, width : width + 2].T.astype(f32), ((0, 6), (0, 0)))
        qkv, mixed, extra, middle, feed, normed, sums_one = run_forward(clip_lengths, rows, weights, gains)
        feed_grads, result, grad_middle, sums_two = run_feed(
            clip_lengths, feed, out_grad, middle, gains, feed_weights
        )
        count = jnp.sum(clip_lengths[:, : SLOTS - 1]).astype(f32)
        squares = jnp.stack([jnp.sum(sums_one[0]), jnp.sum(sums_one[1]), jnp.sum(sums_two[0]), count])
        grads, grad_tokens = run_backward(
            None, clip_lengths, grad_middle, mixed, qkv, extra, normed, rows, weights, gains
        )
        shard = lax.psum_scatter(grads, BOTH, scatter_dimension=0, tiled=True).astype(f32)
        shard_feed = lax.psum_scatter(
            feed_grads.reshape(-1, 2 * hid), BOTH[::-1], scatter_dimension=0, tiled=True
        ).astype(f32)
        stats = lax.psum(squares, BOTH)
        gain_two = lax.psum_scatter(sums_two[1], BOTH, scatter_dimension=0, tiled=True)
        means = jnp.sqrt(stats[:3] / (stats[3] * width))
        parts = shard[:, width + LANES :].reshape(-1, width // LANES, 3, LANES)
        query, key, value = (parts[:, :, j].reshape(-1, width) for j in range(3))
        pairs = ((w_query, query), (w_key, key), (w_value, value))
        gain_one = sum(jnp.sum(w.astype(f32) * g, axis=1) for w, g in pairs) / gain_attention.astype(f32)
        output, expand, reduce = shard[:, :width], shard_feed[:, :hid], shard_feed[:, hid:].T
    return (
        result.reshape(1, total, width),
        grad_tokens.reshape(1, total, width),
        query,
        key,
        value,
        output,
        gain_one,
        gain_two,
        expand,
        reduce,
        means,
    )


def solution(mesh):
    row, flat = P(BOTH, None), P(BOTH)
    whole = P(BOTH, None, None)
    in_specs = (whole, row, whole, row, row, row, row, flat, flat, P("dp", "tp"), P("tp", "dp"))
    out_specs = (whole, whole, row, row, row, row, flat, flat, P("dp", "tp"), P("tp", "dp"), P())
    factors = FACTORS.get((mesh.shape["dp"], mesh.shape["tp"]))
    net = Net(factors) if factors else None
    return jax.shard_map(
        lambda *args: on_device(net, *args), mesh=mesh, in_specs=in_specs, out_specs=out_specs, check_vma=False
    )
```

```python
import jax
import jax.numpy as jnp
import numpy as np
from jax import lax
from jax.experimental import pallas as pl
from jax.experimental.pallas import tpu as pltpu
from jax.sharding import PartitionSpec as P

HEADS = 12
HEAD_DIM = 64
SLOTS = 4
LANES = 128
BLOCK = 256
WIDE = 512
MAXCLIP = 384
GROUP = 256
TRIO = 3 * LANES
NEG = -1e30
LOG2E = 1.4426950408889634
LN2 = 0.6931471805599453
f32 = jnp.float32
bf16 = jnp.bfloat16
BOTH = ("dp", "tp")
VM = pl.BlockSpec(memory_space=pltpu.VMEM)
SM = pl.BlockSpec(memory_space=pltpu.SMEM)


def dot_plain(left, right):
    return jnp.dot(left, right, preferred_element_type=f32)


def dot_first(left, right):
    return lax.dot_general(left, right, (((0,), (0,)), ((), ())), preferred_element_type=f32)


def dot_last(left, right):
    return lax.dot_general(left, right, (((1,), (1,)), ((), ())), preferred_element_type=f32)


def unit_of(rows):
    centred = rows - jnp.mean(rows, axis=-1, keepdims=True)
    inv = lax.rsqrt(jnp.mean(centred * centred, axis=-1, keepdims=True) + 1e-06)
    return centred * inv, inv


def unit_back(grad, unit, inv, gain):
    scaled = grad * gain
    inner = (
        scaled
        - jnp.mean(scaled, axis=-1, keepdims=True)
        - unit * jnp.mean(scaled * unit, axis=-1, keepdims=True)
    )
    return inv * inner


def clip_ends(clip_ref):
    ends, total = [], jnp.int32(0)
    for j in range(SLOTS - 1):
        total = total + clip_ref[0, j]
        ends.append(total)
    return ends


def segment_of(position, ends):
    return sum((position >= e).astype(jnp.int32) for e in ends)


def valid_of(start, count, ends):
    position = start + lax.broadcasted_iota(jnp.int32, (count, 1), 0)
    return (position < ends[-1]).astype(f32)


def row_loop(total, size, body):
    def step(i, carry):
        body(pl.multiple_of(i * size, size))
        return carry

    lax.fori_loop(0, total // size, step, 0)


def head_masks(scale):
    lane = lax.broadcasted_iota(jnp.int32, (1, LANES), 1)
    low = lane < HEAD_DIM
    return lane, low, (jnp.where(low, scale, 0.0).astype(bf16), jnp.where(low, 0.0, scale).astype(bf16))


def lane_index():
    lane = lax.broadcasted_iota(jnp.int32, (1, LANES), 1)
    return lane, lax.rem(lane, HEAD_DIM)


def split_three(value):
    high = value.astype(bf16)
    rest = value - high.astype(f32)
    middle = rest.astype(bf16)
    return high, middle, (rest - middle.astype(f32)).astype(bf16)


def in_lanes(at, first, terms, other):
    out = other
    for i, term in enumerate(terms):
        out = jnp.where(at == first + i, term.astype(f32), out)
    return out


def set_codes(query_ref, key_ref, ends):
    _, at = lane_index()

    def block(r0):
        rows = pl.ds(r0, BLOCK)
        seg = segment_of(r0 + lax.broadcasted_iota(jnp.int32, (BLOCK, 1), 0), ends)
        own = at == seg
        if query_ref is not None:
            query_ref[rows, :] = jnp.where(own, NEG, 0.0).astype(bf16)
        key_ref[rows, :] = jnp.where((at < SLOTS + 3) & jnp.logical_not(own), 1.0, 0.0).astype(bf16)

    row_loop(key_ref.shape[0], BLOCK, block)


def inner_codes(grad_ref, mixed_ref, out_ref):
    total, width = mixed_ref.shape
    _, at = lane_index()
    _, low, _ = head_masks(1.0)

    def block(r0):
        rows = pl.ds(r0, LANES)
        for p in range(width // LANES):
            cols = slice(p * LANES, (p + 1) * LANES)
            both = grad_ref[rows, cols].astype(f32) * mixed_ref[rows, cols].astype(f32)
            sums = (
                jnp.sum(jnp.where(low, both, 0.0), axis=1, keepdims=True),
                jnp.sum(jnp.where(low, 0.0, both), axis=1, keepdims=True),
            )
            first, second = (in_lanes(at, 0, split_three(-x), 0.0) for x in sums)
            out_ref[rows, cols] = jnp.where(low, second, first).astype(bf16)

    row_loop(total, LANES, block)


def set_row(ref, row, value):
    at = lax.broadcasted_iota(jnp.int32, ref.shape, 0) == row
    ref[...] += jnp.where(at, value, 0.0)


def forward_kernel(
    clip_ref, tokens_ref, weights_ref, gains_ref,
    qkv_ref, mixed_ref, extra_ref, middle_ref, feed_ref, normed_ref, sums_ref,
    code_q_ref, code_k_ref,
):
    total, width = tokens_ref.shape
    ends = clip_ends(clip_ref)
    sums_ref[...] = jnp.zeros_like(sums_ref)

    def norm(r0):
        rows = pl.ds(r0, BLOCK)
        x = tokens_ref[rows, :].astype(f32)
        normed_ref[rows, :] = (unit_of(x)[0] * gains_ref[0:1, :]).astype(bf16)
        set_row(sums_ref, 0, jnp.sum(x * x * valid_of(r0, BLOCK, ends), axis=0, keepdims=True))

    row_loop(total, BLOCK, norm)
    set_codes(code_q_ref, code_k_ref, ends)
    for p in range(width // LANES):
        weight = weights_ref[:, width + LANES + p * TRIO : width + LANES + (p + 1) * TRIO]
        project(normed_ref, pl.ds(0, total), weight, qkv_ref, p)

    def pair_block(i, carry):
        blocks = total // WIDE
        pair_forward(
            lax.div(i, blocks), lax.rem(i, blocks), total, qkv_ref, mixed_ref, extra_ref, code_q_ref, code_k_ref
        )
        return carry

    lax.fori_loop(0, width // LANES * (total // WIDE), pair_block, 0)
    middle_ref[...] = dot_plain(mixed_ref[...], weights_ref[:, :width])

    def second(r0):
        rows = pl.ds(r0, BLOCK)
        branch = middle_ref[rows, :]
        middle = tokens_ref[rows, :].astype(f32) + branch
        middle_ref[rows, :] = middle
        feed_ref[rows, :] = (unit_of(middle)[0] * gains_ref[1:2, :]).astype(bf16)
        set_row(sums_ref, 1, jnp.sum(branch * branch * valid_of(r0, BLOCK, ends), axis=0, keepdims=True))

    row_loop(total, BLOCK, second)


def feed_kernel(
    clip_ref, feed_ref, out_grad_ref, middle_ref, gains_ref, weights_ref,
    grads_ref, result_ref, grad_middle_ref, sums_ref,
    grad_ref, active_ref, hidden_ref, out_ref, back_ref,
):
    total, width = feed_ref.shape
    ends = clip_ends(clip_ref)
    step = pl.program_id(0)

    @pl.when(step == 0)
    def _():
        def mask(r0):
            rows = pl.ds(r0, BLOCK)
            grad_ref[rows, :] = (out_grad_ref[rows, :].astype(f32) * valid_of(r0, BLOCK, ends)).astype(bf16)

        row_loop(total, BLOCK, mask)
        out_ref[...] = jnp.zeros_like(out_ref)
        back_ref[...] = jnp.zeros_like(back_ref)
        sums_ref[...] = jnp.zeros_like(sums_ref)

    hid = weights_ref.shape[2] - width
    part = 256
    for n in range(hid // part):
        cols = slice(n * part, (n + 1) * part)
        late = slice(hid + n * part, hid + (n + 1) * part)
        hidden = dot_plain(feed_ref[...], weights_ref[0, :, cols])
        grad_active = dot_plain(grad_ref[...], weights_ref[0, :, late])
        share = 0.5 * (1.0 + lax.erf(hidden * 0.7071067811865476))
        active_ref[:, cols] = (hidden * share).astype(bf16)
        slope = share + hidden * (jnp.exp(-0.5 * hidden * hidden) * 0.3989422804014327)
        hidden_ref[:, cols] = (grad_active * slope).astype(bf16)
    expand, reduce = weights_ref[0, :, :hid], weights_ref[0, :, hid:]
    out_ref[...] += dot_last(active_ref[...], reduce)
    back_ref[...] += dot_last(hidden_ref[...], expand)
    grads_ref[0, :, :hid] = dot_first(feed_ref[...], hidden_ref[...]).astype(bf16)
    grads_ref[0, :, hid:] = dot_first(grad_ref[...], active_ref[...]).astype(bf16)

    @pl.when(step == pl.num_programs(0) - 1)
    def _():
        def finish(r0):
            rows = pl.ds(r0, BLOCK)
            valid = valid_of(r0, BLOCK, ends)
            middle, out, back = middle_ref[rows, :], out_ref[rows, :], back_ref[rows, :]
            result_ref[rows, :] = (middle + out).astype(bf16)
            unit, inv = unit_of(middle)
            grad_middle_ref[rows, :] = (
                grad_ref[rows, :].astype(f32) + unit_back(back, unit, inv, gains_ref[1:2, :])
            )
            set_row(sums_ref, 0, jnp.sum(out * out * valid, axis=0, keepdims=True))
            set_row(sums_ref, 1, jnp.sum(back * unit, axis=0, keepdims=True))

        row_loop(total, BLOCK, finish)


def static_windows(total):
    spans = []
    for r0 in range(0, total, WIDE):
        low = max(0, r0 - MAXCLIP + 1) // LANES * LANES
        high = min(total, -(-(r0 + WIDE + MAXCLIP - 1) // LANES) * LANES)
        spans.append((low, high))
    width = max(high - low for low, high in spans)
    return [min(low, total - width) for low, _ in spans], width


def start_of(starts, block):
    at = jnp.int32(starts[0])
    for i, s in enumerate(starts):
        at = jnp.where(block == i, s, at)
    return pl.multiple_of(at, LANES)


def pair_parts(p, block, total):
    starts, cols = static_windows(total)
    rows = pl.ds(pl.multiple_of(block * WIDE, WIDE), WIDE)
    win = pl.ds(start_of(starts, block), cols)
    return rows, win, [pl.ds(pl.multiple_of(p * TRIO + j * LANES, LANES), LANES) for j in range(3)]


def with_codes(value, code, plain):
    return value * plain[0] + code * plain[1], value * plain[1] + code * plain[0]


def pair_forward(p, block, total, qkv_ref, mixed_ref, extra_ref, code_q_ref, code_k_ref):
    _, at = lane_index()
    _, low, plain = head_masks(1.0)
    rows, win, (at_q, at_k, at_v) = pair_parts(p, block, total)
    query, keys, values = qkv_ref[rows, at_q], qkv_ref[win, at_k], qkv_ref[win, at_v]
    values = jnp.concatenate([values, jnp.ones_like(values)], axis=1)
    code = code_q_ref[rows, :]
    queries, keys = with_codes(query, code, plain), with_codes(keys, code_k_ref[win, :], plain)
    outs, extras = [], []
    for h in range(2):
        scores = dot_last(queries[h], keys[h])
        top = jnp.max(scores, axis=1, keepdims=True)
        mixed = dot_plain(jnp.exp2(scores - top).astype(bf16), values)
        row_sum = mixed[:, LANES:]
        outs.append(mixed[:, :LANES] / row_sum)
        extras.append(in_lanes(at, SLOTS, split_three(-(top + LOG2E * jnp.log(row_sum))), code.astype(f32)))
    lanes = pl.ds(pl.multiple_of(p * LANES, LANES), LANES)
    mixed_ref[rows, lanes] = jnp.where(low, outs[0], outs[1]).astype(bf16)
    extra_ref[rows, lanes] = jnp.where(low, extras[1], extras[0]).astype(bf16)


def pair_back(p, block, total, qkv_ref, grad_ref, extra_ref, inner_ref, code_k_ref, dqkv_ref, dq_ref):
    _, at = lane_index()
    _, low, scaled = head_masks(0.125)
    _, _, plain = head_masks(1.0)
    rows, win, (at_q, at_k, at_v) = pair_parts(p, block, total)
    lanes = pl.ds(pl.multiple_of(p * LANES, LANES), LANES)
    keys, values, query, grad = qkv_ref[rows, at_k], qkv_ref[rows, at_v], qkv_ref[win, at_q], grad_ref[win, lanes]
    ones = jnp.where(at < 3, 1.0, 0.0).astype(bf16)
    key_codes, query_codes = with_codes(keys, code_k_ref[rows, :], plain), with_codes(query, extra_ref[win, lanes], plain)
    value_codes, grad_codes = with_codes(values, ones, plain), with_codes(grad, inner_ref[win, lanes], plain)
    dk, dv, dq = [], [], 0.0
    for h in range(2):
        probs = jnp.exp2(dot_last(key_codes[h], query_codes[h]))
        dv.append(dot_plain(probs.astype(bf16), grad))
        ds = (probs * dot_last(value_codes[h], grad_codes[h])).astype(bf16)
        dk.append(dot_plain(ds, query))
        dq = dq + dot_first(ds, keys * scaled[h])
    dq_ref[win, :] += dq
    dqkv_ref[rows, at_k] = (jnp.where(low, dk[0], dk[1]) * LN2).astype(bf16)
    dqkv_ref[rows, at_v] = jnp.where(low, dv[0], dv[1]).astype(bf16)


def project(normed_ref, rows, weight, qkv_ref, p):
    lane = lax.broadcasted_iota(jnp.int32, (1, TRIO), 1)
    scale = jnp.where(lane < LANES, 0.125 * LOG2E, 1.0)
    at = pl.multiple_of(p * TRIO, LANES)
    qkv_ref[rows, pl.ds(at, TRIO)] = (dot_plain(normed_ref[rows, :], weight) * scale).astype(bf16)


def backward_kernel(
    net,
    clip_ref, grad_middle_hbm, mixed_hbm, qkv_hbm, extra_hbm, normed_hbm, tokens_hbm, weights_hbm, gains_ref,
    *refs,
):
    total, width = mixed_hbm.shape
    ends = clip_ends(clip_ref)
    refs, load_sem, store_sem = refs[:-2], *refs[-2:]
    refs, (qkv_ref, extra_ref, normed_ref, output_weight_ref, weight_ref, sum_ref) = refs[:-6], refs[-6:]
    refs, (grad_middle_ref, mixed_ref) = refs[:-2], refs[-2:]
    if net is not None:
        net.locate()
        net.announce()
    firsts = [
        pltpu.make_async_copy(grad_middle_hbm, grad_middle_ref, load_sem.at[6]),
        pltpu.make_async_copy(mixed_hbm, mixed_ref, load_sem.at[7]),
    ]
    begin(firsts)
    pairs = width // LANES
    loads = [
        pltpu.make_async_copy(source, target, load_sem.at[i])
        for i, (source, target) in enumerate(
            (
                (weights_hbm.at[:, pl.ds(0, width)], output_weight_ref),
                (qkv_hbm, qkv_ref),
                (extra_hbm, extra_ref),
                (normed_hbm, normed_ref),
                (weights_hbm.at[:, pl.ds(width + LANES, pairs * TRIO)], weight_ref),
            )
        )
    ]
    if net is None:
        begin(loads)
        grads_ref, grad_tokens_ref, low_ref, grad_ref, dqkv_ref, dq_ref, inner_ref, code_k_ref = refs
        plan = {}
    else:
        sums_ref, feed_grads_ref, *refs = refs
        early, refs = refs[: 2 * EARLY], refs[2 * EARLY :]
        shard_ref, shard_feed_ref, grad_tokens_ref, low_ref, grad_ref, dqkv_ref, dq_ref, inner_ref, *refs = refs
        code_k_ref, grads_ref, own_ref, send, recv, local, *bufs = refs
        held, bufs = bufs[: 2 * EARLY], bufs[2 * EARLY :]
        halves_in = [
            pltpu.make_async_copy(source, target, load_sem.at[8 + i])
            for i, (source, target) in enumerate(zip(early, held))
        ]
        begin(halves_in)
        begin(loads)
        early = held
        sems = Sems(send, recv)
        feed, att = [], []
        flip = BOTH[::-1]
        for k in range(EARLY):
            for lanes, along in feed_folds(k):
                slots, bufs = [None, early[len(feed)], *bufs[:2]], bufs[2:]
                feed.append(Fold(net, sems, None, flip, lanes, along, slots, shard_feed_ref, steps=(2, 3)))
        span = 2 * GROUP * EARLY
        for k in range(EARLY, feed_grads_ref.shape[-1] // (2 * GROUP)):
            for lanes, along in feed_folds(k):

                def kept(index, start=lanes[0] - span):
                    return own_ref[index + (slice(None), pl.ds(start, GROUP))]

                feed.append(
                    Fold(net, sems, feed_grads_ref, flip, lanes, along, bufs[:4], shard_feed_ref, own=kept)
                )
                bufs = bufs[4:]
        for lanes, along in att_folds(width):
            att.append(Fold(net, sems, grads_ref, BOTH, lanes, along, bufs[:4], shard_ref))
            bufs = bufs[4:]
        early, late = feed[: 2 * EARLY], feed[2 * EARLY :]
        net.meet()
        for p in late:
            p.send(0)
        for copy in halves_in:
            copy.wait()
        for p in early:
            p.send(2)
        mine = tuple(net.place["c"] if n == "c" else slice(None) for n in net.names(flip))
        own = pltpu.make_async_copy(
            feed_grads_ref.at[mine + (slice(None), pl.ds(span, feed_grads_ref.shape[-1] - span))], own_ref, local
        )
        own.start()
        tall = jnp.concatenate([sums_ref[...], jnp.zeros((LANES - 8, width), f32)], axis=0).T
        lane = lax.broadcasted_iota(jnp.int32, (1, LANES), 1)
        for j in range(1, 4):
            tall = jnp.where(lane == j, jnp.sum(sums_ref[j : j + 1, :], axis=1, keepdims=True), tall)
        extras = jnp.where(lane == 4, ends[-1].astype(f32), tall)

    def advance(*todo):
        for pieces, step in todo:
            for piece in pieces:
                piece.add(step)
                if step < 3:
                    piece.send(step + 1)

    def store(lanes, value):
        if net is None:
            grads_ref[:, lanes] = value.astype(bf16)
        else:
            rows = grads_ref.shape[-2]
            for i, index in enumerate(np.ndindex(*net.dims(BOTH))):
                grads_ref[index + (slice(None), lanes)] = value[i * rows : (i + 1) * rows].astype(bf16)

    if net is not None:
        store(slice(width, width + LANES), extras)
    for copy in firsts:
        copy.wait()
    low_ref[...] = grad_middle_ref[...].astype(bf16)
    store(slice(0, width), dot_first(mixed_ref[...], low_ref[...]))
    if net is not None:
        for p in att[:2]:
            p.send(0)
    loads[0].wait()
    grad_ref[...] = dot_last(low_ref[...], output_weight_ref[...]).astype(bf16)
    tokens_ref = low_ref
    tokens = pltpu.make_async_copy(tokens_hbm, tokens_ref, load_sem.at[5])
    tokens.start()
    set_codes(None, code_k_ref, ends)
    inner_codes(grad_ref, mixed_ref, inner_ref)
    moves, ending = {}, {}
    if net is not None:
        own.wait()
        output, pair = att[:2], [att[2 + 2 * p : 4 + 2 * p] for p in range(pairs)]
        moves = {
            0: [(late, 0)],
            1: [(output, 0)],
            2: [(early, 2)],
            3: [(pair[0], 0)],
            4: [(late, 1), (output, 1)],
            5: [(pair[1], 0), (pair[0], 1)],
            6: [(output, 2)],
            7: [(pair[2], 0), (pair[1], 1), (late, 2), (pair[0], 2)],
            8: [(early, 3)],
            9: [(pair[3], 0), (pair[2], 1), (pair[1], 2)],
            11: [(pair[4], 0), (pair[3], 1), (pair[2], 2)],
        }
        ending = {
            0: [(pair[4], 1), (pair[3], 2)],
            1: [(pair[5], 0)],
            4: [(pair[4], 2)],
            5: [(pair[5], 1)],
        }
    for copy in loads[1:]:
        copy.wait()
    blocks = total // WIDE

    def per_pair(p, carry):
        dq_ref[...] = jnp.zeros_like(dq_ref)

        def step(b, carry):
            for i, todo in moves.items():
                pl.when(p * blocks + b == i)(lambda todo=todo: advance(*todo))
            pair_back(p, b, total, qkv_ref, grad_ref, extra_ref, inner_ref, code_k_ref, dqkv_ref, dq_ref)
            return carry

        lax.fori_loop(0, blocks, step, 0)
        at = pl.multiple_of(p * TRIO, LANES)
        dqkv_ref[:, pl.ds(at, LANES)] = dq_ref[...].astype(bf16)
        lanes = pl.ds(pl.multiple_of(width + LANES + at, LANES), TRIO)
        store(lanes, dot_first(normed_ref[...], dqkv_ref[:, pl.ds(at, TRIO)]))
        if net is not None:
            for k in range(pairs):

                @pl.when(p == k)
                def _(k=k):
                    for piece in pair[k]:
                        piece.send(0)

        return carry

    lax.fori_loop(0, pairs, per_pair, 0)
    third = pairs * TRIO // 3
    for j in range(3):
        cols = slice(j * third, (j + 1) * third)
        back = dot_last(dqkv_ref[:, cols], weight_ref[:, cols])
        if j == 0:
            sum_ref[...] = back
        else:
            sum_ref[...] += back
        advance(*ending.get(j, ()))
    tokens.wait()
    finals = []
    for b in range(total // BLOCK):
        rows = pl.ds(b * BLOCK, BLOCK)
        unit, inv = unit_of(tokens_ref[rows, :].astype(f32))
        sum_ref[rows, :] = grad_middle_ref[rows, :] + unit_back(sum_ref[rows, :], unit, inv, gains_ref[0:1, :])
        finals.append(pltpu.make_async_copy(sum_ref.at[rows], grad_tokens_ref.at[rows], store_sem.at[b]))
        finals[-1].start()
        advance(*ending.get(3 + b, ()))
    if net is not None:
        advance((output, 3), (pair[0], 3), (pair[1], 3))
        advance((pair[5], 2), (late, 3), (pair[2], 3), (pair[3], 3), (pair[4], 3), (pair[5], 3))
        for p in feed + att:
            p.drain()
    for copy in finals:
        copy.wait()


def params(**more):
    return pltpu.CompilerParams(vmem_limit_bytes=58 << 20, **more)


def shape(*dims, kind=bf16):
    return jax.ShapeDtypeStruct(dims, kind)


def run_forward(clip, tokens, weights, gains):
    total, width = tokens.shape
    return pl.pallas_call(
        forward_kernel,
        name="layer_forward",
        out_shape=(
            shape(total, 3 * width), shape(total, width), shape(total, width),
            shape(total, width, kind=f32), shape(total, width), shape(total, width), shape(8, width, kind=f32),
        ),
        in_specs=[SM, VM, VM, VM],
        out_specs=(VM,) * 7,
        scratch_shapes=[pltpu.VMEM((total, LANES), bf16), pltpu.VMEM((total, LANES), bf16)],
        compiler_params=params(),
        cost_estimate=pl.CostEstimate(flops=12 * 10**9, bytes_accessed=20 << 20, transcendentals=0),
    )(clip, tokens, weights, gains)


def run_feed(clip, feed, out_grad, middle, gains, weights):
    total, width = feed.shape
    parts, _, both = weights.shape
    one = pl.BlockSpec((1, width, both), lambda t: (t, 0, 0))
    return pl.pallas_call(
        feed_kernel,
        name="feed_both",
        grid=(parts,),
        out_shape=(
            shape(parts, width, both), shape(total, width), shape(total, width, kind=f32), shape(8, width, kind=f32),
        ),
        in_specs=[SM, VM, VM, VM, VM, one],
        out_specs=(one, VM, VM, VM),
        scratch_shapes=[
            pltpu.VMEM((total, width), bf16), pltpu.VMEM((total, both - width), bf16),
            pltpu.VMEM((total, both - width), bf16), pltpu.VMEM((total, width), f32), pltpu.VMEM((total, width), f32),
        ],
        compiler_params=params(),
        cost_estimate=pl.CostEstimate(flops=30 * 10**9, bytes_accessed=30 << 20, transcendentals=0),
    )(clip, feed, out_grad, middle, gains, weights)


MESH = pl.DeviceIdType.MESH
ANY = pl.BlockSpec(memory_space=pl.ANY)
FACTORS = {
    (8, 4): ((("z", 4), ("y", 2)), (("x", 2), ("c", 2))),
}


class Net:
    def __init__(self, factors):
        self.factors = factors
        self.size = {n: s for axis in factors for n, s in axis}
        self.count = 1
        for s in self.size.values():
            self.count *= s

    def locate(self):
        self.place = {}
        for name, axis in zip(BOTH, self.factors):
            left = lax.axis_index(name)
            for n, s in axis[::-1]:
                self.place[n] = lax.rem(left, s)
                left = lax.div(left, s)

    def device(self, dim, value):
        out = []
        for axis in self.factors:
            index = 0
            for n, s in axis:
                index = index * s + (value if n == dim else self.place[n])
            out.append(index)
        return tuple(out)

    def names(self, order):
        axes = dict(zip(BOTH, self.factors))
        return [n for a in order for n, _ in axes[a]]

    def dims(self, order):
        return tuple(self.size[n] for n in self.names(order))

    def view(self, ref, order, lanes, **fixed):
        index = tuple(fixed.get(n, slice(None)) for n in self.names(order))
        return ref.at[index + (slice(None), pl.ds(*lanes))]

    def peers(self, dim):
        s = self.size[dim]
        return [lax.rem(self.place[dim] + o, s) for o in range(1, s)]

    def announce(self):
        barrier = pltpu.get_barrier_semaphore()
        for dim in self.size:
            for v in self.peers(dim):
                pl.semaphore_signal(barrier, inc=1, device_id=self.device(dim, v), device_id_type=MESH)

    def meet(self):
        pl.semaphore_wait(pltpu.get_barrier_semaphore(), sum(s - 1 for s in self.size.values()))


class Sems:
    def __init__(self, send, recv):
        self.send, self.recv, self.used = send, recv, 0

    def take(self):
        self.used += 1
        return self.send.at[self.used - 1], self.recv.at[self.used - 1]


def spread(net, sems, dim, source, target):
    out = []
    for v in net.peers(dim):
        send, recv = sems.take()
        out.append(
            pltpu.make_async_remote_copy(
                src_ref=source, dst_ref=target, send_sem=send, recv_sem=recv,
                device_id=net.device(dim, v), device_id_type=MESH,
            )
        )
    return out


def begin(copies):
    for copy in copies:
        copy.start()


def arrive(copies):
    for copy in copies:
        copy.wait_recv()


class Piece:
    def __init__(self, net, sems, mine, ref, order, lanes, first, second, third):
        def block(free, **other):
            fixed = {n: v for n, v in net.place.items() if n not in free}
            return net.view(ref, order, lanes, **{**fixed, **other})

        def pass_on(dim, part):
            return spread(net, sems, dim, part, part)

        self.left = False
        self.z = spread(net, sems, first, mine.at[:, pl.ds(*lanes)], block(()))
        self.one = pass_on(second, block((first,)))
        self.two = pass_on(third, block((first, second)))
        self.twins = [
            pass_on("c", block((first,))),
            sum((pass_on("c", block((first,), **{second: v})) for v in net.peers(second)), []),
            sum((pass_on("c", block((first, second), **{third: v})) for v in net.peers(third)), []),
        ]

    def start(self):
        begin(self.z)

    def leave(self):
        for copy in self.z:
            copy.wait_send()
        self.left = True

    def step_one(self):
        arrive(self.z)
        begin(self.one + self.twins[0])

    def step_two(self):
        arrive(self.one)
        begin(self.two + self.twins[1])

    def step_three(self):
        arrive(self.two)
        begin(self.twins[2])

    def ready(self):
        arrive(sum(self.twins, []))

    def drain(self):
        for copy in ([] if self.left else self.z) + self.one + self.two + sum(self.twins, []):
            copy.wait_send()


def copies_of(net):
    z, y, x, c = (net.size[n] - 1 for n in "zyxc")
    return z + y + x + c * (1 + z + y + x)


def lane_parts(width, count):
    tiles, out, at = width // LANES, [], 0
    for i in range(count):
        take = (tiles - at) // (count - i)
        out.append((at * LANES, take * LANES))
        at += take
    return out


ORDERS = (("z", "y", "x"), ("z", "x", "y"))
ORDERS_LATE = (("y", "z", "x"), ("x", "z", "y"))


def att_spans(width):
    start = width + LANES
    spans = [(width, LANES + TRIO)] + [(start + p * TRIO, TRIO) for p in range(1, width // LANES)]
    return spans + [(0, width)]


def halves(start, size):
    return [(start + at, take) for at, take in lane_parts(size, 2)]


def fused_forward_kernel(
    net,
    clip_ref, tokens_ref, w_reduce_ref, out_grad_ref, w_query_ref, w_key_ref, w_value_ref, w_output_ref, gain_ref,
    w_expand_ref,
    att_all, feed_all, qkv_hbm, mixed_hbm, extra_hbm, normed_hbm, grads_ref, result_hbm, grad_middle_hbm, sums_ref,
    gains_ref, half_0, half_1, half_2, half_3, qkv_ref, mixed_ref, extra_ref, normed_ref, result_ref, grad_middle_ref, store_sem, mine_ref, both_ref, gain_tile_ref, group_ref, output_weight_ref, grad_ref, middle_ref, feed_ref, active_ref, hidden_ref, out_ref,
    chunk_ref, stage_ref, code_q_ref, code_k_ref, send, recv, local, chunk_sem, stage_sem, *early,
):
    total, width = tokens_ref.shape
    pairs = width // LANES
    hid = w_expand_ref.shape[1]
    chunks = hid // GROUP
    ends = clip_ends(clip_ref)
    flip = BOTH[::-1]
    net.locate()
    net.announce()

    moves = [(w_output_ref, mine_ref.at[:, pl.ds(0, width)]), (gain_ref, mine_ref.at[:, pl.ds(width, LANES)])]
    for p in range(pairs):
        for j, ref in enumerate((w_query_ref, w_key_ref, w_value_ref)):
            at = width + LANES + p * TRIO + j * LANES
            moves.append((ref.at[:, pl.ds(p * LANES, LANES)], mine_ref.at[:, pl.ds(at, LANES)]))
    for k in range(chunks):
        for kind, ref in enumerate((w_expand_ref, w_reduce_ref)):
            moves.append((ref.at[:, pl.ds(k * GROUP, GROUP)], both_ref.at[:, pl.ds((2 * k + kind) * GROUP, GROUP)]))
    copies = [pltpu.make_async_copy(src, dst, local.at[i]) for i, (src, dst) in enumerate(moves)]
    used = len(copies)
    copies.append(pltpu.make_async_copy(out_grad_ref, grad_ref, local.at[used]))
    for copy in copies:
        copy.start()
    for copy in copies[:used]:
        copy.wait()
    net.meet()
    sems = Sems(send, recv)
    att = [
        [Piece(net, sems, mine_ref, att_all, BOTH, lanes, *ORDERS[i]) for i, lanes in enumerate(halves(*span))]
        for span in att_spans(width)
    ]
    feed = [
        [
            Piece(net, sems, both_ref, feed_all, flip, lanes, *(ORDERS_LATE if k >= LATE else ORDERS)[i])
            for i, lanes in enumerate(halves(2 * k * GROUP, 2 * GROUP))
        ]
        for k in range(chunks)
    ]
    folds = []
    for k in range(EARLY):
        for kind, (lanes, along) in enumerate(feed_folds(k)):

            def staged(index, kind=kind):
                at = dict(zip([n for n in net.names(flip) if n != "c"], index))
                q = at["x"] * net.size["c"] + net.place["c"]
                return stage_ref[kind, at["z"], at["y"], :, pl.ds(pl.multiple_of(q * GROUP, GROUP), GROUP)]

            bufs, early = early[:2], early[2:]
            folds.append(Fold(net, sems, grads_ref, flip, lanes, along, bufs, own=staged, steps=(0, 1)))
    own = [
        pltpu.make_async_copy(mine_ref, net.view(att_all, BOTH, (0, mine_ref.shape[1]), **net.place), local.at[0]),
        pltpu.make_async_copy(both_ref, net.view(feed_all, flip, (0, both_ref.shape[1]), **net.place), local.at[1]),
    ]
    for copy in own:
        copy.start()

    def act(*moves):
        for name, pair in moves:
            for piece in pair:
                getattr(piece, name)()

    pair, output = att[:-1], att[-1]
    act(("start", pair[0]))
    sums_ref[...] = jnp.zeros_like(sums_ref)
    copies[used].wait()
    for copy in own:
        copy.wait()

    def norm(r0):
        rows = pl.ds(r0, BLOCK)
        x = tokens_ref[rows, :].astype(f32)
        valid = valid_of(r0, BLOCK, ends)
        middle_ref[rows, :] = unit_of(x)[0]
        grad_ref[rows, :] = (grad_ref[rows, :].astype(f32) * valid).astype(bf16)
        set_row(sums_ref, 1, jnp.sum(x * x * valid, axis=0, keepdims=True))

    row_loop(total, BLOCK, norm)
    set_codes(code_q_ref, code_k_ref, ends)
    for p in range(pairs):
        act(("leave", pair[p]), ("start", pair[p + 1] if p + 1 < pairs else feed[0]), ("step_one", pair[p]))
        if p >= 2:
            act(("step_two", pair[p - 2]))
        if p >= 4:
            act(("step_three", pair[p - 4]))
    act(("ready", pair[0]))

    def fetch(lanes, target, sem):
        return pltpu.make_async_copy(net.view(att_all, BOTH, lanes), target, sem)

    def flat(value):
        return value.reshape(width, value.shape[-1])

    tile = fetch((width, LANES), gain_tile_ref, local.at[0])
    tile.start()
    fetch((width + LANES, TRIO), group_ref.at[0], local.at[1]).start()
    tile.wait()
    gains_ref[...] = flat(gain_tile_ref[...].astype(f32)).T[:8]

    def scale(r0):
        rows = pl.ds(r0, BLOCK)
        normed_ref[rows, :] = (middle_ref[rows, :] * gains_ref[0:1, :]).astype(bf16)

    row_loop(total, BLOCK, scale)
    plan = {
        0: [("step_two", pair[4]), ("step_three", pair[2]), ("ready", pair[1])],
        1: [("step_two", pair[5]), ("step_three", pair[3]), ("start", output)],
        2: [("start", feed[1]), ("step_three", pair[4]), ("ready", pair[2])],
        3: [("step_one", feed[0]), ("step_three", pair[5])],
        4: [("start", feed[2]), ("step_one", output), ("ready", pair[3])],
        6: [("step_one", feed[2]), ("step_two", output), ("step_two", feed[0]), ("ready", pair[4])],
        8: [("step_one", feed[1]), ("ready", pair[5])],
        9: [("step_three", output)],
        11: [("step_three", feed[0])],
    }
    blocks = total // WIDE

    def per_pair(p, carry):
        slot = lax.rem(p, 2)
        fetch((0, TRIO), group_ref.at[slot], local.at[1]).wait()
        project(normed_ref, pl.ds(0, total), flat(group_ref[slot]), qkv_ref, p)

        def step(b, carry):
            for i, todo in plan.items():
                pl.when(p * blocks + b == i)(lambda todo=todo: act(*todo))

            @pl.when((b == 1) & (p + 1 < pairs))
            def _():
                start = pl.multiple_of(width + LANES + (p + 1) * TRIO, LANES)
                fetch((start, TRIO), group_ref.at[1 - slot], local.at[1]).start()

            pair_forward(p, b, total, qkv_ref, mixed_ref, extra_ref, code_q_ref, code_k_ref)
            return carry

        lax.fori_loop(0, blocks, step, 0)
        return carry

    lax.fori_loop(0, pairs, per_pair, 0)
    act(("ready", output))
    fetch((0, width), output_weight_ref, local.at[1]).start()
    outs = [
        pltpu.make_async_copy(ref, target, store_sem.at[i])
        for i, (ref, target) in enumerate(
            ((qkv_ref, qkv_hbm), (mixed_ref, mixed_hbm), (normed_ref, normed_hbm), (extra_ref, extra_hbm))
        )
    ]
    for copy in outs:
        copy.start()
    fetch((0, width), output_weight_ref, local.at[1]).wait()
    middle_ref[...] = dot_plain(mixed_ref[...], flat(output_weight_ref[...]))
    act(("step_two", feed[1]))

    def second(r0):
        rows = pl.ds(r0, BLOCK)
        branch = middle_ref[rows, :]
        middle = tokens_ref[rows, :].astype(f32) + branch
        middle_ref[rows, :] = middle
        feed_ref[rows, :] = (unit_of(middle)[0] * gains_ref[1:2, :]).astype(bf16)
        set_row(sums_ref, 2, jnp.sum(branch * branch * valid_of(r0, BLOCK, ends), axis=0, keepdims=True))

    row_loop(total, BLOCK, second)
    act(("ready", feed[0]))
    feed_plan = {(0, 2): [("step_three", feed[1]), ("step_two", feed[2])], (1, 2): [("step_three", feed[2])]}

    tp = net.names(("tp",))
    quarters = list(np.ndindex(*(net.size[n] for n in tp)))
    both_kinds = range(2)

    def place(ref, quarter, kind, k):
        at = (2 * k + kind) * GROUP
        at = at if isinstance(at, int) else pl.multiple_of(at, GROUP)
        return ref.at[quarter + (slice(None),) * (len(ref.shape) - len(quarter) - 1) + (pl.ds(at, GROUP),)]

    def part(ref, q):
        return ref.at[(slice(None),) * (len(ref.shape) - 1) + (pl.ds(q * GROUP, GROUP),)]

    def chunk_copies(k, slot):
        return [
            pltpu.make_async_copy(
                place(feed_all, quarter, kind, k), part(chunk_ref.at[slot, kind], q), chunk_sem.at[slot, kind, q]
            )
            for kind in both_kinds
            for q, quarter in enumerate(quarters)
        ]

    def stage_copies(k):
        return [
            pltpu.make_async_copy(part(stage_ref.at[kind], q), place(grads_ref, quarter, kind, k), stage_sem.at[kind, q])
            for kind in both_kinds
            for q, quarter in enumerate(quarters)
        ]

    for copy in chunk_copies(0, 0):
        copy.start()
    out_ref[...] = jnp.zeros_like(out_ref)
    grad_middle_ref[...] = jnp.zeros_like(grad_middle_ref)

    def chunk(k, carry):
        slot = lax.rem(k, 2)
        for copy in chunk_copies(k, slot):
            copy.wait()

        def weights(kind):
            return chunk_ref[slot, kind].reshape(width, len(quarters) * GROUP)

        for q in range(len(quarters)):
            for (a, b), todo in feed_plan.items():
                if q == b:
                    pl.when(k == a)(lambda todo=todo: act(*todo))
            if q == 1:

                @pl.when(k > 0)
                def _():
                    for copy in stage_copies(k - 1):
                        copy.wait()

                for j in range(EARLY):

                    @pl.when(k == j + 1)
                    def _(j=j):
                        for p in folds[2 * j : 2 * j + 2]:
                            p.send(0)

            cols = slice(q * GROUP, (q + 1) * GROUP)
            hidden = dot_plain(feed_ref[...], weights(0)[:, cols])
            grad_active = dot_plain(grad_ref[...], weights(1)[:, cols])
            share = 0.5 * (1.0 + lax.erf(hidden * 0.7071067811865476))
            active_ref[:, cols] = (hidden * share).astype(bf16)
            slope = share + hidden * (jnp.exp(-0.5 * hidden * hidden) * 0.3989422804014327)
            hidden_ref[:, cols] = (grad_active * slope).astype(bf16)
        for j in range(chunks - 1):

            @pl.when(k == j)
            def _(j=j):
                act(("ready", feed[j + 1]))
                for copy in chunk_copies(j + 1, (j + 1) % 2):
                    copy.start()

        for j in range(EARLY):

            @pl.when(k == j + 1)
            def _(j=j):
                for p in folds[2 * j : 2 * j + 2]:
                    p.add(0)
                    p.send(1)

        out_ref[...] += dot_last(active_ref[...], weights(1))
        grad_middle_ref[...] += dot_last(hidden_ref[...], weights(0))
        for kind, (left, right) in enumerate(((feed_ref, hidden_ref), (grad_ref, active_ref))):
            stage_ref[kind] = dot_first(left[...], right[...]).reshape(stage_ref.shape[1:]).astype(bf16)
        for copy in stage_copies(k):
            copy.start()
        return carry

    lax.fori_loop(0, chunks, chunk, 0)

    for i in range(total // BLOCK):
        rows = pl.ds(i * BLOCK, BLOCK)
        middle, out, back = middle_ref[rows, :], out_ref[rows, :], grad_middle_ref[rows, :]
        result_ref[rows, :] = (middle + out).astype(bf16)
        unit, inv = unit_of(middle)
        grad_middle_ref[rows, :] = grad_ref[rows, :].astype(f32) + unit_back(back, unit, inv, gains_ref[1:2, :])
        set_row(sums_ref, 3, jnp.sum(out * out * valid_of(i * BLOCK, BLOCK, ends), axis=0, keepdims=True))
        set_row(sums_ref, 0, jnp.sum(back * unit, axis=0, keepdims=True))
        for j, (ref, target) in enumerate(((result_ref, result_hbm), (grad_middle_ref, grad_middle_hbm))):
            outs.append(pltpu.make_async_copy(ref.at[rows], target.at[rows], store_sem.at[4 + 2 * i + j]))
            outs[-1].start()
    for i, (p, target) in enumerate(zip(folds, (half_0, half_1, half_2, half_3))):
        p.add(1)
        outs.append(pltpu.make_async_copy(p.bufs[1].at[pl.ds(0, 1)], target, local.at[i]))
        outs[-1].start()
    for copy in outs:
        copy.wait()
    for copy in stage_copies(chunks - 1):
        copy.wait()
    for p in folds:
        p.drain()
    for pair in att + feed:
        for piece in pair:
            piece.drain()


def run_fused_forward(net, clip, tokens, out_grad, weights, gain_tile, w_expand, w_reduce):
    total, width = tokens.shape
    rows, rows_feed = width // net.count, w_expand.shape[0]
    lanes, hid = 4 * width + LANES, w_expand.shape[1]
    flip = BOTH[::-1]
    ff = (*net.dims(flip), rows_feed, 2 * hid)
    wide = GROUP * int(np.prod(net.dims(("tp",))))
    inner = tuple(net.size[n] for n in net.names(("dp",))) + (rows_feed, wide)
    count = 2 * (len(att_spans(width)) + hid // GROUP) * copies_of(net) + 4 * EARLY * max(net.size.values())
    dma = pltpu.SemaphoreType.DMA
    early, halves_out = [], []
    for k in range(EARLY):
        for fold in feed_folds(k):
            shapes = Fold.shapes(net, flip, rows_feed, *fold)[:2]
            early += [pltpu.VMEM(dims, bf16) for dims in shapes]
            halves_out.append(shape(1, *shapes[1][1:]))
    return pl.pallas_call(
        lambda *refs: fused_forward_kernel(net, *refs),
        name="layer_forward_feed",
        out_shape=(
            shape(*net.dims(BOTH), rows, lanes), shape(*ff), shape(total, 3 * width), shape(total, width),
            shape(total, width), shape(total, width), shape(*ff), shape(total, width),
            shape(total, width, kind=f32), shape(8, width, kind=f32), shape(8, width, kind=f32), *halves_out,
        ),
        in_specs=[SM, VM] + [ANY] * 8,
        out_specs=(ANY, ANY, ANY, ANY, ANY, ANY, ANY, ANY, ANY, VM, VM) + (ANY,) * len(halves_out),
        scratch_shapes=[
            pltpu.VMEM((total, 3 * width), bf16), pltpu.VMEM((total, width), bf16), pltpu.VMEM((total, width), bf16),
            pltpu.VMEM((total, width), bf16), pltpu.VMEM((total, width), bf16), pltpu.VMEM((total, width), f32), dma((4 + 2 * total // BLOCK,)),
            pltpu.VMEM((rows, lanes), bf16), pltpu.VMEM((rows_feed, 2 * hid), bf16), pltpu.VMEM((*net.dims(BOTH), rows, LANES), bf16),
            pltpu.VMEM((2, *net.dims(BOTH), rows, TRIO), bf16), pltpu.VMEM((*net.dims(BOTH), rows, width), bf16),
            pltpu.VMEM((total, width), bf16),
            pltpu.VMEM((total, width), f32), pltpu.VMEM((total, width), bf16), pltpu.VMEM((total, wide), bf16),
            pltpu.VMEM((total, wide), bf16), pltpu.VMEM((total, width), f32), pltpu.VMEM((2, 2, *inner), bf16),
            pltpu.VMEM((2, *inner), bf16), pltpu.VMEM((total, LANES), bf16), pltpu.VMEM((total, LANES), bf16),
            dma((count,)), dma((count,)),
            dma((4 + 3 * (width // LANES) + 2 * hid // GROUP,)), dma((2, 2, wide // GROUP)), dma((2, wide // GROUP)),
            *early,
        ],
        compiler_params=params(collective_id=1, has_side_effects=True),
    )(clip, tokens, w_reduce, out_grad, *weights, gain_tile, w_expand)


def store_at(ref, index, lanes, value):
    ref[tuple(index) + (slice(None), lanes)] = value


def each(dims, body, index=()):
    count = 1
    for size in dims:
        count *= size
    if count <= 4:
        for tail in np.ndindex(*dims):
            body(index + tail)
    else:

        def step(i, carry):
            each(dims[1:], body, index + (i,))
            return carry

        lax.fori_loop(0, dims[0], step, 0)


class Fold:
    def __init__(self, net, sems, ref, order, lanes, along, bufs, out=None, own=None, steps=(0, 1, 2, 3)):
        self.net, self.lanes, self.along, self.bufs, self.out, self.steps = net, lanes, along, bufs, out, steps
        names = net.names(order)
        self.names = [[n for n in names if n not in along[:k]] for k in range(5)]
        self.ref, self.own = ref, own
        self.copies = {}
        for k in steps:
            dim = along[k]
            source, cols = (ref, lanes) if k == 0 else (bufs[k - 1].at[0], (0, lanes[1]))
            self.copies[k] = []
            for o, v in enumerate(net.peers(dim)):
                index = tuple(v if n == dim else slice(None) for n in self.names[k])
                s, r = sems.take()
                self.copies[k].append(
                    pltpu.make_async_remote_copy(
                        src_ref=source.at[index + (slice(None), pl.ds(*cols))], dst_ref=bufs[k].at[o],
                        send_sem=s, recv_sem=r, device_id=net.device(dim, v), device_id_type=MESH,
                    )
                )

    @staticmethod
    def shapes(net, order, rows, lanes, along):
        names, out = net.names(order), []
        for k, dim in enumerate(along):
            left = [net.size[n] for n in names if n not in along[: k + 1]]
            out.append((net.size[dim] - 1, *left, rows, lanes[1]))
        return out

    def send(self, k):
        begin(self.copies[k])

    def add(self, k):
        arrive(self.copies[k])
        dim, buf, cols = self.along[k], self.bufs[k], slice(0, self.lanes[1])
        here = self.net.place[dim]
        wide = pl.ds(*self.lanes)

        def one(index):
            at = dict(zip(self.names[k + 1], index))
            full = tuple(at.get(n, here) for n in self.names[k])
            if k > 0:
                total = self.bufs[k - 1][(0,) + full + (slice(None), cols)].astype(f32)
            elif self.own is not None:
                total = self.own(index).astype(f32)
            else:
                total = self.ref[full + (slice(None), wide)].astype(f32)
            terms = [total] + [buf[(o,) + index].astype(f32) for o in range(self.net.size[dim] - 1)]
            if len(terms) > 2:
                size = len(terms)
                total = 0.0
                for v in range(size):
                    back = lax.rem(here - v + size, size)
                    term = terms[0]
                    for o in range(1, size):
                        term = jnp.where(back == o, terms[o], term)
                    total = total + term
            else:
                total = terms[0] + terms[1]
            if k == 3:
                self.out[:, wide] = total
            else:
                buf[(0,) + index] = total.astype(bf16)

        each([self.net.size[n] for n in self.names[k + 1]], one)

    def drain(self):
        for copies in self.copies.values():
            for copy in copies:
                copy.wait_send()


ALONG = (("c", "x", "y", "z"), ("c", "y", "x", "z"))


def feed_folds(k):
    return [((2 * GROUP * k + GROUP * i, GROUP), ALONG[i]) for i in range(2)]


EARLY = 2
LATE = 2


def att_folds(width):
    out = []
    spans = [(0, width + LANES)] + [(width + LANES + p * TRIO, TRIO) for p in range(width // LANES)]
    for start, size in spans:
        for i, (at, take) in enumerate(lane_parts(size, 2)):
            out.append(((start + at, take), ALONG[i % 2]))
    return out


def run_backward(net, clip, grad_middle, mixed, qkv, extra, normed, tokens, weights, gains, *more_args):
    total, width = tokens.shape
    lanes = weights.shape[1]
    scratch = [
        pltpu.VMEM((total, width), bf16), pltpu.VMEM((total, width), bf16), pltpu.VMEM((total, 3 * width), bf16),
        pltpu.VMEM((total, LANES), f32), pltpu.VMEM((total, width), bf16), pltpu.VMEM((total, LANES), bf16),
    ]
    operands = [clip, grad_middle, mixed, qkv, extra, normed, tokens, weights, gains]
    in_specs = [SM] + [ANY] * 7 + [VM]
    out_shape = (shape(width, lanes), shape(total, width, kind=f32))
    more = {}
    if net is not None:
        feed_grads = more_args[1]
        rows, rows_feed = width // net.count, feed_grads.shape[-2]
        hid = feed_grads.shape[-1] // 2
        flip = BOTH[::-1]
        operands += more_args
        in_specs += [VM, ANY] + [ANY] * (2 * EARLY)
        out_shape = (shape(rows, lanes, kind=f32), shape(rows_feed, 2 * hid, kind=f32), out_shape[1])
        scratch.append(pltpu.VMEM((*net.dims(BOTH), rows, lanes), bf16))
        kept = tuple(net.size[n] for n in net.names(flip) if n != "c")
        scratch.append(pltpu.VMEM((*kept, rows_feed, 2 * hid - 2 * GROUP * EARLY), bf16))
        bufs = []
        for k in range(hid // GROUP):
            for f in feed_folds(k):
                bufs += Fold.shapes(net, flip, rows_feed, *f)[2 if k < EARLY else 0 :]
        for f in att_folds(width):
            bufs += Fold.shapes(net, BOTH, rows, *f)
        count = sum(dims[0] for dims in bufs)
        scratch += [pltpu.SemaphoreType.DMA((count,)), pltpu.SemaphoreType.DMA((count,)), pltpu.SemaphoreType.DMA]
        scratch += [pltpu.VMEM(half.shape, bf16) for half in more_args[2:]]
        scratch += [pltpu.VMEM(dims, bf16) for dims in bufs]
        more = dict(collective_id=2, has_side_effects=True)
    scratch += [
        pltpu.VMEM((total, width), f32), pltpu.VMEM((total, width), bf16),
        pltpu.VMEM((total, 3 * width), bf16), pltpu.VMEM((total, width), bf16), pltpu.VMEM((total, width), bf16),
        pltpu.VMEM((width, width), bf16), pltpu.VMEM((width, 3 * width), bf16), pltpu.VMEM((total, width), f32),
        pltpu.SemaphoreType.DMA((8 + 2 * EARLY,)), pltpu.SemaphoreType.DMA((total // BLOCK,)),
    ]
    return pl.pallas_call(
        lambda *refs: backward_kernel(net, *refs),
        name="layer_backward",
        out_shape=out_shape,
        in_specs=in_specs,
        out_specs=(VM,) * (len(out_shape) - 1) + (ANY,),
        scratch_shapes=scratch,
        compiler_params=params(**more),
        cost_estimate=pl.CostEstimate(flops=22 * 10**9, bytes_accessed=30 << 20, transcendentals=0),
    )(*operands)


def unpack_kernel(
    shard_ref, feed_ref, w_query_ref, w_key_ref, w_value_ref, gain_ref, result_in, grad_in,
    query_ref, key_ref, value_ref, output_ref, expand_ref, reduce_ref, gain_one_ref, gain_two_ref, means_ref,
    result_out, grad_out, result_ref, grad_ref, sem,
):
    width = output_ref.shape[1]
    parts = [
        (source.at[pl.ds(r0, BLOCK)], held.at[pl.ds(r0, BLOCK)], target.at[pl.ds(r0, BLOCK)])
        for r0 in range(0, result_ref.shape[0], BLOCK)
        for source, held, target in ((result_in, result_ref, result_out), (grad_in, grad_ref, grad_out))
    ]
    loads = [pltpu.make_async_copy(source, held, sem.at[i]) for i, (source, held, _) in enumerate(parts)]
    copies = [pltpu.make_async_copy(held, target, sem.at[i]) for i, (_, held, target) in enumerate(parts)]
    begin(loads)
    output_ref[...] = shard_ref[:, :width]
    for k in range(expand_ref.shape[1] // GROUP):
        cols = slice(k * GROUP, (k + 1) * GROUP)
        expand_ref[:, cols] = feed_ref[:, 2 * k * GROUP : (2 * k + 1) * GROUP]
        reduce_ref[:, cols] = feed_ref[:, (2 * k + 1) * GROUP : (2 * k + 2) * GROUP]
    gain = 0.0
    owned = (w_query_ref, w_key_ref, w_value_ref)
    for j, (out, weight) in enumerate(zip((query_ref, key_ref, value_ref), owned)):
        for p in range(width // LANES):
            at = width + LANES + p * TRIO + j * LANES
            out[:, p * LANES : (p + 1) * LANES] = shard_ref[:, at : at + LANES]
        gain = gain + jnp.sum(weight[...].astype(f32) * out[...], axis=1, keepdims=True)
    gain = gain / gain_ref[:, :1].astype(f32)
    lane = lax.broadcasted_iota(jnp.int32, (1, LANES), 1)
    tile = shard_ref[:, width : width + LANES]
    means = jnp.sqrt(tile / (tile[:, 4:5] * width))
    tile = jnp.where(lane == 5, gain, jnp.where(lane == 0, tile, means))
    tile = jnp.concatenate([tile, jnp.zeros((LANES - tile.shape[0], LANES), f32)], axis=0)
    rows = tile.T
    count = gain_one_ref.shape[0]
    gain_one_ref[...] = rows[5, :count]
    gain_two_ref[...] = rows[0, :count]
    lane = lax.broadcasted_iota(jnp.int32, (1, LANES), 1)
    means_ref[...] = jnp.where(lane == 0, rows[1:2], jnp.where(lane == 1, rows[2:3], rows[3:4]))[0, :3]
    for load, copy in zip(loads, copies):
        load.wait()
        copy.start()
    for copy in copies:
        copy.wait()


def run_unpack(shard, shard_feed, weights, gain_tile, result, grad_tokens):
    rows, width = weights[0].shape
    rows_feed, both = shard_feed.shape
    return pl.pallas_call(
        unpack_kernel,
        name="unpack_outputs",
        out_shape=(
            *(shape(rows, width, kind=f32) for _ in range(4)), shape(rows_feed, both // 2, kind=f32),
            shape(rows_feed, both // 2, kind=f32), shape(rows, kind=f32), shape(rows, kind=f32), shape(3, kind=f32),
            shape(*result.shape), shape(*grad_tokens.shape, kind=f32),
        ),
        in_specs=[VM] * 6 + [ANY] * 2,
        out_specs=(VM,) * 9 + (ANY,) * 2,
        scratch_shapes=[
            pltpu.VMEM(result.shape, bf16), pltpu.VMEM(grad_tokens.shape, f32),
            pltpu.SemaphoreType.DMA((2 * result.shape[0] // BLOCK,)),
        ],
        compiler_params=params(),
    )(shard, shard_feed, *weights, gain_tile, result, grad_tokens)


def on_device(
    net,
    tokens, clip_lengths, out_grad, w_query, w_key, w_value, w_output, gain_attention, gain_feed, w_expand, w_reduce,
):
    _, total, width = tokens.shape
    rows = tokens.reshape(total, width)
    out_grad = out_grad.reshape(total, width)
    lane = lax.broadcasted_iota(jnp.int32, (1, LANES), 1)
    gain_tile = jnp.where(lane == 0, gain_attention[:, None], jnp.where(lane == 1, gain_feed[:, None], 0))
    hid = w_expand.shape[1]
    if net is not None:
        weights, _, qkv, mixed, extra, normed, feed_grads, result, grad_middle, sums, gains, *early = run_fused_forward(
            net, clip_lengths, rows, out_grad, (w_query, w_key, w_value, w_output), gain_tile, w_expand, w_reduce.T
        )
        weights = weights.reshape(width, -1)
        shard, shard_feed, grad_tokens = run_backward(
            net, clip_lengths, grad_middle, mixed, qkv, extra, normed, rows, weights, gains, sums, feed_grads, *early
        )
        query, key, value, output, expand, reduce, gain_one, gain_two, means, result, grad_tokens = run_unpack(
            shard, shard_feed, (w_query, w_key, w_value), gain_tile, result, grad_tokens
        )
        reduce = reduce.T
    else:
        mine = [w_output, gain_tile]
        for p in range(width // LANES):
            mine += [w[:, p * LANES : (p + 1) * LANES] for w in (w_query, w_key, w_value)]
        weights = lax.all_gather(jnp.concatenate(mine, axis=1), BOTH, axis=0, tiled=True)
        both = jnp.concatenate([w_expand, w_reduce.T], axis=1)
        feed_weights = lax.all_gather(both, BOTH[::-1], axis=0, tiled=True).reshape(-1, width, 2 * hid)
        gains = jnp.pad(weights[:, width : width + 2].T.astype(f32), ((0, 6), (0, 0)))
        qkv, mixed, extra, middle, feed, normed, sums_one = run_forward(clip_lengths, rows, weights, gains)
        feed_grads, result, grad_middle, sums_two = run_feed(
            clip_lengths, feed, out_grad, middle, gains, feed_weights
        )
        count = jnp.sum(clip_lengths[:, : SLOTS - 1]).astype(f32)
        squares = jnp.stack([jnp.sum(sums_one[0]), jnp.sum(sums_one[1]), jnp.sum(sums_two[0]), count])
        grads, grad_tokens = run_backward(
            None, clip_lengths, grad_middle, mixed, qkv, extra, normed, rows, weights, gains
        )
        shard = lax.psum_scatter(grads, BOTH, scatter_dimension=0, tiled=True).astype(f32)
        shard_feed = lax.psum_scatter(
            feed_grads.reshape(-1, 2 * hid), BOTH[::-1], scatter_dimension=0, tiled=True
        ).astype(f32)
        stats = lax.psum(squares, BOTH)
        gain_two = lax.psum_scatter(sums_two[1], BOTH, scatter_dimension=0, tiled=True)
        means = jnp.sqrt(stats[:3] / (stats[3] * width))
        parts = shard[:, width + LANES :].reshape(-1, width // LANES, 3, LANES)
        query, key, value = (parts[:, :, j].reshape(-1, width) for j in range(3))
        pairs = ((w_query, query), (w_key, key), (w_value, value))
        gain_one = sum(jnp.sum(w.astype(f32) * g, axis=1) for w, g in pairs) / gain_attention.astype(f32)
        output, expand, reduce = shard[:, :width], shard_feed[:, :hid], shard_feed[:, hid:].T
    return (
        result.reshape(1, total, width),
        grad_tokens.reshape(1, total, width),
        query,
        key,
        value,
        output,
        gain_one,
        gain_two,
        expand,
        reduce,
        means,
    )


def solution(mesh):
    row, flat = P(BOTH, None), P(BOTH)
    whole = P(BOTH, None, None)
    in_specs = (whole, row, whole, row, row, row, row, flat, flat, P("dp", "tp"), P("tp", "dp"))
    out_specs = (whole, whole, row, row, row, row, flat, flat, P("dp", "tp"), P("tp", "dp"), P())
    factors = FACTORS.get((mesh.shape["dp"], mesh.shape["tp"]))
    net = Net(factors) if factors else None
    return jax.shard_map(
        lambda *args: on_device(net, *args), mesh=mesh, in_specs=in_specs, out_specs=out_specs, check_vma=False
    )
```
